128 devices in a mesh: segment: 8 (over z, x_hi), replica: 16 (over x_lo, y, core).
Axes of the slice: x: 4 (x_hi: 2, x_lo: 2; x = x_hi * 2 + x_lo), y: 4, z: 4, core: 2. Of those that a mesh axis runs over, the one named last changes fastest.
Arguments:
- clips: bfloat16 [32, 4, 24, 16, 128], P('replica'), may hold values from -6 to 6
- offsets: int32 [32, 2], P('replica'), may hold values from 0 to 8
- weights: bfloat16 [8, 3456, 128], P('segment'), may hold values from -5 to 5
- moment: float32 [8, 3456, 128], P('segment', 'replica'), may hold values from -6 to 6
- second: float32 [8, 3456, 128], P('segment', 'replica'), may hold values from 0.25 to 4
- stale_grads: float32 [8, 3456, 128], P('segment', 'replica'), may hold values from -6 to 6
- cotangent: bfloat16 [32, 4, 16, 8, 128], P('replica'), may hold values from -6 to 6
Outputs:
- grads: float32 [8, 3456, 128], P('segment', 'replica')
- new_moment: float32 [8, 3456, 128], P('segment', 'replica')
- new_second: float32 [8, 3456, 128], P('segment', 'replica')
- new_weights: bfloat16 [8, 3456, 128], P('segment')
The draws below stay inside these ranges and needn't reach their ends.
Inputs may be any that keep to these rules, and one draw needn't show every extreme that they name: `offsets`: each offset lets the tile lie inside its clip.
All inputs are finite; a program needn't handle non-finite values.
Results may differ from the reference program's by a relative error of at most 0.03.
Values may be sent and summed in bfloat16 or wider, within the bound.
A program may use at most 64 MiB of HBM per device.

```python
import math
import jax
import jax.numpy as jnp
from jax import lax

CHAN = 128
FRAMES = 4
TILE_H = 16
TILE_W = 8
SEGMENTS = 8
TAP_ROWS = 3456
TILES = 32
CLIP_H = 24
CLIP_W = 16


def touch_ends(entries, stream_key, least, largest):
    dims = entries.shape
    index_at = [jax.random.randint(jax.random.fold_in(stream_key, axis), (), 0, dims[axis]) for axis in range(len(dims))]
    entries = entries.at[tuple(index_at)].set(least)
    longest = dims.index(max(dims))
    index_at[longest] = (index_at[longest] + 1) % dims[longest]
    return entries.at[tuple(index_at)].set(largest)


def level_of(own_key, shape, shards, least, largest):
    gain, own = 1.0, jax.random.fold_in(own_key, 6)
    for position, parts in shards:
        draws = jnp.exp(jax.random.uniform(jax.random.fold_in(own, position), (parts,), jnp.float32, least / len(shards), largest / len(shards)))
        gain = gain * jnp.repeat(draws, shape[position] // parts).reshape([-1 if axis == position else 1 for axis in range(len(shape))])
    return gain


def normal_values(rng, shape, spread, limit, cuts=(), dtype=jnp.bfloat16):
    result = spread * jax.random.normal(rng, shape, jnp.float32)
    if cuts:
        result = result * level_of(rng, shape, cuts, -0.22, 0.18)
    return jnp.clip(result, -limit, limit).astype(dtype)


def setup_inputs(seed: int = 0) -> dict:
    key_of = jax.random.split(jax.random.key(seed), 8)
    clips = normal_values(key_of[0], (TILES, FRAMES, CLIP_H, CLIP_W, CHAN), 1.0, 6.0, ((0, 16),))
    offsets = touch_ends(jax.random.randint(key_of[1], (TILES, 2), 0, TILE_W + 1), jax.random.fold_in(key_of[1], 1), 0, TILE_W).astype(jnp.int32)
    weights = normal_values(key_of[2], (SEGMENTS, TAP_ROWS, CHAN), 1.0, 5.0, ((0, 8),))
    moment = normal_values(key_of[3], (SEGMENTS, TAP_ROWS, CHAN), 1.0, 6.0, ((0, 8), (1, 16)), jnp.float32)
    second = jnp.clip(jnp.exp(math.log(4.0) - 2.7725887 * jax.random.uniform(key_of[4], (SEGMENTS, TAP_ROWS, CHAN), jnp.float32) ** level_of(key_of[4], (SEGMENTS, TAP_ROWS, CHAN), ((0, 8), (1, 16)), -0.2, 0.2)), 0.25, 4.0)
    stale_grads = normal_values(key_of[5], (SEGMENTS, TAP_ROWS, CHAN), 1.0, 6.0, ((0, 8), (1, 16)), jnp.float32)
    cotangent = normal_values(key_of[6], (TILES, FRAMES, TILE_H, TILE_W, CHAN), 1.0, 6.0, ((0, 16),))
    return {"clips": clips, "offsets": offsets, "weights": weights, "moment": moment, "second": second, "stale_grads": stale_grads, "cotangent": cotangent}


beta_one = 0.9
beta_two = 0.95
learn_rate = 0.05
adam_eps = 1e-08

def gather_taps(field):
    depth, height, width, chans = field.shape
    padded = jnp.pad(field, ((2, 0), (1, 1), (1, 1), (0, 0)))
    pieces = [padded[shift_t:shift_t + depth, shift_y:shift_y + height, shift_x:shift_x + width] for shift_t in range(3) for shift_y in range(3) for shift_x in range(3)]
    return jnp.stack(pieces, axis=3).reshape(depth * height * width, 27 * chans)

def spread_taps(blocks, depth, height, width, chans):
    blocks = blocks.reshape(depth, height, width, 27, chans)
    total = jnp.zeros((depth + 2, height + 2, width + 2, chans), jnp.float32)
    index = 0
    for shift_t in range(3):
        for shift_y in range(3):
            for shift_x in range(3):
                total = total.at[shift_t:shift_t + depth, shift_y:shift_y + height, shift_x:shift_x + width].add(blocks[:, :, :, index])
                index = index + 1
    return total[2:, 1:-1, 1:-1]

def reference(clips, offsets, weights, moment, second, stale_grads, cotangent):
    scale = 2.0 / math.sqrt(TAP_ROWS)
    anchor = jnp.zeros((), jnp.int32)

    def one_tile(total, item):
        clip, offset, cot = item
        field = lax.dynamic_slice(clip, (anchor, offset[0].astype(jnp.int32), offset[1].astype(jnp.int32), anchor), (FRAMES, TILE_H, TILE_W, CHAN))
        stored = []
        pre_acts = []
        for section in range(SEGMENTS):
            patches = gather_taps(field)
            pre = jnp.dot(patches, weights[section], preferred_element_type=jnp.float32) * scale
            stored.append(patches)
            pre_acts.append(pre)
            field = jax.nn.silu(pre).astype(jnp.bfloat16).reshape(FRAMES, TILE_H, TILE_W, CHAN)
        upstream = cot.reshape(-1, CHAN)
        pieces = [None] * SEGMENTS
        for section in range(SEGMENTS - 1, -1, -1):
            pre = pre_acts[section]
            sigma = jax.nn.sigmoid(pre)
            delta = (upstream.astype(jnp.float32) * sigma * (1.0 + pre * (1.0 - sigma))).astype(jnp.bfloat16)
            pieces[section] = lax.dot_general(stored[section], delta, (((0,), (0,)), ((), ())), preferred_element_type=jnp.float32) * scale
            if section > 0:
                back = lax.dot_general(delta, weights[section], (((1,), (1,)), ((), ())), preferred_element_type=jnp.float32)
                upstream = (spread_taps(back, FRAMES, TILE_H, TILE_W, CHAN) * scale).astype(jnp.bfloat16).reshape(-1, CHAN)
        return (total + jnp.stack(pieces), None)
    start = jnp.zeros((SEGMENTS, TAP_ROWS, CHAN), jnp.float32)
    total, _ = lax.scan(one_tile, start, (clips, offsets, cotangent))
    grads = total * (4.0 / math.sqrt(TILES * FRAMES * TILE_H * TILE_W))
    new_moment = beta_one * moment + (1.0 - beta_one) * stale_grads
    new_second = beta_two * second + (1.0 - beta_two) * stale_grads * stale_grads
    new_weights = (weights.astype(jnp.float32) - learn_rate * new_moment / (jnp.sqrt(new_second) + adam_eps)).astype(jnp.bfloat16)
    return (grads, new_moment, new_second, new_weights)
```

```python
import math

import jax
import jax.numpy as jnp
from jax import lax
from jax.experimental import pallas as pl
from jax.experimental.pallas import tpu as pltpu
from jax.sharding import PartitionSpec as P

beta_one = 0.9
beta_two = 0.95
learn_rate = 0.05
adam_eps = 1e-08

F32 = jnp.float32
BF16 = jnp.bfloat16
FRAMES, HEIGHT, WIDTH, CHAN = 4, 16, 8, 128
PLANE = HEIGHT * WIDTH
CELLS = FRAMES * PLANE
SECTIONS = 8
TAPS = 27
ROWS = TAPS * CHAN
SCALE = 2.0 / math.sqrt(ROWS)
GRAD_SCALE = SCALE * 4.0 / math.sqrt(32 * CELLS)


def dot(a, b):
    return jnp.dot(a, b, preferred_element_type=F32)


def store_shifted(store, value):
    row = lax.broadcasted_iota(jnp.int32, (CELLS, CHAN), 0) % HEIGHT
    zero = jnp.zeros_like(value)
    for b in range(3):
        if b == 0:
            moved = jnp.where(row == 0, zero, pltpu.roll(value, 1, 0))
        elif b == 1:
            moved = value
        else:
            moved = jnp.where(row == HEIGHT - 1, zero, pltpu.roll(value, CELLS - 1, 0))
        store(b, moved.astype(BF16).reshape(FRAMES, WIDTH, HEIGHT, CHAN))


def forward_section(s, w, taps, slope, last):
    total = None
    pieces = []
    for a in range(3):
        frames = 2 + a
        first = FRAMES - frames
        lhs = jnp.concatenate(
            [
                taps[s, a + first : a + FRAMES, c : c + WIDTH].reshape(frames * PLANE, 3 * CHAN)
                for c in range(3)
            ],
            axis=1,
        )
        rhs = jnp.concatenate(
            [w[s, (a * 3 + b) * 3 + c] for c in range(3) for b in range(3)], axis=0
        )
        pieces.append(dot(lhs, rhs))
    total = pieces[2]
    total = jnp.concatenate(
        [
            total[:PLANE],
            total[PLANE : 2 * PLANE] + pieces[1][:PLANE],
            total[2 * PLANE :] + pieces[1][PLANE:] + pieces[0],
        ],
        axis=0,
    )
    pre = total * SCALE
    sigma = jax.nn.sigmoid(pre)
    slope[s] = sigma * (1.0 + pre * (1.0 - sigma))

    @pl.when(s < last)
    def _():
        def store(b, moved):
            taps[s + 1, 2:, 1 : 1 + WIDTH, :, b * CHAN : (b + 1) * CHAN] = moved

        store_shifted(store, pre * sigma)


def shifted_delta(s, upstream, slope, back):
    delta = upstream[...] * slope[s]

    def store(b, moved):
        back[:FRAMES, 1 : 1 + WIDTH, :, b * CHAN : (b + 1) * CHAN] = moved

    store_shifted(store, delta)


def weight_grad(s, taps, back, put):
    field = taps[s, 2:, 1 : 1 + WIDTH, :, CHAN : 2 * CHAN].reshape(CELLS, CHAN)
    turned = field.astype(F32).T.astype(BF16)
    for a in range(3):
        frames = 2 + a
        lhs = turned[:, : frames * PLANE]
        for c in range(3):
            rhs = back[2 - a : 2 - a + frames, 2 - c : 2 - c + WIDTH].reshape(
                frames * PLANE, 3 * CHAN
            )
            out = dot(lhs, rhs) * GRAD_SCALE
            for b in range(3):
                put((a * 3 + b) * 3 + c, out[:, (2 - b) * CHAN : (3 - b) * CHAN])


def input_grad(s, w, back, upstream):
    pieces = []
    for a in range(3):
        frames = 2 + a
        lhs = jnp.concatenate(
            [
                back[2 - a : 2 - a + frames, 2 - c : 2 - c + WIDTH].reshape(
                    frames * PLANE, 3 * CHAN
                )
                for c in range(3)
            ],
            axis=1,
        )
        rhs = jnp.concatenate(
            [w[s, (a * 3 + 2 - b) * 3 + c] for c in range(3) for b in range(3)], axis=1
        )
        pieces.append(
            lax.dot_general(lhs, rhs, (((1,), (1,)), ((), ())), preferred_element_type=F32)
        )
    total = pieces[2]
    total = jnp.concatenate(
        [
            total[: 2 * PLANE] + pieces[1][: 2 * PLANE] + pieces[0],
            total[2 * PLANE : 3 * PLANE] + pieces[1][2 * PLANE :],
            total[3 * PLANE :],
        ],
        axis=0,
    )
    upstream[...] = total * SCALE


def crop(clip, offset_y, offset_x, taps):
    row = lax.broadcasted_iota(jnp.int32, (PLANE, clip.shape[-2]), 0)
    col = lax.broadcasted_iota(jnp.int32, (PLANE, clip.shape[-2]), 1)
    clip_w = 16
    want = (row % HEIGHT + offset_y) * clip_w + row // HEIGHT + offset_x
    pick = jnp.where(want == col, 1.0, 0.0).astype(BF16)
    field = jnp.concatenate([dot(pick, clip[t]) for t in range(FRAMES)], axis=0)

    def store(b, moved):
        taps[0, 2:, 1 : 1 + WIDTH, :, b * CHAN : (b + 1) * CHAN] = moved

    store_shifted(store, field)


def reorder(cotangent, upstream):
    row = lax.broadcasted_iota(jnp.int32, (PLANE, PLANE), 0)
    col = lax.broadcasted_iota(jnp.int32, (PLANE, PLANE), 1)
    pick = jnp.where(row % HEIGHT * WIDTH + row // HEIGHT == col, 1.0, 0.0).astype(BF16)
    for t in range(FRAMES):
        upstream[t * PLANE : (t + 1) * PLANE] = dot(pick, cotangent[t])


def clear_edges(taps, back):
    def wipe(s, _):
        taps[s, :2] = jnp.zeros((2, WIDTH + 2, HEIGHT, 3 * CHAN), BF16)
        taps[s, 2:, 0] = jnp.zeros((FRAMES, HEIGHT, 3 * CHAN), BF16)
        taps[s, 2:, WIDTH + 1] = jnp.zeros((FRAMES, HEIGHT, 3 * CHAN), BF16)
        return 0

    lax.fori_loop(0, SECTIONS, wipe, 0)
    back[FRAMES:] = jnp.zeros((2, WIDTH + 2, HEIGHT, 3 * CHAN), BF16)
    back[:FRAMES, 0] = jnp.zeros((FRAMES, HEIGHT, 3 * CHAN), BF16)
    back[:FRAMES, WIDTH + 1] = jnp.zeros((FRAMES, HEIGHT, 3 * CHAN), BF16)


def window_kernel(offsets, clips, w, cotangent, out, taps, back, slope, upstream):
    segment = lax.axis_index("segment")
    depth = segment // 2
    mine = segment % 2
    clear_edges(taps, back)
    crop(clips.at[mine], offsets[mine, 0], offsets[mine, 1], taps)
    reorder(cotangent.at[mine], upstream)

    def forward(s, _):
        forward_section(s, w, taps, slope, SECTIONS - 1)
        return 0

    lax.fori_loop(0, SECTIONS, forward, 0)

    def backward(i, _):
        s = SECTIONS - 1 - i
        shifted_delta(s, upstream, slope, back)

        @pl.when(s // 2 == depth)
        def _():
            def put(tap, block):
                out[s % 2, tap] = block.astype(BF16)

            weight_grad(s, taps, back, put)

        @pl.when(s > 0)
        def _():
            input_grad(s, w, back, upstream)

        return 0

    lax.fori_loop(0, SECTIONS, backward, 0)


def window(offsets, clips, w, cotangent):
    vmem = pl.BlockSpec(memory_space=pltpu.VMEM)
    return pl.pallas_call(
        window_kernel,
        out_shape=jax.ShapeDtypeStruct((2, TAPS, CHAN, CHAN), BF16),
        in_specs=[pl.BlockSpec(memory_space=pltpu.SMEM), vmem, vmem, vmem],
        out_specs=vmem,
        scratch_shapes=[
            pltpu.VMEM((SECTIONS, FRAMES + 2, WIDTH + 2, HEIGHT, 3 * CHAN), BF16),
            pltpu.VMEM((FRAMES + 2, WIDTH + 2, HEIGHT, 3 * CHAN), BF16),
            pltpu.VMEM((SECTIONS, CELLS, CHAN), F32),
            pltpu.VMEM((CELLS, CHAN), F32),
        ],
        compiler_params=pltpu.CompilerParams(vmem_limit_bytes=56 << 20),
    )(offsets, clips, w, cotangent)


def adam_rows(weights, moment, second, stale_grads):
    rows = moment.shape[1]
    start = lax.axis_index("replica") * rows
    local = lax.dynamic_slice_in_dim(weights[0], start, rows, 0).astype(F32)
    first_new = beta_one * moment[0] + (1.0 - beta_one) * stale_grads[0]
    second_new = beta_two * second[0] + (1.0 - beta_two) * stale_grads[0] * stale_grads[0]
    fresh = (local - learn_rate * first_new / (jnp.sqrt(second_new) + adam_eps)).astype(BF16)
    whole = lax.all_gather(fresh, "replica", axis=0, tiled=True)
    return (first_new[None], second_new[None], whole[None])


def shards(clips, offsets, weights, moment, second, stale_grads, cotangent):
    micro = clips.shape[0]
    mine = lax.axis_index("segment") % 2
    gathered = lax.all_gather(weights[0], "segment", axis=0)
    partial = window(
        offsets,
        clips.reshape(micro, FRAMES, -1, CHAN),
        gathered.reshape(SECTIONS, TAPS, CHAN, CHAN),
        cotangent.reshape(micro, FRAMES, PLANE, CHAN),
    )
    keep = lax.dynamic_index_in_dim(partial, mine, 0, keepdims=False)
    give = lax.dynamic_index_in_dim(partial, 1 - mine, 0, keepdims=False)
    taken = lax.ppermute(give, "segment", [(s, s ^ 1) for s in range(SECTIONS)])
    pair = (keep.astype(F32) + taken.astype(F32)).astype(BF16)
    count = lax.axis_size("replica")
    pieces = lax.all_to_all(pair.reshape(count, -1, CHAN), "replica", 0, 0, tiled=True)
    grads = jnp.sum(pieces.astype(F32), axis=0)
    first_new, second_new, whole = adam_rows(weights, moment, second, stale_grads)
    return (grads[None], first_new, second_new, whole)


def solution(mesh):
    placed = (
        P("replica", None, None, None, None),
        P("replica", None),
        P("segment", None, None),
        P("segment", "replica", None),
        P("segment", "replica", None),
        P("segment", "replica", None),
        P("replica", None, None, None, None),
    )
    return jax.shard_map(
        shards,
        mesh=mesh,
        in_specs=placed,
        out_specs=(
            P("segment", "replica", None),
            P("segment", "replica", None),
            P("segment", "replica", None),
            P("segment", None, None),
        ),
        check_vma=False,
    )
```

```python
import math

import jax
import jax.numpy as jnp
from jax import lax
from jax.experimental import pallas as pl
from jax.experimental.pallas import tpu as pltpu
from jax.sharding import PartitionSpec as P

beta_one = 0.9
beta_two = 0.95
learn_rate = 0.05
adam_eps = 1e-08

F32 = jnp.float32
BF16 = jnp.bfloat16
FRAMES, HEIGHT, WIDTH, CHAN = 4, 16, 8, 128
PLANE = HEIGHT * WIDTH
CELLS = FRAMES * PLANE
SECTIONS = 8
TAPS = 27
ROWS = TAPS * CHAN
SCALE = 2.0 / math.sqrt(ROWS)
GRAD_SCALE = SCALE * 4.0 / math.sqrt(32 * CELLS)


def dot(a, b):
    return jnp.dot(a, b, preferred_element_type=F32)


def store_shifted(store, value):
    row = lax.broadcasted_iota(jnp.int32, (CELLS, CHAN), 0) % HEIGHT
    zero = jnp.zeros_like(value)
    for b in range(3):
        if b == 0:
            moved = jnp.where(row == 0, zero, pltpu.roll(value, 1, 0))
        elif b == 1:
            moved = value
        else:
            moved = jnp.where(row == HEIGHT - 1, zero, pltpu.roll(value, CELLS - 1, 0))
        store(b, moved.astype(BF16).reshape(FRAMES, WIDTH, HEIGHT, CHAN))


def tap_rows(w, s, tap):
    return w[s, tap * CHAN : (tap + 1) * CHAN]


def forward_section(s, w, taps, slope, last):
    total = None
    pieces = []
    for a in range(3):
        frames = 2 + a
        first = FRAMES - frames
        lhs = jnp.concatenate(
            [
                taps[s, a + first : a + FRAMES, c : c + WIDTH].reshape(frames * PLANE, 3 * CHAN)
                for c in range(3)
            ],
            axis=1,
        )
        rhs = jnp.concatenate(
            [tap_rows(w, s, (a * 3 + b) * 3 + c) for c in range(3) for b in range(3)], axis=0
        )
        pieces.append(dot(lhs, rhs))
    total = pieces[2]
    total = jnp.concatenate(
        [
            total[:PLANE],
            total[PLANE : 2 * PLANE] + pieces[1][:PLANE],
            total[2 * PLANE :] + pieces[1][PLANE:] + pieces[0],
        ],
        axis=0,
    )
    pre = total * SCALE
    sigma = jax.nn.sigmoid(pre)
    slope[s] = sigma * (1.0 + pre * (1.0 - sigma))

    @pl.when(s < last)
    def _():
        def store(b, moved):
            taps[s + 1, 2:, 1 : 1 + WIDTH, :, b * CHAN : (b + 1) * CHAN] = moved

        store_shifted(store, pre * sigma)


def shifted_delta(s, upstream, slope, back):
    delta = upstream[...] * slope[s]

    def store(b, moved):
        back[:FRAMES, 1 : 1 + WIDTH, :, b * CHAN : (b + 1) * CHAN] = moved

    store_shifted(store, delta)


def weight_grad(s, taps, back, put):
    field = taps[s, 2:, 1 : 1 + WIDTH, :, CHAN : 2 * CHAN].reshape(CELLS, CHAN)
    turned = field.astype(F32).T.astype(BF16)
    for a in range(3):
        frames = 2 + a
        lhs = turned[:, : frames * PLANE]
        for c in range(3):
            rhs = back[2 - a : 2 - a + frames, 2 - c : 2 - c + WIDTH].reshape(
                frames * PLANE, 3 * CHAN
            )
            out = dot(lhs, rhs) * GRAD_SCALE
            for b in range(3):
                put((a * 3 + b) * 3 + c, out[:, (2 - b) * CHAN : (3 - b) * CHAN])


def input_grad(s, w, back, upstream):
    pieces = []
    for a in range(3):
        frames = 2 + a
        lhs = jnp.concatenate(
            [
                back[2 - a : 2 - a + frames, 2 - c : 2 - c + WIDTH].reshape(
                    frames * PLANE, 3 * CHAN
                )
                for c in range(3)
            ],
            axis=1,
        )
        rhs = jnp.concatenate(
            [tap_rows(w, s, (a * 3 + 2 - b) * 3 + c) for c in range(3) for b in range(3)], axis=1
        )
        pieces.append(
            lax.dot_general(lhs, rhs, (((1,), (1,)), ((), ())), preferred_element_type=F32)
        )
    total = pieces[2]
    total = jnp.concatenate(
        [
            total[: 2 * PLANE] + pieces[1][: 2 * PLANE] + pieces[0],
            total[2 * PLANE : 3 * PLANE] + pieces[1][2 * PLANE :],
            total[3 * PLANE :],
        ],
        axis=0,
    )
    upstream[...] = total * SCALE


def crop(clip, offset_y, offset_x, taps):
    row = lax.broadcasted_iota(jnp.int32, (PLANE, clip.shape[-2]), 0)
    col = lax.broadcasted_iota(jnp.int32, (PLANE, clip.shape[-2]), 1)
    clip_w = 16
    want = (row % HEIGHT + offset_y) * clip_w + row // HEIGHT + offset_x
    pick = jnp.where(want == col, 1.0, 0.0).astype(BF16)
    field = jnp.concatenate([dot(pick, clip[t]) for t in range(FRAMES)], axis=0)

    def store(b, moved):
        taps[0, 2:, 1 : 1 + WIDTH, :, b * CHAN : (b + 1) * CHAN] = moved

    store_shifted(store, field)


def reorder(cotangent, upstream):
    row = lax.broadcasted_iota(jnp.int32, (PLANE, PLANE), 0)
    col = lax.broadcasted_iota(jnp.int32, (PLANE, PLANE), 1)
    pick = jnp.where(row % HEIGHT * WIDTH + row // HEIGHT == col, 1.0, 0.0).astype(BF16)
    for t in range(FRAMES):
        upstream[t * PLANE : (t + 1) * PLANE] = dot(pick, cotangent[t])


def clear_edges(taps, back):
    def wipe(s, _):
        taps[s, :2] = jnp.zeros((2, WIDTH + 2, HEIGHT, 3 * CHAN), BF16)
        taps[s, 2:, 0] = jnp.zeros((FRAMES, HEIGHT, 3 * CHAN), BF16)
        taps[s, 2:, WIDTH + 1] = jnp.zeros((FRAMES, HEIGHT, 3 * CHAN), BF16)
        return 0

    lax.fori_loop(0, SECTIONS, wipe, 0)
    back[FRAMES:] = jnp.zeros((2, WIDTH + 2, HEIGHT, 3 * CHAN), BF16)
    back[:FRAMES, 0] = jnp.zeros((FRAMES, HEIGHT, 3 * CHAN), BF16)
    back[:FRAMES, WIDTH + 1] = jnp.zeros((FRAMES, HEIGHT, 3 * CHAN), BF16)


MESH_ID = pl.DeviceIdType.MESH
HALF = ROWS // 2
PIECE = HALF // 4


class Place:
    def __init__(self):
        segment = lax.axis_index("segment")
        replica = lax.axis_index("replica")
        self.z, self.hi = segment // 2, segment % 2
        self.lo, self.y, self.core = replica // 8, replica // 2 % 4, replica % 2

    def at(self, dz=0, hi=0, lo=0, dy=0, core=0):
        z = (self.z + dz) % 4
        y = (self.y + dy) % 4
        own = [(self.hi + hi) % 2, (self.lo + lo) % 2, (self.core + core) % 2]
        return (z * 2 + own[0], own[1] * 8 + y * 2 + own[2])

    def partners(self):
        away = [self.at(dz=k) for k in (1, 2, 3)]
        across = [self.at(dz=k, hi=1, lo=1) for k in range(4)]
        return away + across + [self.at(lo=1)] + [self.at(dy=k) for k in (1, 2, 3)] + [self.at(core=1)]


def remote(src, dst, send, receive, device):
    return pltpu.make_async_remote_copy(
        src_ref=src,
        dst_ref=dst,
        send_sem=send,
        recv_sem=receive,
        device_id=device,
        device_id_type=MESH_ID,
    )


def by_pair(dz, dh):
    return (dz % 2 == 1) if dh == 0 else (dz == 0)


class Gather:
    def __init__(self, here, w, first_send, first_recv, pair_sem, ring_send, ring_recv, core_sem):
        self.here, self.w = here, w
        self.first_send, self.first_recv = first_send, first_recv
        self.pair_sem, self.ring_send, self.ring_recv = pair_sem, ring_send, ring_recv
        self.core_sem = core_sem
        self.own = here.z * 2 + here.hi

    def rows(self, s, start, count):
        return self.w.at[s, pl.ds(pl.multiple_of(start, PIECE), count)]

    def half(self, s, core):
        return self.rows(s, core * HALF, HALF)

    def pair_part(self, s, lo):
        return self.rows(s, self.here.core * HALF + lo * 2 * PIECE, 2 * PIECE)

    def ring_part(self, s, y):
        return self.rows(s, self.here.core * HALF + y * PIECE, PIECE)

    def firsts(self):
        for slot, (dz, dh) in enumerate([(1, 0), (3, 0), (0, 1), (2, 0), (1, 1), (3, 1), (2, 1)]):
            if by_pair(dz, dh):
                part = self.pair_part(self.own, self.here.lo)
            else:
                part = self.ring_part(self.own, self.here.y)
            yield remote(
                part,
                part,
                self.first_send.at[slot],
                self.first_recv.at[self.own],
                self.here.at(dz=dz, hi=dh, lo=dh),
            )

    def start(self):
        for copy in self.firsts():
            copy.start()

    def paired(self, s):
        dz = (self.here.z + 4 - s // 2) % 4
        dh = (self.here.hi + s) % 2
        return dh, ((1 - dh) * (dz % 2) + dh * ((dz + 3) // 4 * -1 + 1)) == 1

    def relay(self, s):
        here = self.here
        dh, paired = self.paired(s)

        @pl.when(paired)
        def _():
            part = self.pair_part(s, (here.lo + dh) % 2)
            remote(part, part, self.first_send.at[0], self.first_recv.at[s], here.at()).wait_recv()
            self.pair_copy(s, dh).start()

        @pl.when(jnp.logical_not(paired))
        def _():
            part = self.ring_part(s, here.y)
            remote(part, part, self.first_send.at[0], self.first_recv.at[s], here.at()).wait_recv()
            for k in (1, 3, 2):
                self.ring_copy(s, k).start()

    def pair_copy(self, s, dh):
        part = self.pair_part(s, (self.here.lo + dh) % 2)
        return remote(
            part, part, self.pair_sem.at[0, s], self.pair_sem.at[1, s], self.here.at(lo=1)
        )

    def ring_copy(self, s, k):
        part = self.ring_part(s, self.here.y)
        return remote(
            part, part, self.ring_send.at[s, k - 1], self.ring_recv.at[s, k - 1], self.here.at(dy=k)
        )

    def core_copy(self, s):
        part = self.half(s, self.here.core)
        return remote(
            part, part, self.core_sem.at[0, s], self.core_sem.at[1, s], self.here.at(core=1)
        )

    def swap(self, s):
        here = self.here
        dh, paired = self.paired(s)

        @pl.when(paired)
        def _():
            part = self.pair_part(s, (here.lo + dh + 1) % 2)
            remote(
                part, part, self.pair_sem.at[0, s], self.pair_sem.at[1, s], here.at(lo=1)
            ).wait_recv()

        @pl.when(jnp.logical_not(paired))
        def _():
            for k in (1, 3, 2):
                part = self.ring_part(s, (here.y + 4 - k) % 4)
                remote(
                    part,
                    part,
                    self.ring_send.at[s, k - 1],
                    self.ring_recv.at[s, k - 1],
                    here.at(dy=k),
                ).wait_recv()

        self.core_copy(s).start()

    def arrive(self, s):
        part = self.half(s, 1 - self.here.core)
        remote(
            part, part, self.core_sem.at[0, s], self.core_sem.at[1, s], self.here.at(core=1)
        ).wait_recv()

    def finish(self):
        for copy in self.firsts():
            copy.wait_send()

        def each(s, _):
            @pl.when(s != self.own)
            def _():
                dh, paired = self.paired(s)

                @pl.when(paired)
                def _():
                    self.pair_copy(s, dh).wait_send()

                @pl.when(jnp.logical_not(paired))
                def _():
                    for k in (1, 3, 2):
                        self.ring_copy(s, k).wait_send()

                self.core_copy(s).wait_send()

            return 0

        lax.fori_loop(0, SECTIONS, each, 0)


def window_kernel(
    offsets,
    clips,
    weights,
    cotangent,
    out,
    w,
    taps,
    back,
    slope,
    upstream,
    load_sem,
    first_send,
    first_recv,
    pair_sem,
    ring_send,
    ring_recv,
    core_sem,
):
    here = Place()
    gather = Gather(here, w, first_send, first_recv, pair_sem, ring_send, ring_recv, core_sem)
    load = pltpu.make_async_copy(weights, w.at[gather.own], load_sem)
    load.start()
    barrier = pltpu.get_barrier_semaphore()
    partners = here.partners()
    for partner in partners:
        pl.semaphore_signal(barrier, inc=1, device_id=partner, device_id_type=MESH_ID)
    load.wait()
    pl.semaphore_wait(barrier, len(partners))
    gather.start()

    clear_edges(taps, back)
    crop(clips.at[here.hi], offsets[here.hi, 0], offsets[here.hi, 1], taps)
    reorder(cotangent.at[here.hi], upstream)

    def forward(tick, _):
        @pl.when((tick < SECTIONS) & (tick != gather.own))
        def _():
            gather.relay(tick)

        later = tick - 1

        @pl.when((later >= 0) & (later < SECTIONS) & (later != gather.own))
        def _():
            gather.swap(later)

        s = tick - 2

        @pl.when(s >= 0)
        def _():
            @pl.when(s != gather.own)
            def _():
                gather.arrive(s)

            forward_section(s, w, taps, slope, SECTIONS - 1)

        return 0

    lax.fori_loop(0, SECTIONS + 2, forward, 0)

    def backward(i, _):
        s = SECTIONS - 1 - i
        shifted_delta(s, upstream, slope, back)

        @pl.when(s // 2 == here.z)
        def _():
            def put(tap, block):
                out[s % 2, tap] = block.astype(BF16)

            weight_grad(s, taps, back, put)

        @pl.when(s > 0)
        def _():
            input_grad(s, w, back, upstream)

        return 0

    lax.fori_loop(0, SECTIONS, backward, 0)
    gather.finish()


def window(offsets, clips, weights, cotangent):
    vmem = pl.BlockSpec(memory_space=pltpu.VMEM)
    dma = pltpu.SemaphoreType.DMA
    return pl.pallas_call(
        window_kernel,
        out_shape=jax.ShapeDtypeStruct((2, TAPS, CHAN, CHAN), BF16),
        in_specs=[
            pl.BlockSpec(memory_space=pltpu.SMEM),
            vmem,
            pl.BlockSpec(memory_space=pl.ANY),
            vmem,
        ],
        out_specs=vmem,
        scratch_shapes=[
            pltpu.VMEM((SECTIONS, ROWS, CHAN), BF16),
            pltpu.VMEM((SECTIONS, FRAMES + 2, WIDTH + 2, HEIGHT, 3 * CHAN), BF16),
            pltpu.VMEM((FRAMES + 2, WIDTH + 2, HEIGHT, 3 * CHAN), BF16),
            pltpu.VMEM((SECTIONS, CELLS, CHAN), F32),
            pltpu.VMEM((CELLS, CHAN), F32),
            dma,
            dma((7,)),
            dma((SECTIONS,)),
            dma((2, SECTIONS)),
            dma((SECTIONS, 3)),
            dma((SECTIONS, 3)),
            dma((2, SECTIONS)),
        ],
        compiler_params=pltpu.CompilerParams(
            vmem_limit_bytes=56 << 20, collective_id=0, has_side_effects=True
        ),
    )(offsets, clips, weights, cotangent)


def adam_rows(weights, moment, second, stale_grads):
    rows = moment.shape[1]
    start = lax.axis_index("replica") * rows
    local = lax.dynamic_slice_in_dim(weights[0], start, rows, 0).astype(F32)
    first_new = beta_one * moment[0] + (1.0 - beta_one) * stale_grads[0]
    second_new = beta_two * second[0] + (1.0 - beta_two) * stale_grads[0] * stale_grads[0]
    fresh = (local - learn_rate * first_new / (jnp.sqrt(second_new) + adam_eps)).astype(BF16)
    whole = lax.all_gather(fresh, "replica", axis=0, tiled=True)
    return (first_new[None], second_new[None], whole[None])


def shards(clips, offsets, weights, moment, second, stale_grads, cotangent):
    micro = clips.shape[0]
    mine = lax.axis_index("segment") % 2
    partial = window(
        offsets,
        clips.reshape(micro, FRAMES, -1, CHAN),
        weights[0],
        cotangent.reshape(micro, FRAMES, PLANE, CHAN),
    )
    keep = lax.dynamic_index_in_dim(partial, mine, 0, keepdims=False)
    give = lax.dynamic_index_in_dim(partial, 1 - mine, 0, keepdims=False)
    taken = lax.ppermute(give, "segment", [(s, s ^ 1) for s in range(SECTIONS)])
    pair = (keep.astype(F32) + taken.astype(F32)).astype(BF16)
    count = lax.axis_size("replica")
    pieces = lax.all_to_all(pair.reshape(count, -1, CHAN), "replica", 0, 0, tiled=True)
    grads = jnp.sum(pieces.astype(F32), axis=0)
    first_new, second_new, whole = adam_rows(weights, moment, second, stale_grads)
    return (grads[None], first_new, second_new, whole)


def solution(mesh):
    placed = (
        P("replica", None, None, None, None),
        P("replica", None),
        P("segment", None, None),
        P("segment", "replica", None),
        P("segment", "replica", None),
        P("segment", "replica", None),
        P("replica", None, None, None, None),
    )
    return jax.shard_map(
        shards,
        mesh=mesh,
        in_specs=placed,
        out_specs=(
            P("segment", "replica", None),
            P("segment", "replica", None),
            P("segment", "replica", None),
            P("segment", None, None),
        ),
        check_vma=False,
    )
```

```python
import math

import jax
import jax.numpy as jnp
from jax import lax
from jax.experimental import pallas as pl
from jax.experimental.pallas import tpu as pltpu
from jax.sharding import PartitionSpec as P

beta_one = 0.9
beta_two = 0.95
learn_rate = 0.05
adam_eps = 1e-08

F32 = jnp.float32
BF16 = jnp.bfloat16
FRAMES, HEIGHT, WIDTH, CHAN = 4, 16, 8, 128
PLANE = HEIGHT * WIDTH
CELLS = FRAMES * PLANE
SECTIONS = 8
TAPS = 27
ROWS = TAPS * CHAN
SCALE = 2.0 / math.sqrt(ROWS)
GRAD_SCALE = SCALE * 4.0 / math.sqrt(32 * CELLS)


def dot(a, b):
    return jnp.dot(a, b, preferred_element_type=F32)


def store_shifted(store, value):
    row = lax.broadcasted_iota(jnp.int32, (CELLS, CHAN), 0) % HEIGHT
    zero = jnp.zeros_like(value)
    for b in range(3):
        if b == 0:
            moved = jnp.where(row == 0, zero, pltpu.roll(value, 1, 0))
        elif b == 1:
            moved = value
        else:
            moved = jnp.where(row == HEIGHT - 1, zero, pltpu.roll(value, CELLS - 1, 0))
        store(b, moved.astype(BF16).reshape(FRAMES, WIDTH, HEIGHT, CHAN))


def tap_rows(w, s, tap):
    return w[s, tap * CHAN : (tap + 1) * CHAN]


def forward_section(s, w, taps, slope, last):
    total = None
    pieces = []
    for a in range(3):
        frames = 2 + a
        first = FRAMES - frames
        lhs = jnp.concatenate(
            [
                taps[s, a + first : a + FRAMES, c : c + WIDTH].reshape(frames * PLANE, 3 * CHAN)
                for c in range(3)
            ],
            axis=1,
        )
        rhs = jnp.concatenate(
            [tap_rows(w, s, (a * 3 + b) * 3 + c) for c in range(3) for b in range(3)], axis=0
        )
        pieces.append(dot(lhs, rhs))
    total = pieces[2]
    total = jnp.concatenate(
        [
            total[:PLANE],
            total[PLANE : 2 * PLANE] + pieces[1][:PLANE],
            total[2 * PLANE :] + pieces[1][PLANE:] + pieces[0],
        ],
        axis=0,
    )
    pre = total * SCALE
    sigma = jax.nn.sigmoid(pre)
    slope[s] = sigma * (1.0 + pre * (1.0 - sigma))

    @pl.when(s < last)
    def _():
        def store(b, moved):
            taps[s + 1, 2:, 1 : 1 + WIDTH, :, b * CHAN : (b + 1) * CHAN] = moved

        store_shifted(store, pre * sigma)


def shifted_delta(s, upstream, slope, back):
    delta = upstream[...] * slope[s]

    def store(b, moved):
        back[:FRAMES, 1 : 1 + WIDTH, :, b * CHAN : (b + 1) * CHAN] = moved

    store_shifted(store, delta)


def weight_grad(s, taps, back, put):
    field = taps[s, 2:, 1 : 1 + WIDTH, :, CHAN : 2 * CHAN].reshape(CELLS, CHAN)
    turned = field.astype(F32).T.astype(BF16)
    for a in range(3):
        frames = 2 + a
        lhs = turned[:, : frames * PLANE]
        for c in range(3):
            rhs = back[2 - a : 2 - a + frames, 2 - c : 2 - c + WIDTH].reshape(
                frames * PLANE, 3 * CHAN
            )
            out = dot(lhs, rhs) * GRAD_SCALE
            for b in range(3):
                put((a * 3 + b) * 3 + c, out[:, (2 - b) * CHAN : (3 - b) * CHAN])


def input_grad(s, w, back, upstream):
    pieces = []
    for a in range(3):
        frames = 2 + a
        lhs = jnp.concatenate(
            [
                back[2 - a : 2 - a + frames, 2 - c : 2 - c + WIDTH].reshape(
                    frames * PLANE, 3 * CHAN
                )
                for c in range(3)
            ],
            axis=1,
        )
        rhs = jnp.concatenate(
            [tap_rows(w, s, (a * 3 + 2 - b) * 3 + c) for c in range(3) for b in range(3)], axis=1
        )
        pieces.append(
            lax.dot_general(lhs, rhs, (((1,), (1,)), ((), ())), preferred_element_type=F32)
        )
    total = pieces[2]
    total = jnp.concatenate(
        [
            total[: 2 * PLANE] + pieces[1][: 2 * PLANE] + pieces[0],
            total[2 * PLANE : 3 * PLANE] + pieces[1][2 * PLANE :],
            total[3 * PLANE :],
        ],
        axis=0,
    )
    upstream[...] = total * SCALE


def crop(clip, offset_y, offset_x, taps):
    row = lax.broadcasted_iota(jnp.int32, (PLANE, clip.shape[-2]), 0)
    col = lax.broadcasted_iota(jnp.int32, (PLANE, clip.shape[-2]), 1)
    clip_w = 16
    want = (row % HEIGHT + offset_y) * clip_w + row // HEIGHT + offset_x
    pick = jnp.where(want == col, 1.0, 0.0).astype(BF16)
    field = jnp.concatenate([dot(pick, clip[t]) for t in range(FRAMES)], axis=0)

    def store(b, moved):
        taps[0, 2:, 1 : 1 + WIDTH, :, b * CHAN : (b + 1) * CHAN] = moved

    store_shifted(store, field)


def reorder(cotangent, upstream):
    row = lax.broadcasted_iota(jnp.int32, (PLANE, PLANE), 0)
    col = lax.broadcasted_iota(jnp.int32, (PLANE, PLANE), 1)
    pick = jnp.where(row % HEIGHT * WIDTH + row // HEIGHT == col, 1.0, 0.0).astype(BF16)
    for t in range(FRAMES):
        upstream[t * PLANE : (t + 1) * PLANE] = dot(pick, cotangent[t])


def clear_edges(taps, back):
    def wipe(s, _):
        taps[s, :2] = jnp.zeros((2, WIDTH + 2, HEIGHT, 3 * CHAN), BF16)
        taps[s, 2:, 0] = jnp.zeros((FRAMES, HEIGHT, 3 * CHAN), BF16)
        taps[s, 2:, WIDTH + 1] = jnp.zeros((FRAMES, HEIGHT, 3 * CHAN), BF16)
        return 0

    lax.fori_loop(0, SECTIONS, wipe, 0)
    back[FRAMES:] = jnp.zeros((2, WIDTH + 2, HEIGHT, 3 * CHAN), BF16)
    back[:FRAMES, 0] = jnp.zeros((FRAMES, HEIGHT, 3 * CHAN), BF16)
    back[:FRAMES, WIDTH + 1] = jnp.zeros((FRAMES, HEIGHT, 3 * CHAN), BF16)


MESH_ID = pl.DeviceIdType.MESH
HALF = ROWS // 2
PIECE = HALF // 4
SHARD = ROWS // 16


class Place:
    def __init__(self):
        segment = lax.axis_index("segment")
        replica = lax.axis_index("replica")
        self.z, self.hi = segment // 2, segment % 2
        self.lo, self.y, self.core = replica // 8, replica // 2 % 4, replica % 2

    def at(self, dz=0, hi=0, lo=0, dy=0, core=0):
        z = (self.z + dz) % 4
        y = (self.y + dy) % 4
        own = [(self.hi + hi) % 2, (self.lo + lo) % 2, (self.core + core) % 2]
        return (z * 2 + own[0], own[1] * 8 + y * 2 + own[2])

    def partners(self):
        away = [self.at(dz=k) for k in (1, 2, 3)]
        across = [self.at(dz=k, hi=1, lo=1) for k in range(4)]
        return away + across + [self.at(lo=1), self.at(hi=1)] + [self.at(dy=k) for k in (1, 2, 3)] + [self.at(core=1)]


def remote(src, dst, send, receive, device):
    return pltpu.make_async_remote_copy(
        src_ref=src,
        dst_ref=dst,
        send_sem=send,
        recv_sem=receive,
        device_id=device,
        device_id_type=MESH_ID,
    )


def by_pair(dz, dh):
    return (dz % 2 == 1) if dh == 0 else (dz == 0)


class Gather:
    def __init__(self, here, w, first_send, first_recv, pair_sem, ring_send, ring_recv, core_sem):
        self.here, self.w = here, w
        self.first_send, self.first_recv = first_send, first_recv
        self.pair_sem, self.ring_send, self.ring_recv = pair_sem, ring_send, ring_recv
        self.core_sem = core_sem
        self.own = here.z * 2 + here.hi

    def rows(self, s, start, count):
        return self.w.at[s, pl.ds(pl.multiple_of(start, PIECE), count)]

    def half(self, s, core):
        return self.rows(s, core * HALF, HALF)

    def pair_part(self, s, lo):
        return self.rows(s, self.here.core * HALF + lo * 2 * PIECE, 2 * PIECE)

    def ring_part(self, s, y):
        return self.rows(s, self.here.core * HALF + y * PIECE, PIECE)

    def firsts(self):
        for slot, (dz, dh) in enumerate([(1, 0), (3, 0), (0, 1), (2, 0), (1, 1), (3, 1), (2, 1)]):
            if by_pair(dz, dh):
                part = self.pair_part(self.own, self.here.lo)
            else:
                part = self.ring_part(self.own, self.here.y)
            yield remote(
                part,
                part,
                self.first_send.at[slot],
                self.first_recv.at[self.own],
                self.here.at(dz=dz, hi=dh, lo=dh),
            )

    def start(self):
        for copy in self.firsts():
            copy.start()

    def paired(self, s):
        dz = (self.here.z + 4 - s // 2) % 4
        dh = (self.here.hi + s) % 2
        return dh, ((1 - dh) * (dz % 2) + dh * ((dz + 3) // 4 * -1 + 1)) == 1

    def relay(self, s):
        here = self.here
        dh, paired = self.paired(s)

        @pl.when(paired)
        def _():
            part = self.pair_part(s, (here.lo + dh) % 2)
            remote(part, part, self.first_send.at[0], self.first_recv.at[s], here.at()).wait_recv()
            self.pair_copy(s, dh).start()

        @pl.when(jnp.logical_not(paired))
        def _():
            part = self.ring_part(s, here.y)
            remote(part, part, self.first_send.at[0], self.first_recv.at[s], here.at()).wait_recv()
            for k in (1, 3, 2):
                self.ring_copy(s, k).start()

    def pair_copy(self, s, dh):
        part = self.pair_part(s, (self.here.lo + dh) % 2)
        return remote(
            part, part, self.pair_sem.at[0, s], self.pair_sem.at[1, s], self.here.at(lo=1)
        )

    def ring_copy(self, s, k):
        part = self.ring_part(s, self.here.y)
        return remote(
            part, part, self.ring_send.at[s, k - 1], self.ring_recv.at[s, k - 1], self.here.at(dy=k)
        )

    def core_copy(self, s):
        part = self.half(s, self.here.core)
        return remote(
            part, part, self.core_sem.at[0, s], self.core_sem.at[1, s], self.here.at(core=1)
        )

    def swap(self, s):
        here = self.here
        dh, paired = self.paired(s)

        @pl.when(paired)
        def _():
            part = self.pair_part(s, (here.lo + dh + 1) % 2)
            remote(
                part, part, self.pair_sem.at[0, s], self.pair_sem.at[1, s], here.at(lo=1)
            ).wait_recv()

        @pl.when(jnp.logical_not(paired))
        def _():
            for k in (1, 3, 2):
                part = self.ring_part(s, (here.y + 4 - k) % 4)
                remote(
                    part,
                    part,
                    self.ring_send.at[s, k - 1],
                    self.ring_recv.at[s, k - 1],
                    here.at(dy=k),
                ).wait_recv()

        self.core_copy(s).start()

    def arrive(self, s):
        part = self.half(s, 1 - self.here.core)
        remote(
            part, part, self.core_sem.at[0, s], self.core_sem.at[1, s], self.here.at(core=1)
        ).wait_recv()

    def finish(self):
        for copy in self.firsts():
            copy.wait_send()

        def each(s, _):
            @pl.when(s != self.own)
            def _():
                dh, paired = self.paired(s)

                @pl.when(paired)
                def _():
                    self.pair_copy(s, dh).wait_send()

                @pl.when(jnp.logical_not(paired))
                def _():
                    for k in (1, 3, 2):
                        self.ring_copy(s, k).wait_send()

                self.core_copy(s).wait_send()

            return 0

        lax.fori_loop(0, SECTIONS, each, 0)


class Exchange:
    def __init__(self, here, total, give, taken, summed, ring, kept, crossed, sems):
        self.here = here
        self.total, self.give, self.taken, self.summed = total, give, taken, summed
        self.ring, self.kept, self.crossed = ring, kept, crossed
        self.core_sem, self.ring_send, self.ring_recv, self.cross_send, self.cross_recv = sems

    def shard(self, i, j, core):
        start = pl.multiple_of((2 * j + core) * SHARD, 8)
        return self.total[i, pl.ds(start, SHARD)]

    def core_copy(self, i):
        return remote(
            self.give.at[i],
            self.taken.at[i],
            self.core_sem.at[0, i],
            self.core_sem.at[1, i],
            self.here.at(core=1),
        )

    def to_core(self, i):
        for j in range(8):
            self.give[i, j] = self.shard(i, j, 1 - self.here.core).astype(BF16)
        self.core_copy(i).start()

    def ring_copy(self, i, k):
        return remote(
            self.summed.at[i, :, (self.here.y + k) % 4],
            self.ring.at[i, k - 1],
            self.ring_send.at[i, k - 1],
            self.ring_recv.at[i, k - 1],
            self.here.at(dy=k),
        )

    def to_ring(self, i):
        self.core_copy(i).wait_recv()
        for j in range(8):
            both = self.shard(i, j, self.here.core) + self.taken[i, j].astype(F32)
            self.summed[i, j // 4, j % 4] = both.astype(BF16)
        for k in (2, 1, 3):
            self.ring_copy(i, k).start()

    def cross_copy(self, i, slot):
        hi, lo = ((0, 1), (1, 0), (1, 1))[slot]
        return remote(
            self.kept.at[i, (self.here.lo + lo) % 2],
            self.crossed.at[slot],
            self.cross_send.at[slot],
            self.cross_recv.at[slot],
            self.here.at(hi=hi, lo=lo),
        )

    def to_cross(self, i):
        for k in (1, 3, 2):
            self.ring_copy(i, k).wait_recv()
        for lo in range(2):
            value = self.summed[i, lo, self.here.y].astype(F32)
            for k in range(3):
                value = value + self.ring[i, k, lo].astype(F32)
            self.kept[i, lo] = value.astype(BF16)

        @pl.when(self.here.hi == i)
        def _():
            self.cross_copy(i, 0).start()

        @pl.when(self.here.hi != i)
        def _():
            self.cross_copy(i, 1).start()
            self.cross_copy(i, 2).start()

    def finish(self, grads):
        for slot in range(3):
            self.cross_copy(0, slot).wait_recv()
        value = self.kept[self.here.hi, self.here.lo].astype(F32)
        for slot in range(3):
            value = value + self.crossed[slot].astype(F32)
        grads[...] = value
        for i in range(2):
            self.core_copy(i).wait_send()
            for k in (1, 2, 3):
                self.ring_copy(i, k).wait_send()
        for slot in range(3):
            self.cross_copy(0, slot).wait_send()


class Renewal:
    def __init__(self, here, fresh, ring_sem, pair_sem, core_sem):
        self.here, self.fresh = here, fresh
        self.ring_sem, self.pair_sem, self.core_sem = ring_sem, pair_sem, core_sem

    def compute(self, rows, moment, second, stale, new_moment, new_second):
        here = self.here
        first = beta_one * moment[...] + (1.0 - beta_one) * stale[...]
        square = beta_two * second[...] + (1.0 - beta_two) * stale[...] * stale[...]
        new_moment[...] = first
        new_second[...] = square
        step = learn_rate * first / (jnp.sqrt(square) + adam_eps)
        self.fresh[here.lo, here.y, here.core] = (rows[...].astype(F32) - step).astype(BF16)

    def ring_copy(self, k, back=0):
        part = self.fresh.at[self.here.lo, (self.here.y + back) % 4, self.here.core]
        return remote(
            part, part, self.ring_sem.at[0, k - 1], self.ring_sem.at[1, k - 1], self.here.at(dy=k)
        )

    def pair_copy(self, lo=0):
        part = self.fresh.at[(self.here.lo + lo) % 2, :, self.here.core]
        return remote(part, part, self.pair_sem.at[0], self.pair_sem.at[1], self.here.at(lo=1))

    def core_copy(self, core=0):
        part = self.fresh.at[:, :, (self.here.core + core) % 2]
        return remote(part, part, self.core_sem.at[0], self.core_sem.at[1], self.here.at(core=1))

    def to_ring(self):
        for k in (2, 1, 3):
            self.ring_copy(k).start()

    def to_pair(self):
        for k in (1, 3, 2):
            self.ring_copy(k, 4 - k).wait_recv()
        self.pair_copy().start()

    def to_core(self):
        self.pair_copy(1).wait_recv()
        self.core_copy().start()

    def arrive(self):
        self.core_copy(1).wait_recv()

    def finish(self):
        for k in (1, 2, 3):
            self.ring_copy(k).wait_send()
        self.pair_copy().wait_send()
        self.core_copy().wait_send()


def window_kernel(
    offsets,
    clips,
    weights,
    shards16,
    moment,
    second,
    stale,
    cotangent,
    grads,
    new_moment,
    new_second,
    new_weights,
    w,
    taps,
    back,
    slope,
    upstream,
    rows,
    fresh,
    total,
    give,
    taken,
    summed,
    ring,
    kept,
    crossed,
    load_sem,
    first_send,
    first_recv,
    pair_sem,
    ring_send,
    ring_recv,
    core_sem,
    sum_core,
    sum_ring_send,
    sum_ring_recv,
    cross_send,
    cross_recv,
    renew_ring,
    renew_pair,
    renew_core,
):
    here = Place()
    gather = Gather(here, w, first_send, first_recv, pair_sem, ring_send, ring_recv, core_sem)
    exchange = Exchange(
        here,
        total,
        give,
        taken,
        summed,
        ring,
        kept,
        crossed,
        (sum_core, sum_ring_send, sum_ring_recv, cross_send, cross_recv),
    )
    renewal = Renewal(here, fresh, renew_ring, renew_pair, renew_core)
    load = pltpu.make_async_copy(weights, w.at[gather.own], load_sem.at[0])
    load.start()
    own_rows = pltpu.make_async_copy(
        shards16.at[here.lo * 8 + here.y * 2 + here.core], rows, load_sem.at[1]
    )
    own_rows.start()
    barrier = pltpu.get_barrier_semaphore()
    partners = here.partners()
    for partner in partners:
        pl.semaphore_signal(barrier, inc=1, device_id=partner, device_id_type=MESH_ID)
    load.wait()
    pl.semaphore_wait(barrier, len(partners))
    gather.start()

    clear_edges(taps, back)
    crop(clips.at[here.hi], offsets[here.hi, 0], offsets[here.hi, 1], taps)
    reorder(cotangent.at[here.hi], upstream)
    own_rows.wait()
    renewal.compute(rows, moment, second, stale, new_moment, new_second)

    def forward(tick, _):
        @pl.when((tick < SECTIONS) & (tick != gather.own))
        def _():
            gather.relay(tick)

        later = tick - 1

        @pl.when((later >= 0) & (later < SECTIONS) & (later != gather.own))
        def _():
            gather.swap(later)

        s = tick - 2

        @pl.when(s >= 0)
        def _():
            @pl.when(s != gather.own)
            def _():
                gather.arrive(s)

            forward_section(s, w, taps, slope, SECTIONS - 1)

        return 0

    lax.fori_loop(0, SECTIONS + 2, forward, 0)
    renewal.to_ring()

    def backward(i, _):
        s = SECTIONS - 1 - i
        shifted_delta(s, upstream, slope, back)

        @pl.when(s == 2 * here.z)
        def _():
            exchange.to_ring(1)

        @pl.when(s // 2 == here.z)
        def _():
            def put(tap, block):
                total[s % 2, tap * CHAN : (tap + 1) * CHAN] = block

            weight_grad(s, taps, back, put)
            exchange.to_core(s % 2)

        @pl.when(s == 2 * here.z)
        def _():
            exchange.to_cross(1)

        @pl.when(s > 0)
        def _():
            input_grad(s, w, back, upstream)

        @pl.when(s == 5)
        def _():
            renewal.to_pair()

        @pl.when(s == 3)
        def _():
            renewal.to_core()

        return 0

    lax.fori_loop(0, SECTIONS, backward, 0)
    renewal.arrive()
    store = pltpu.make_async_copy(fresh, new_weights, load_sem.at[0])
    store.start()
    exchange.to_ring(0)
    exchange.to_cross(0)
    exchange.finish(grads)
    renewal.finish()
    gather.finish()
    store.wait()


def window(offsets, clips, weights, moment, second, stale, cotangent):
    vmem = pl.BlockSpec(memory_space=pltpu.VMEM)
    away = pl.BlockSpec(memory_space=pl.ANY)
    dma = pltpu.SemaphoreType.DMA
    shard = jax.ShapeDtypeStruct((SHARD, CHAN), F32)
    return pl.pallas_call(
        window_kernel,
        out_shape=(shard, shard, shard, jax.ShapeDtypeStruct((2, 4, 2, SHARD, CHAN), BF16)),
        in_specs=[
            pl.BlockSpec(memory_space=pltpu.SMEM),
            vmem,
            away,
            away,
            vmem,
            vmem,
            vmem,
            vmem,
        ],
        out_specs=(vmem, vmem, vmem, away),
        scratch_shapes=[
            pltpu.VMEM((SECTIONS, ROWS, CHAN), BF16),
            pltpu.VMEM((SECTIONS, FRAMES + 2, WIDTH + 2, HEIGHT, 3 * CHAN), BF16),
            pltpu.VMEM((FRAMES + 2, WIDTH + 2, HEIGHT, 3 * CHAN), BF16),
            pltpu.VMEM((SECTIONS, CELLS, CHAN), F32),
            pltpu.VMEM((CELLS, CHAN), F32),
            pltpu.VMEM((SHARD, CHAN), BF16),
            pltpu.VMEM((2, 4, 2, SHARD, CHAN), BF16),
            pltpu.VMEM((2, ROWS, CHAN), F32),
            pltpu.VMEM((2, 8, SHARD, CHAN), BF16),
            pltpu.VMEM((2, 8, SHARD, CHAN), BF16),
            pltpu.VMEM((2, 2, 4, SHARD, CHAN), BF16),
            pltpu.VMEM((2, 3, 2, SHARD, CHAN), BF16),
            pltpu.VMEM((2, 2, SHARD, CHAN), BF16),
            pltpu.VMEM((3, SHARD, CHAN), BF16),
            dma((2,)),
            dma((7,)),
            dma((SECTIONS,)),
            dma((2, SECTIONS)),
            dma((SECTIONS, 3)),
            dma((SECTIONS, 3)),
            dma((2, SECTIONS)),
            dma((2, 2)),
            dma((2, 3)),
            dma((2, 3)),
            dma((3,)),
            dma((3,)),
            dma((2, 3)),
            dma((2,)),
            dma((2,)),
        ],
        compiler_params=pltpu.CompilerParams(
            vmem_limit_bytes=56 << 20, collective_id=0, has_side_effects=True
        ),
    )(
        offsets,
        clips,
        weights,
        weights.reshape(16, SHARD, CHAN),
        moment,
        second,
        stale,
        cotangent,
    )


def shards(clips, offsets, weights, moment, second, stale_grads, cotangent):
    micro = clips.shape[0]
    grads, first_new, second_new, fresh = window(
        offsets,
        clips.reshape(micro, FRAMES, -1, CHAN),
        weights[0],
        moment[0],
        second[0],
        stale_grads[0],
        cotangent.reshape(micro, FRAMES, PLANE, CHAN),
    )
    return (grads[None], first_new[None], second_new[None], fresh.reshape(1, ROWS, CHAN))


def solution(mesh):
    placed = (
        P("replica", None, None, None, None),
        P("replica", None),
        P("segment", None, None),
        P("segment", "replica", None),
        P("segment", "replica", None),
        P("segment", "replica", None),
        P("replica", None, None, None, None),
    )
    return jax.shard_map(
        shards,
        mesh=mesh,
        in_specs=placed,
        out_specs=(
            P("segment", "replica", None),
            P("segment", "replica", None),
            P("segment", "replica", None),
            P("segment", None, None),
        ),
        check_vma=False,
    )
```

```python
import math

import jax
import jax.numpy as jnp
from jax import lax
from jax.experimental import pallas as pl
from jax.experimental.pallas import tpu as pltpu
from jax.sharding import PartitionSpec as P

beta_one = 0.9
beta_two = 0.95
learn_rate = 0.05
adam_eps = 1e-08

F32 = jnp.float32
BF16 = jnp.bfloat16
FRAMES, HEIGHT, WIDTH, CHAN = 4, 16, 8, 128
PLANE = HEIGHT * WIDTH
CELLS = FRAMES * PLANE
SECTIONS = 8
TAPS = 27
ROWS = TAPS * CHAN
SCALE = 2.0 / math.sqrt(ROWS)
GRAD_SCALE = SCALE * 4.0 / math.sqrt(32 * CELLS)


def dot(a, b):
    return jnp.dot(a, b, preferred_element_type=F32)


def store_shifted(store, value):
    row = lax.broadcasted_iota(jnp.int32, (CELLS, CHAN), 0) % HEIGHT
    zero = jnp.zeros_like(value)
    for b in range(3):
        if b == 0:
            moved = jnp.where(row == 0, zero, pltpu.roll(value, 1, 0))
        elif b == 1:
            moved = value
        else:
            moved = jnp.where(row == HEIGHT - 1, zero, pltpu.roll(value, CELLS - 1, 0))
        store(b, moved.astype(BF16).reshape(FRAMES, WIDTH, HEIGHT, CHAN))


def tap_rows(w, s, tap):
    return w[s, tap * CHAN : (tap + 1) * CHAN]


def dot_turned(a, b):
    return lax.dot_general(a, b, (((1,), (1,)), ((), ())), preferred_element_type=F32)


def tap_block(w, s, times, turn, axis):
    columns = []
    for a in times:
        taps = [turn(b, c) for c in range(3) for b in range(3)]
        columns.append(
            jnp.concatenate([tap_rows(w, s, (a * 3 + b) * 3 + c) for b, c in taps], axis=axis)
        )
    return jnp.concatenate(columns, axis=1 - axis)


def field_columns(field):
    padded = field.reshape(FRAMES, WIDTH + 2, HEIGHT, 3 * CHAN)
    return jnp.concatenate(
        [padded[:, c : c + WIDTH].reshape(CELLS, 3 * CHAN) for c in range(3)], axis=1
    )


def forward_section(s, w, taps, slope, last):
    field = taps[s].reshape(FRAMES * (WIDTH + 2) * HEIGHT, 3 * CHAN)
    lhs = field_columns(field)
    late = dot(lhs, tap_block(w, s, (1, 2), lambda b, c: (b, c), 0))
    early = dot(lhs[: 2 * PLANE], tap_block(w, s, (0,), lambda b, c: (b, c), 0))
    total = late[:, CHAN:] + jnp.concatenate(
        [
            jnp.zeros((PLANE, CHAN), F32),
            late[:PLANE, :CHAN],
            late[PLANE : 3 * PLANE, :CHAN] + early,
        ],
        axis=0,
    )
    pre = total * SCALE
    sigma = jax.nn.sigmoid(pre)
    slope[s] = sigma * (1.0 + pre * (1.0 - sigma))

    @pl.when(s < last)
    def _():
        def store(b, moved):
            taps[s + 1, :, 1 : 1 + WIDTH, :, b * CHAN : (b + 1) * CHAN] = moved

        store_shifted(store, pre * sigma)


def shifted_delta(s, upstream, slope, back):
    delta = upstream[...] * slope[s]

    def store(b, moved):
        back[:, 1 : 1 + WIDTH, :, b * CHAN : (b + 1) * CHAN] = moved

    store_shifted(store, delta)


def weight_grad(s, taps, back, put):
    field = taps[s, :, 1 : 1 + WIDTH, :, CHAN : 2 * CHAN].reshape(CELLS, CHAN)
    turned = field.astype(F32).T.astype(BF16)
    for a in range(3):
        frames = 2 + a
        lhs = turned[:, : frames * PLANE]
        rhs = jnp.concatenate(
            [
                back[2 - a : 2 - a + frames, 2 - c : 2 - c + WIDTH].reshape(
                    frames * PLANE, 3 * CHAN
                )
                for c in range(3)
            ],
            axis=1,
        )
        out = dot(lhs, rhs) * GRAD_SCALE
        for c in range(3):
            for b in range(3):
                first = (c * 3 + 2 - b) * CHAN
                put((a * 3 + b) * 3 + c, out[:, first : first + CHAN])


def input_grad(s, w, back, upstream):
    field = back[...].reshape(FRAMES * (WIDTH + 2) * HEIGHT, 3 * CHAN)
    lhs = field_columns(field)
    flip = lambda b, c: (2 - b, 2 - c)
    late = dot_turned(lhs, tap_block(w, s, (1, 2), flip, 1))
    early = dot_turned(lhs[2 * PLANE :], tap_block(w, s, (0,), flip, 1))
    total = late[:, CHAN:] + jnp.concatenate(
        [
            late[PLANE : 2 * PLANE, :CHAN] + early[:PLANE],
            late[2 * PLANE : 3 * PLANE, :CHAN] + early[PLANE:],
            late[3 * PLANE :, :CHAN],
            jnp.zeros((PLANE, CHAN), F32),
        ],
        axis=0,
    )
    upstream[...] = total * SCALE


def crop(clip, offset_y, offset_x, taps):
    row = lax.broadcasted_iota(jnp.int32, (PLANE, clip.shape[-2]), 0)
    col = lax.broadcasted_iota(jnp.int32, (PLANE, clip.shape[-2]), 1)
    clip_w = 16
    want = (row % HEIGHT + offset_y) * clip_w + row // HEIGHT + offset_x
    pick = jnp.where(want == col, 1.0, 0.0).astype(BF16)
    field = jnp.concatenate([dot(pick, clip[t]) for t in range(FRAMES)], axis=0)

    def store(b, moved):
        taps[0, :, 1 : 1 + WIDTH, :, b * CHAN : (b + 1) * CHAN] = moved

    store_shifted(store, field)


def reorder(cotangent, upstream):
    row = lax.broadcasted_iota(jnp.int32, (PLANE, PLANE), 0)
    col = lax.broadcasted_iota(jnp.int32, (PLANE, PLANE), 1)
    pick = jnp.where(row % HEIGHT * WIDTH + row // HEIGHT == col, 1.0, 0.0).astype(BF16)
    for t in range(FRAMES):
        upstream[t * PLANE : (t + 1) * PLANE] = dot(pick, cotangent[t])


def clear_edges(taps, back):
    edge = jnp.zeros((FRAMES, HEIGHT, 3 * CHAN), BF16)

    def wipe(s, _):
        taps[s, :, 0] = edge
        taps[s, :, WIDTH + 1] = edge
        return 0

    lax.fori_loop(0, SECTIONS, wipe, 0)
    back[:, 0] = edge
    back[:, WIDTH + 1] = edge


MESH_ID = pl.DeviceIdType.MESH
HALF = ROWS // 2
PIECE = HALF // 4
SHARD = ROWS // 16


class Place:
    def __init__(self):
        segment = lax.axis_index("segment")
        replica = lax.axis_index("replica")
        self.z, self.hi = segment // 2, segment % 2
        self.lo, self.y, self.core = replica // 8, replica // 2 % 4, replica % 2

    def at(self, dz=0, hi=0, lo=0, dy=0, core=0):
        z = (self.z + dz) % 4
        y = (self.y + dy) % 4
        own = [(self.hi + hi) % 2, (self.lo + lo) % 2, (self.core + core) % 2]
        return (z * 2 + own[0], own[1] * 8 + y * 2 + own[2])

    def partners(self):
        away = [self.at(dz=k) for k in (1, 2, 3)]
        across = [self.at(dz=k, hi=1, lo=1) for k in range(4)]
        return away + across + [self.at(lo=1), self.at(hi=1)] + [self.at(dy=k) for k in (1, 2, 3)] + [self.at(core=1)]


def remote(src, dst, send, receive, device):
    return pltpu.make_async_remote_copy(
        src_ref=src,
        dst_ref=dst,
        send_sem=send,
        recv_sem=receive,
        device_id=device,
        device_id_type=MESH_ID,
    )


DIRECT, PAIR, RING, NEAR = range(4)
MODES = {
    (1, 0): DIRECT,
    (3, 0): DIRECT,
    (2, 0): NEAR,
    (0, 1): PAIR,
    (1, 1): RING,
    (3, 1): RING,
    (2, 1): NEAR,
}
ORDER = ((2, 0), (2, 1), (1, 0), (3, 0), (0, 1), (1, 1), (3, 1))


class Gather:
    def __init__(self, here, w, first_send, first_recv, relay_send, relay_recv, core_sem):
        self.here, self.w = here, w
        self.first_send, self.first_recv = first_send, first_recv
        self.relay_send, self.relay_recv = relay_send, relay_recv
        self.core_sem = core_sem
        self.own = here.z * 2 + here.hi

    def rows(self, s, core, start, count):
        first = core * HALF + start * PIECE
        return self.w.at[s, pl.ds(pl.multiple_of(first, PIECE), count * PIECE)]

    def mine(self, s, start, count):
        return self.rows(s, self.here.core, start, count)

    def first_parts(self, s, mode, lo):
        if mode == DIRECT:
            return [self.mine(s, 0, 4)]
        if mode == PAIR:
            return [self.mine(s, 2 * lo, 2)]
        if mode == RING:
            return [self.mine(s, self.here.y, 1)]
        return [self.mine(s, self.here.y, 1), self.mine(s, (self.here.y + 2) % 4, 1)]

    def firsts(self):
        sends = [[], []]
        for dz, dh in ORDER:
            lo = (self.here.lo + dh) % 2
            for n, part in enumerate(self.first_parts(self.own, MODES[dz, dh], lo)):
                sends[n].append((n, part, self.here.at(dz=dz, hi=dh, lo=dh)))
        for slot, (n, part, device) in enumerate(sends[0] + sends[1]):
            yield remote(
                part, part, self.first_send.at[slot], self.first_recv.at[self.own, n], device
            )

    def start(self):
        for copy in self.firsts():
            copy.start()

    def by_mode(self, s, act):
        dz = (self.here.z + 4 - s // 2) % 4
        dh = (self.here.hi + s) % 2
        for mode in range(4):
            hits = [key for key, value in MODES.items() if value == mode]
            if hits:
                cond = (dz == hits[0][0]) & (dh == hits[0][1])
                for key in hits[1:]:
                    cond = cond | ((dz == key[0]) & (dh == key[1]))

                @pl.when(cond)
                def _():
                    act(mode)

    def wait(self, part, receive):
        remote(part, part, self.first_send.at[0], receive, self.here.at()).wait_recv()

    def relays(self, s, mode):
        here = self.here
        if mode == PAIR:
            hops = [(here.at(lo=1), self.mine(s, 2 * here.lo, 2), self.mine(s, 2 - 2 * here.lo, 2))]
        elif mode == DIRECT:
            hops = []
        else:
            hops = [
                (here.at(dy=k), self.mine(s, here.y, 1), self.mine(s, (here.y + 4 - k) % 4, 1))
                for k in ((1, 3, 2) if mode == RING else (1, 3))
            ]
        for n, (device, part, back) in enumerate(hops):
            yield (
                remote(part, part, self.relay_send.at[s, n], self.relay_recv.at[s, n], device),
                back,
                self.relay_recv.at[s, n],
            )

    def relay(self, s):
        def act(mode):
            if mode != DIRECT:
                self.wait(self.first_parts(s, mode, self.here.lo)[0], self.first_recv.at[s, 0])
            for copy, _, _ in self.relays(s, mode):
                copy.start()

        self.by_mode(s, act)

    def core_copy(self, s):
        part = self.mine(s, 0, 4)
        return remote(
            part, part, self.core_sem.at[0, s], self.core_sem.at[1, s], self.here.at(core=1)
        )

    def swap(self, s):
        def act(mode):
            for n, part in enumerate(self.first_parts(s, mode, self.here.lo)):
                if n > 0 or mode == DIRECT:
                    self.wait(part, self.first_recv.at[s, n])
            for _, part, receive in self.relays(s, mode):
                self.wait(part, receive)

        self.by_mode(s, act)
        self.core_copy(s).start()

    def arrive(self, s):
        self.wait(self.rows(s, 1 - self.here.core, 0, 4), self.core_sem.at[1, s])

    def finish(self):
        for copy in self.firsts():
            copy.wait_send()

        def each(s, _):
            @pl.when(s != self.own)
            def _():
                def act(mode):
                    for copy, _, _ in self.relays(s, mode):
                        copy.wait_send()

                self.by_mode(s, act)
                self.core_copy(s).wait_send()

            return 0

        lax.fori_loop(0, SECTIONS, each, 0)


class Exchange:
    def __init__(self, here, total, give, taken, summed, ring, kept, crossed, sems):
        self.here = here
        self.total, self.give, self.taken, self.summed = total, give, taken, summed
        self.ring, self.kept, self.crossed = ring, kept, crossed
        self.core_sem, self.ring_send, self.ring_recv, self.cross_send, self.cross_recv = sems

    def shard(self, i, j, core):
        start = pl.multiple_of((2 * j + core) * SHARD, 8)
        return self.total[i, pl.ds(start, SHARD)]

    def core_copy(self, i):
        return remote(
            self.give.at[i],
            self.taken.at[i],
            self.core_sem.at[0, i],
            self.core_sem.at[1, i],
            self.here.at(core=1),
        )

    def to_core(self, i):
        for j in range(8):
            self.give[i, j] = self.shard(i, j, 1 - self.here.core).astype(BF16)
        self.core_copy(i).start()

    def ring_copy(self, i, k):
        return remote(
            self.summed.at[i, :, (self.here.y + k) % 4],
            self.ring.at[i, k - 1],
            self.ring_send.at[i, k - 1],
            self.ring_recv.at[i, k - 1],
            self.here.at(dy=k),
        )

    def to_ring(self, i):
        self.core_copy(i).wait_recv()
        for j in range(8):
            both = self.shard(i, j, self.here.core) + self.taken[i, j].astype(F32)
            self.summed[i, j // 4, j % 4] = both.astype(BF16)
        for k in (2, 1, 3):
            self.ring_copy(i, k).start()

    def cross_copy(self, i, slot):
        hi, lo = ((0, 1), (1, 0), (1, 1))[slot]
        return remote(
            self.kept.at[i, (self.here.lo + lo) % 2],
            self.crossed.at[slot],
            self.cross_send.at[slot],
            self.cross_recv.at[slot],
            self.here.at(hi=hi, lo=lo),
        )

    def to_cross(self, i):
        for k in (1, 3, 2):
            self.ring_copy(i, k).wait_recv()
        for lo in range(2):
            value = self.summed[i, lo, self.here.y].astype(F32)
            for k in range(3):
                value = value + self.ring[i, k, lo].astype(F32)
            self.kept[i, lo] = value.astype(BF16)

        @pl.when(self.here.hi == i)
        def _():
            self.cross_copy(i, 0).start()

        @pl.when(self.here.hi != i)
        def _():
            self.cross_copy(i, 1).start()
            self.cross_copy(i, 2).start()

    def finish(self, grads):
        for slot in range(3):
            self.cross_copy(0, slot).wait_recv()
        value = self.kept[self.here.hi, self.here.lo].astype(F32)
        for slot in range(3):
            value = value + self.crossed[slot].astype(F32)
        grads[...] = value
        for i in range(2):
            self.core_copy(i).wait_send()
            for k in (1, 2, 3):
                self.ring_copy(i, k).wait_send()
        for slot in range(3):
            self.cross_copy(0, slot).wait_send()


class Renewal:
    def __init__(self, here, fresh, ring_sem, pair_sem, core_sem):
        self.here, self.fresh = here, fresh
        self.ring_sem, self.pair_sem, self.core_sem = ring_sem, pair_sem, core_sem

    def compute(self, rows, moment, second, stale, new_moment, new_second):
        here = self.here
        first = beta_one * moment[...] + (1.0 - beta_one) * stale[...]
        square = beta_two * second[...] + (1.0 - beta_two) * stale[...] * stale[...]
        new_moment[...] = first
        new_second[...] = square
        step = learn_rate * first / (jnp.sqrt(square) + adam_eps)
        self.fresh[here.lo, here.y, here.core] = (rows[...].astype(F32) - step).astype(BF16)

    def ring_copy(self, k, back=0):
        part = self.fresh.at[self.here.lo, (self.here.y + back) % 4, self.here.core]
        return remote(
            part, part, self.ring_sem.at[0, k - 1], self.ring_sem.at[1, k - 1], self.here.at(dy=k)
        )

    def pair_copy(self, lo=0):
        part = self.fresh.at[(self.here.lo + lo) % 2, :, self.here.core]
        return remote(part, part, self.pair_sem.at[0], self.pair_sem.at[1], self.here.at(lo=1))

    def core_copy(self, core=0):
        part = self.fresh.at[:, :, (self.here.core + core) % 2]
        return remote(part, part, self.core_sem.at[0], self.core_sem.at[1], self.here.at(core=1))

    def to_ring(self):
        for k in (2, 1, 3):
            self.ring_copy(k).start()

    def to_pair(self):
        for k in (1, 3, 2):
            self.ring_copy(k, 4 - k).wait_recv()
        self.pair_copy().start()

    def to_core(self):
        self.pair_copy(1).wait_recv()
        self.core_copy().start()

    def arrive(self):
        self.core_copy(1).wait_recv()

    def finish(self):
        for k in (1, 2, 3):
            self.ring_copy(k).wait_send()
        self.pair_copy().wait_send()
        self.core_copy().wait_send()


def window_kernel(
    offsets,
    clips,
    weights,
    shards16,
    moment,
    second,
    stale,
    cotangent,
    grads,
    new_moment,
    new_second,
    new_weights,
    w,
    taps,
    back,
    slope,
    upstream,
    rows,
    fresh,
    total,
    give,
    taken,
    summed,
    ring,
    kept,
    crossed,
    load_sem,
    first_send,
    first_recv,
    relay_send,
    relay_recv,
    core_sem,
    sum_core,
    sum_ring_send,
    sum_ring_recv,
    cross_send,
    cross_recv,
    renew_ring,
    renew_pair,
    renew_core,
):
    here = Place()
    gather = Gather(here, w, first_send, first_recv, relay_send, relay_recv, core_sem)
    exchange = Exchange(
        here,
        total,
        give,
        taken,
        summed,
        ring,
        kept,
        crossed,
        (sum_core, sum_ring_send, sum_ring_recv, cross_send, cross_recv),
    )
    renewal = Renewal(here, fresh, renew_ring, renew_pair, renew_core)
    load = pltpu.make_async_copy(weights, w.at[gather.own], load_sem.at[0])
    load.start()
    own_rows = pltpu.make_async_copy(
        shards16.at[here.lo * 8 + here.y * 2 + here.core], rows, load_sem.at[1]
    )
    own_rows.start()
    barrier = pltpu.get_barrier_semaphore()
    partners = here.partners()
    for partner in partners:
        pl.semaphore_signal(barrier, inc=1, device_id=partner, device_id_type=MESH_ID)
    load.wait()
    pl.semaphore_wait(barrier, len(partners))
    gather.start()

    clear_edges(taps, back)
    crop(clips.at[here.hi], offsets[here.hi, 0], offsets[here.hi, 1], taps)
    reorder(cotangent.at[here.hi], upstream)
    own_rows.wait()
    renewal.compute(rows, moment, second, stale, new_moment, new_second)

    def passing(s, _):
        @pl.when(s != gather.own)
        def _():
            gather.relay(s)

        return 0

    lax.fori_loop(0, SECTIONS, passing, 0)
    renewal.to_ring()

    def forward(tick, _):
        @pl.when((tick < SECTIONS) & (tick != gather.own))
        def _():
            gather.swap(tick)

        s = tick - 1

        @pl.when(s >= 0)
        def _():
            @pl.when(s != gather.own)
            def _():
                gather.arrive(s)

            forward_section(s, w, taps, slope, SECTIONS - 1)

        return 0

    lax.fori_loop(0, SECTIONS + 1, forward, 0)
    renewal.to_pair()

    def backward(i, _):
        s = SECTIONS - 1 - i
        shifted_delta(s, upstream, slope, back)

        @pl.when(s == 2 * here.z)
        def _():
            exchange.to_ring(1)

        @pl.when(s // 2 == here.z)
        def _():
            def put(tap, block):
                total[s % 2, tap * CHAN : (tap + 1) * CHAN] = block

            weight_grad(s, taps, back, put)
            exchange.to_core(s % 2)

        @pl.when(s > 0)
        def _():
            input_grad(s, w, back, upstream)

        @pl.when(s == 1)
        def _():
            renewal.to_core()

        return 0

    lax.fori_loop(0, SECTIONS, backward, 0)
    renewal.arrive()
    store = pltpu.make_async_copy(fresh, new_weights, load_sem.at[0])
    store.start()
    exchange.to_ring(0)
    exchange.to_cross(1)
    exchange.to_cross(0)
    exchange.finish(grads)
    renewal.finish()
    gather.finish()
    store.wait()


def window(offsets, clips, weights, moment, second, stale, cotangent):
    vmem = pl.BlockSpec(memory_space=pltpu.VMEM)
    away = pl.BlockSpec(memory_space=pl.ANY)
    dma = pltpu.SemaphoreType.DMA
    shard = jax.ShapeDtypeStruct((SHARD, CHAN), F32)
    return pl.pallas_call(
        window_kernel,
        out_shape=(shard, shard, shard, jax.ShapeDtypeStruct((2, 4, 2, SHARD, CHAN), BF16)),
        in_specs=[
            pl.BlockSpec(memory_space=pltpu.SMEM),
            vmem,
            away,
            away,
            vmem,
            vmem,
            vmem,
            vmem,
        ],
        out_specs=(vmem, vmem, vmem, away),
        scratch_shapes=[
            pltpu.VMEM((SECTIONS, ROWS, CHAN), BF16),
            pltpu.VMEM((SECTIONS, FRAMES, WIDTH + 2, HEIGHT, 3 * CHAN), BF16),
            pltpu.VMEM((FRAMES, WIDTH + 2, HEIGHT, 3 * CHAN), BF16),
            pltpu.VMEM((SECTIONS, CELLS, CHAN), F32),
            pltpu.VMEM((CELLS, CHAN), F32),
            pltpu.VMEM((SHARD, CHAN), BF16),
            pltpu.VMEM((2, 4, 2, SHARD, CHAN), BF16),
            pltpu.VMEM((2, ROWS, CHAN), F32),
            pltpu.VMEM((2, 8, SHARD, CHAN), BF16),
            pltpu.VMEM((2, 8, SHARD, CHAN), BF16),
            pltpu.VMEM((2, 2, 4, SHARD, CHAN), BF16),
            pltpu.VMEM((2, 3, 2, SHARD, CHAN), BF16),
            pltpu.VMEM((2, 2, SHARD, CHAN), BF16),
            pltpu.VMEM((3, SHARD, CHAN), BF16),
            dma((2,)),
            dma((14,)),
            dma((SECTIONS, 2)),
            dma((SECTIONS, 3)),
            dma((SECTIONS, 3)),
            dma((2, SECTIONS)),
            dma((2, 2)),
            dma((2, 3)),
            dma((2, 3)),
            dma((3,)),
            dma((3,)),
            dma((2, 3)),
            dma((2,)),
            dma((2,)),
        ],
        compiler_params=pltpu.CompilerParams(
            vmem_limit_bytes=56 << 20, collective_id=0, has_side_effects=True
        ),
    )(
        offsets,
        clips,
        weights,
        weights.reshape(16, SHARD, CHAN),
        moment,
        second,
        stale,
        cotangent,
    )


def shards(clips, offsets, weights, moment, second, stale_grads, cotangent):
    micro = clips.shape[0]
    grads, first_new, second_new, fresh = window(
        offsets,
        clips.reshape(micro, FRAMES, -1, CHAN),
        weights[0],
        moment[0],
        second[0],
        stale_grads[0],
        cotangent.reshape(micro, FRAMES, PLANE, CHAN),
    )
    return (grads[None], first_new[None], second_new[None], fresh.reshape(1, ROWS, CHAN))


def solution(mesh):
    placed = (
        P("replica", None, None, None, None),
        P("replica", None),
        P("segment", None, None),
        P("segment", "replica", None),
        P("segment", "replica", None),
        P("segment", "replica", None),
        P("replica", None, None, None, None),
    )
    return jax.shard_map(
        shards,
        mesh=mesh,
        in_specs=placed,
        out_specs=(
            P("segment", "replica", None),
            P("segment", "replica", None),
            P("segment", "replica", None),
            P("segment", None, None),
        ),
        check_vma=False,
    )
```

```python
import math

import jax
import jax.numpy as jnp
from jax import lax
from jax.experimental import pallas as pl
from jax.experimental.pallas import tpu as pltpu
from jax.sharding import PartitionSpec as P

beta_one = 0.9
beta_two = 0.95
learn_rate = 0.05
adam_eps = 1e-08

F32 = jnp.float32
BF16 = jnp.bfloat16
FRAMES, HEIGHT, WIDTH, CHAN = 4, 16, 8, 128
PLANE = HEIGHT * WIDTH
CELLS = FRAMES * PLANE
SECTIONS = 8
TAPS = 27
ROWS = TAPS * CHAN
SCALE = 2.0 / math.sqrt(ROWS)
GRAD_SCALE = SCALE * 4.0 / math.sqrt(32 * CELLS)


def dot(a, b):
    return jnp.dot(a, b, preferred_element_type=F32)


def store_shifted(store, value):
    row = lax.broadcasted_iota(jnp.int32, (CELLS, CHAN), 0) % HEIGHT
    zero = jnp.zeros_like(value)
    for b in range(3):
        if b == 0:
            moved = jnp.where(row == 0, zero, pltpu.roll(value, 1, 0))
        elif b == 1:
            moved = value
        else:
            moved = jnp.where(row == HEIGHT - 1, zero, pltpu.roll(value, CELLS - 1, 0))
        store(b, moved.astype(BF16).reshape(FRAMES, WIDTH, HEIGHT, CHAN))


def tap_rows(w, s, tap):
    return w[s, tap * CHAN : (tap + 1) * CHAN]


def dot_turned(a, b):
    return lax.dot_general(a, b, (((1,), (1,)), ((), ())), preferred_element_type=F32)


def tap_block(w, s, times, turn, axis):
    columns = []
    for a in times:
        taps = [turn(b, c) for c in range(3) for b in range(3)]
        columns.append(
            jnp.concatenate([tap_rows(w, s, (a * 3 + b) * 3 + c) for b, c in taps], axis=axis)
        )
    return jnp.concatenate(columns, axis=1 - axis)


def field_columns(field):
    padded = field.reshape(FRAMES, WIDTH + 2, HEIGHT, 3 * CHAN)
    return jnp.concatenate(
        [padded[:, c : c + WIDTH].reshape(CELLS, 3 * CHAN) for c in range(3)], axis=1
    )


def forward_section(s, w, taps, slope, last):
    field = taps[s].reshape(FRAMES * (WIDTH + 2) * HEIGHT, 3 * CHAN)
    lhs = field_columns(field)
    late = dot(lhs, tap_block(w, s, (1, 2), lambda b, c: (b, c), 0))
    early = dot(lhs[: 2 * PLANE], tap_block(w, s, (0,), lambda b, c: (b, c), 0))
    total = late[:, CHAN:] + jnp.concatenate(
        [
            jnp.zeros((PLANE, CHAN), F32),
            late[:PLANE, :CHAN],
            late[PLANE : 3 * PLANE, :CHAN] + early,
        ],
        axis=0,
    )
    pre = total * SCALE
    sigma = jax.nn.sigmoid(pre)
    slope[s] = sigma * (1.0 + pre * (1.0 - sigma))

    @pl.when(s < last)
    def _():
        def store(b, moved):
            taps[s + 1, :, 1 : 1 + WIDTH, :, b * CHAN : (b + 1) * CHAN] = moved

        store_shifted(store, pre * sigma)


def shifted_delta(s, upstream, slope, back):
    delta = upstream[...] * slope[s]

    def store(b, moved):
        back[:, 1 : 1 + WIDTH, :, b * CHAN : (b + 1) * CHAN] = moved

    store_shifted(store, delta)


def weight_grad(s, taps, back, put):
    field = taps[s, :, 1 : 1 + WIDTH, :, CHAN : 2 * CHAN].reshape(CELLS, CHAN)
    turned = field.astype(F32).T.astype(BF16)
    for a in range(3):
        frames = 2 + a
        lhs = turned[:, : frames * PLANE]
        rhs = jnp.concatenate(
            [
                back[2 - a : 2 - a + frames, 2 - c : 2 - c + WIDTH].reshape(
                    frames * PLANE, 3 * CHAN
                )
                for c in range(3)
            ],
            axis=1,
        )
        out = dot(lhs, rhs) * GRAD_SCALE
        for c in range(3):
            for b in range(3):
                first = (c * 3 + 2 - b) * CHAN
                put((a * 3 + b) * 3 + c, out[:, first : first + CHAN])


def input_grad(s, w, back, upstream):
    field = back[...].reshape(FRAMES * (WIDTH + 2) * HEIGHT, 3 * CHAN)
    lhs = field_columns(field)
    flip = lambda b, c: (2 - b, 2 - c)
    late = dot_turned(lhs, tap_block(w, s, (1, 2), flip, 1))
    early = dot_turned(lhs[2 * PLANE :], tap_block(w, s, (0,), flip, 1))
    total = late[:, CHAN:] + jnp.concatenate(
        [
            late[PLANE : 2 * PLANE, :CHAN] + early[:PLANE],
            late[2 * PLANE : 3 * PLANE, :CHAN] + early[PLANE:],
            late[3 * PLANE :, :CHAN],
            jnp.zeros((PLANE, CHAN), F32),
        ],
        axis=0,
    )
    upstream[...] = total * SCALE


def crop(clip, offset_y, offset_x, taps):
    row = lax.broadcasted_iota(jnp.int32, (PLANE, clip.shape[-2]), 0)
    col = lax.broadcasted_iota(jnp.int32, (PLANE, clip.shape[-2]), 1)
    clip_w = 16
    want = (row % HEIGHT + offset_y) * clip_w + row // HEIGHT + offset_x
    pick = jnp.where(want == col, 1.0, 0.0).astype(BF16)
    field = jnp.concatenate([dot(pick, clip[t]) for t in range(FRAMES)], axis=0)

    def store(b, moved):
        taps[0, :, 1 : 1 + WIDTH, :, b * CHAN : (b + 1) * CHAN] = moved

    store_shifted(store, field)


def reorder(cotangent, upstream):
    row = lax.broadcasted_iota(jnp.int32, (PLANE, PLANE), 0)
    col = lax.broadcasted_iota(jnp.int32, (PLANE, PLANE), 1)
    pick = jnp.where(row % HEIGHT * WIDTH + row // HEIGHT == col, 1.0, 0.0).astype(BF16)
    for t in range(FRAMES):
        upstream[t * PLANE : (t + 1) * PLANE] = dot(pick, cotangent[t])


def clear_edges(taps, back):
    edge = jnp.zeros((FRAMES, HEIGHT, 3 * CHAN), BF16)

    def wipe(s, _):
        taps[s, :, 0] = edge
        taps[s, :, WIDTH + 1] = edge
        return 0

    lax.fori_loop(0, SECTIONS, wipe, 0)
    back[:, 0] = edge
    back[:, WIDTH + 1] = edge


MESH_ID = pl.DeviceIdType.MESH
HALF = ROWS // 2
PIECE = HALF // 4
SHARD = ROWS // 16


class Place:
    def __init__(self):
        segment = lax.axis_index("segment")
        replica = lax.axis_index("replica")
        self.z, self.hi = segment // 2, segment % 2
        self.lo, self.y, self.core = replica // 8, replica // 2 % 4, replica % 2

    def at(self, dz=0, hi=0, lo=0, dy=0, core=0):
        z = (self.z + dz) % 4
        y = (self.y + dy) % 4
        own = [(self.hi + hi) % 2, (self.lo + lo) % 2, (self.core + core) % 2]
        return (z * 2 + own[0], own[1] * 8 + y * 2 + own[2])

    def partners(self):
        away = [self.at(dz=k) for k in (1, 2, 3)]
        across = [self.at(dz=k, hi=1, lo=1) for k in range(4)]
        return away + across + [self.at(lo=1), self.at(hi=1)] + [self.at(dy=k) for k in (1, 2, 3)] + [self.at(core=1)]


def remote(src, dst, send, receive, device):
    return pltpu.make_async_remote_copy(
        src_ref=src,
        dst_ref=dst,
        send_sem=send,
        recv_sem=receive,
        device_id=device,
        device_id_type=MESH_ID,
    )


DIRECT, PAIR, RING, NEAR = range(4)
MODES = {
    (1, 0): DIRECT,
    (3, 0): DIRECT,
    (2, 0): NEAR,
    (0, 1): PAIR,
    (1, 1): RING,
    (3, 1): RING,
    (2, 1): NEAR,
}
ORDER = ((2, 0), (2, 1), (1, 0), (3, 0), (0, 1), (1, 1), (3, 1))


class Gather:
    def __init__(self, here, w, first_send, first_recv, relay_send, relay_recv, core_sem):
        self.here, self.w = here, w
        self.first_send, self.first_recv = first_send, first_recv
        self.relay_send, self.relay_recv = relay_send, relay_recv
        self.core_sem = core_sem
        self.own = here.z * 2 + here.hi

    def rows(self, s, core, start, count):
        first = core * HALF + start * PIECE
        return self.w.at[s, pl.ds(pl.multiple_of(first, PIECE), count * PIECE)]

    def mine(self, s, start, count):
        return self.rows(s, self.here.core, start, count)

    def first_parts(self, s, mode, lo):
        if mode == DIRECT:
            return [self.mine(s, 0, 4)]
        if mode == PAIR:
            return [self.mine(s, 2 * lo, 2)]
        if mode == RING:
            return [self.mine(s, self.here.y, 1)]
        return [self.mine(s, self.here.y, 1), self.mine(s, (self.here.y + 2) % 4, 1)]

    def firsts(self):
        sends = [[], []]
        for dz, dh in ORDER:
            lo = (self.here.lo + dh) % 2
            for n, part in enumerate(self.first_parts(self.own, MODES[dz, dh], lo)):
                sends[n].append((n, part, self.here.at(dz=dz, hi=dh, lo=dh)))
        for slot, (n, part, device) in enumerate(sends[0] + sends[1]):
            yield remote(
                part, part, self.first_send.at[slot], self.first_recv.at[self.own, n], device
            )

    def start(self):
        for copy in self.firsts():
            copy.start()

    def by_mode(self, s, act):
        dz = (self.here.z + 4 - s // 2) % 4
        dh = (self.here.hi + s) % 2
        for mode in range(4):
            hits = [key for key, value in MODES.items() if value == mode]
            if hits:
                cond = (dz == hits[0][0]) & (dh == hits[0][1])
                for key in hits[1:]:
                    cond = cond | ((dz == key[0]) & (dh == key[1]))

                @pl.when(cond)
                def _():
                    act(mode)

    def wait(self, part, receive):
        remote(part, part, self.first_send.at[0], receive, self.here.at()).wait_recv()

    def relays(self, s, mode):
        here = self.here
        if mode == PAIR:
            hops = [(here.at(lo=1), self.mine(s, 2 * here.lo, 2), self.mine(s, 2 - 2 * here.lo, 2))]
        elif mode == DIRECT:
            hops = []
        else:
            hops = [
                (here.at(dy=k), self.mine(s, here.y, 1), self.mine(s, (here.y + 4 - k) % 4, 1))
                for k in ((1, 3, 2) if mode == RING else (1, 3))
            ]
        for n, (device, part, back) in enumerate(hops):
            yield (
                remote(part, part, self.relay_send.at[s, n], self.relay_recv.at[s, n], device),
                back,
                self.relay_recv.at[s, n],
            )

    def relay(self, s):
        def act(mode):
            if mode != DIRECT:
                self.wait(self.first_parts(s, mode, self.here.lo)[0], self.first_recv.at[s, 0])
            for copy, _, _ in self.relays(s, mode):
                copy.start()

        self.by_mode(s, act)

    def core_copy(self, s):
        part = self.mine(s, 0, 4)
        return remote(
            part, part, self.core_sem.at[0, s], self.core_sem.at[1, s], self.here.at(core=1)
        )

    def swap(self, s):
        def act(mode):
            for n, part in enumerate(self.first_parts(s, mode, self.here.lo)):
                if n > 0 or mode == DIRECT:
                    self.wait(part, self.first_recv.at[s, n])
            for _, part, receive in self.relays(s, mode):
                self.wait(part, receive)

        self.by_mode(s, act)
        self.core_copy(s).start()

    def arrive(self, s):
        self.wait(self.rows(s, 1 - self.here.core, 0, 4), self.core_sem.at[1, s])

    def finish(self):
        for copy in self.firsts():
            copy.wait_send()

        def each(s, _):
            @pl.when(s != self.own)
            def _():
                def act(mode):
                    for copy, _, _ in self.relays(s, mode):
                        copy.wait_send()

                self.by_mode(s, act)
                self.core_copy(s).wait_send()

            return 0

        lax.fori_loop(0, SECTIONS, each, 0)


class Exchange:
    def __init__(self, here, total, give, taken, summed, ring, kept, crossed, sems):
        self.here = here
        self.total, self.give, self.taken, self.summed = total, give, taken, summed
        self.ring, self.kept, self.crossed = ring, kept, crossed
        self.core_sem, self.ring_send, self.ring_recv, self.cross_send, self.cross_recv = sems

    def shard(self, i, j, core):
        start = pl.multiple_of((2 * j + core) * SHARD, 8)
        return self.total[i, pl.ds(start, SHARD)]

    def core_copy(self, i):
        return remote(
            self.give.at[i],
            self.taken.at[i],
            self.core_sem.at[0, i],
            self.core_sem.at[1, i],
            self.here.at(core=1),
        )

    def to_core(self, i):
        for j in range(8):
            self.give[i, j] = self.shard(i, j, 1 - self.here.core).astype(BF16)
        self.core_copy(i).start()

    def ring_copy(self, i, k):
        return remote(
            self.summed.at[i, :, (self.here.y + k) % 4],
            self.ring.at[i, k - 1],
            self.ring_send.at[i, k - 1],
            self.ring_recv.at[i, k - 1],
            self.here.at(dy=k),
        )

    def to_ring(self, i):
        self.core_copy(i).wait_recv()
        for j in range(8):
            both = self.shard(i, j, self.here.core) + self.taken[i, j].astype(F32)
            self.summed[i, j // 4, j % 4] = both.astype(BF16)
        for k in (2, 1, 3):
            self.ring_copy(i, k).start()

    def cross_copy(self, i, slot):
        hi, lo = ((0, 1), (1, 0), (1, 1))[slot]
        return remote(
            self.kept.at[i, (self.here.lo + lo) % 2],
            self.crossed.at[slot],
            self.cross_send.at[slot],
            self.cross_recv.at[slot],
            self.here.at(hi=hi, lo=lo),
        )

    def to_cross(self, i):
        for k in (1, 3, 2):
            self.ring_copy(i, k).wait_recv()
        for lo in range(2):
            value = self.summed[i, lo, self.here.y].astype(F32)
            for k in range(3):
                value = value + self.ring[i, k, lo].astype(F32)
            self.kept[i, lo] = value.astype(BF16)

        @pl.when(self.here.hi == i)
        def _():
            self.cross_copy(i, 0).start()

        @pl.when(self.here.hi != i)
        def _():
            self.cross_copy(i, 1).start()
            self.cross_copy(i, 2).start()

    def finish(self, grads):
        for slot in range(3):
            self.cross_copy(0, slot).wait_recv()
        value = self.kept[self.here.hi, self.here.lo].astype(F32)
        for slot in range(3):
            value = value + self.crossed[slot].astype(F32)
        grads[...] = value
        for i in range(2):
            self.core_copy(i).wait_send()
            for k in (1, 2, 3):
                self.ring_copy(i, k).wait_send()
        for slot in range(3):
            self.cross_copy(0, slot).wait_send()


def moments(moment, second, stale):
    first = beta_one * moment + (1.0 - beta_one) * stale
    square = beta_two * second + (1.0 - beta_two) * stale * stale
    return first, square


class Renewal:
    def __init__(self, here, fresh, ring_sem, pair_sem, core_sem):
        self.here, self.fresh = here, fresh
        self.ring_sem, self.pair_sem, self.core_sem = ring_sem, pair_sem, core_sem

    def compute(self, rows, moment, second, stale):
        here = self.here
        first, square = moments(moment[...], second[...], stale[...])
        step = learn_rate * first / (jnp.sqrt(square) + adam_eps)
        self.fresh[here.lo, here.y, here.core] = (rows[...].astype(F32) - step).astype(BF16)

    def ring_copy(self, k, back=0):
        part = self.fresh.at[self.here.lo, (self.here.y + back) % 4, self.here.core]
        return remote(
            part, part, self.ring_sem.at[0, k - 1], self.ring_sem.at[1, k - 1], self.here.at(dy=k)
        )

    def pair_copy(self, lo=0):
        part = self.fresh.at[(self.here.lo + lo) % 2, :, self.here.core]
        return remote(part, part, self.pair_sem.at[0], self.pair_sem.at[1], self.here.at(lo=1))

    def core_copy(self, core=0):
        part = self.fresh.at[:, :, (self.here.core + core) % 2]
        return remote(part, part, self.core_sem.at[0], self.core_sem.at[1], self.here.at(core=1))

    def to_ring(self):
        for k in (2, 1, 3):
            self.ring_copy(k).start()

    def to_pair(self):
        for k in (1, 3, 2):
            self.ring_copy(k, 4 - k).wait_recv()
        self.pair_copy().start()

    def to_core(self):
        self.pair_copy(1).wait_recv()
        self.core_copy().start()

    def arrive(self):
        self.core_copy(1).wait_recv()

    def finish(self):
        for k in (1, 2, 3):
            self.ring_copy(k).wait_send()
        self.pair_copy().wait_send()
        self.core_copy().wait_send()


def window_kernel(
    offsets,
    clips,
    weights,
    shards16,
    moment,
    second,
    stale,
    cotangent,
    grads,
    new_weights,
    w,
    taps,
    back,
    slope,
    upstream,
    rows,
    clip,
    given,
    old,
    fresh,
    total,
    give,
    taken,
    summed,
    ring,
    kept,
    crossed,
    load_sem,
    first_send,
    first_recv,
    relay_send,
    relay_recv,
    core_sem,
    sum_core,
    sum_ring_send,
    sum_ring_recv,
    cross_send,
    cross_recv,
    renew_ring,
    renew_pair,
    renew_core,
):
    here = Place()
    gather = Gather(here, w, first_send, first_recv, relay_send, relay_recv, core_sem)
    exchange = Exchange(
        here,
        total,
        give,
        taken,
        summed,
        ring,
        kept,
        crossed,
        (sum_core, sum_ring_send, sum_ring_recv, cross_send, cross_recv),
    )
    renewal = Renewal(here, fresh, renew_ring, renew_pair, renew_core)
    load = pltpu.make_async_copy(weights, w.at[gather.own], load_sem.at[0])
    load.start()
    loads = [
        pltpu.make_async_copy(source, place, load_sem.at[n + 1])
        for n, (source, place) in enumerate(
            (
                (clips.at[here.hi], clip),
                (cotangent.at[here.hi], given),
                (shards16.at[here.lo * 8 + here.y * 2 + here.core], rows),
                (moment, old.at[0]),
                (second, old.at[1]),
                (stale, old.at[2]),
            )
        )
    ]
    barrier = pltpu.get_barrier_semaphore()
    partners = here.partners()
    for partner in partners:
        pl.semaphore_signal(barrier, inc=1, device_id=partner, device_id_type=MESH_ID)
    for other in loads:
        other.start()
    load.wait()
    pl.semaphore_wait(barrier, len(partners))
    gather.start()

    clear_edges(taps, back)
    for other in loads:
        other.wait()
    crop(clip, offsets[here.hi, 0], offsets[here.hi, 1], taps)
    reorder(given, upstream)
    renewal.compute(rows, old.at[0], old.at[1], old.at[2])

    def passing(s, _):
        @pl.when(s != gather.own)
        def _():
            gather.relay(s)

        return 0

    lax.fori_loop(0, SECTIONS, passing, 0)
    renewal.to_ring()

    def forward(tick, _):
        @pl.when((tick < SECTIONS) & (tick != gather.own))
        def _():
            gather.swap(tick)

        s = tick - 1

        @pl.when(s >= 0)
        def _():
            @pl.when(s != gather.own)
            def _():
                gather.arrive(s)

            forward_section(s, w, taps, slope, SECTIONS - 1)

        return 0

    lax.fori_loop(0, SECTIONS + 1, forward, 0)
    renewal.to_pair()

    def backward(i, _):
        s = SECTIONS - 1 - i
        shifted_delta(s, upstream, slope, back)

        @pl.when(s == 2 * here.z)
        def _():
            exchange.to_ring(1)

        @pl.when(s // 2 == here.z)
        def _():
            def put(tap, block):
                total[s % 2, tap * CHAN : (tap + 1) * CHAN] = block

            weight_grad(s, taps, back, put)
            exchange.to_core(s % 2)

        @pl.when(s > 0)
        def _():
            input_grad(s, w, back, upstream)

        @pl.when(s == 1)
        def _():
            renewal.to_core()

        return 0

    lax.fori_loop(0, SECTIONS, backward, 0)
    renewal.arrive()
    store = pltpu.make_async_copy(fresh, new_weights, load_sem.at[0])
    store.start()
    exchange.to_ring(0)
    exchange.to_cross(1)
    exchange.to_cross(0)
    exchange.finish(grads)
    renewal.finish()
    gather.finish()
    store.wait()


def window(offsets, clips, weights, moment, second, stale, cotangent):
    vmem = pl.BlockSpec(memory_space=pltpu.VMEM)
    away = pl.BlockSpec(memory_space=pl.ANY)
    dma = pltpu.SemaphoreType.DMA
    shard = jax.ShapeDtypeStruct((SHARD, CHAN), F32)
    return pl.pallas_call(
        window_kernel,
        out_shape=(shard, jax.ShapeDtypeStruct((2, 4, 2, SHARD, CHAN), BF16)),
        in_specs=[pl.BlockSpec(memory_space=pltpu.SMEM)] + [away] * 7,
        out_specs=(vmem, away),
        scratch_shapes=[
            pltpu.VMEM((SECTIONS, ROWS, CHAN), BF16),
            pltpu.VMEM((SECTIONS, FRAMES, WIDTH + 2, HEIGHT, 3 * CHAN), BF16),
            pltpu.VMEM((FRAMES, WIDTH + 2, HEIGHT, 3 * CHAN), BF16),
            pltpu.VMEM((SECTIONS, CELLS, CHAN), F32),
            pltpu.VMEM((CELLS, CHAN), F32),
            pltpu.VMEM((SHARD, CHAN), BF16),
            pltpu.VMEM(clips.shape[1:], BF16),
            pltpu.VMEM(cotangent.shape[1:], BF16),
            pltpu.VMEM((3, SHARD, CHAN), F32),
            pltpu.VMEM((2, 4, 2, SHARD, CHAN), BF16),
            pltpu.VMEM((2, ROWS, CHAN), F32),
            pltpu.VMEM((2, 8, SHARD, CHAN), BF16),
            pltpu.VMEM((2, 8, SHARD, CHAN), BF16),
            pltpu.VMEM((2, 2, 4, SHARD, CHAN), BF16),
            pltpu.VMEM((2, 3, 2, SHARD, CHAN), BF16),
            pltpu.VMEM((2, 2, SHARD, CHAN), BF16),
            pltpu.VMEM((3, SHARD, CHAN), BF16),
            dma((7,)),
            dma((14,)),
            dma((SECTIONS, 2)),
            dma((SECTIONS, 3)),
            dma((SECTIONS, 3)),
            dma((2, SECTIONS)),
            dma((2, 2)),
            dma((2, 3)),
            dma((2, 3)),
            dma((3,)),
            dma((3,)),
            dma((2, 3)),
            dma((2,)),
            dma((2,)),
        ],
        compiler_params=pltpu.CompilerParams(
            vmem_limit_bytes=56 << 20, collective_id=0, has_side_effects=True
        ),
    )(
        offsets,
        clips,
        weights,
        weights.reshape(16, SHARD, CHAN),
        moment,
        second,
        stale,
        cotangent,
    )


def finish_kernel(
    summed, moment, second, stale, gathered, grads, new_moment, new_second, new_weights, *scratch
):
    own, m, v, g, room, load_sem, store_sem = scratch
    places = (room, own, g, m, v)
    loads = [
        pltpu.make_async_copy(source, place, load_sem.at[n])
        for n, (source, place) in enumerate(
            zip((gathered, summed, stale, moment, second), places)
        )
    ]
    stores = [
        pltpu.make_async_copy(place, target, store_sem.at[n])
        for n, (place, target) in enumerate(
            zip((room, own, m, v), (new_weights, grads, new_moment, new_second))
        )
    ]
    for load in loads:
        load.start()
    for n in range(2):
        loads[n].wait()
        stores[n].start()
    for load in loads[2:]:
        load.wait()
    first, square = moments(m[...], v[...], g[...])
    m[...] = first
    v[...] = square
    for store in stores[2:]:
        store.start()
    for store in stores:
        store.wait()


def finish(summed, moment, second, stale, gathered):
    away = pl.BlockSpec(memory_space=pl.ANY)
    shard = jax.ShapeDtypeStruct((SHARD, CHAN), F32)
    return pl.pallas_call(
        finish_kernel,
        out_shape=(shard, shard, shard, jax.ShapeDtypeStruct(gathered.shape, BF16)),
        in_specs=[away] * 5,
        out_specs=(away,) * 4,
        scratch_shapes=[pltpu.VMEM((SHARD, CHAN), F32)] * 4
        + [
            pltpu.VMEM(gathered.shape, BF16),
            pltpu.SemaphoreType.DMA((5,)),
            pltpu.SemaphoreType.DMA((4,)),
        ],
        compiler_params=pltpu.CompilerParams(vmem_limit_bytes=56 << 20),
    )(summed, moment, second, stale, gathered)


def shards(clips, offsets, weights, moment, second, stale_grads, cotangent):
    micro = clips.shape[0]
    summed, fresh = window(
        offsets,
        clips.reshape(micro, FRAMES, -1, CHAN),
        weights[0],
        moment[0],
        second[0],
        stale_grads[0],
        cotangent.reshape(micro, FRAMES, PLANE, CHAN),
    )
    grads, first_new, second_new, fresh = finish(
        summed, moment[0], second[0], stale_grads[0], fresh
    )
    return (grads[None], first_new[None], second_new[None], fresh.reshape(1, ROWS, CHAN))


def solution(mesh):
    placed = (
        P("replica", None, None, None, None),
        P("replica", None),
        P("segment", None, None),
        P("segment", "replica", None),
        P("segment", "replica", None),
        P("segment", "replica", None),
        P("replica", None, None, None, None),
    )
    return jax.shard_map(
        shards,
        mesh=mesh,
        in_specs=placed,
        out_specs=(
            P("segment", "replica", None),
            P("segment", "replica", None),
            P("segment", "replica", None),
            P("segment", None, None),
        ),
        check_vma=False,
    )
```

```python
import math

import jax
import jax.numpy as jnp
from jax import lax
from jax.experimental import pallas as pl
from jax.experimental.pallas import tpu as pltpu
from jax.sharding import PartitionSpec as P

beta_one = 0.9
beta_two = 0.95
learn_rate = 0.05
adam_eps = 1e-08

F32 = jnp.float32
BF16 = jnp.bfloat16
FRAMES, HEIGHT, WIDTH, CHAN = 4, 16, 8, 128
PLANE = HEIGHT * WIDTH
CELLS = FRAMES * PLANE
SECTIONS = 8
TAPS = 27
ROWS = TAPS * CHAN
SCALE = 2.0 / math.sqrt(ROWS)
GRAD_SCALE = SCALE * 4.0 / math.sqrt(32 * CELLS)


def dot(a, b):
    return jnp.dot(a, b, preferred_element_type=F32)


def store_shifted(store, value):
    row = lax.broadcasted_iota(jnp.int32, (CELLS, CHAN), 0) % HEIGHT
    zero = jnp.zeros_like(value)
    for b in range(3):
        if b == 0:
            moved = jnp.where(row == 0, zero, pltpu.roll(value, 1, 0))
        elif b == 1:
            moved = value
        else:
            moved = jnp.where(row == HEIGHT - 1, zero, pltpu.roll(value, CELLS - 1, 0))
        store(b, moved.astype(BF16).reshape(FRAMES, WIDTH, HEIGHT, CHAN))


def tap_rows(w, s, tap):
    return w[s, tap * CHAN : (tap + 1) * CHAN]


def dot_turned(a, b):
    return lax.dot_general(a, b, (((1,), (1,)), ((), ())), preferred_element_type=F32)


def tap_block(w, s, times, turn, axis):
    columns = []
    for a in times:
        taps = [turn(b, c) for c in range(3) for b in range(3)]
        columns.append(
            jnp.concatenate([tap_rows(w, s, (a * 3 + b) * 3 + c) for b, c in taps], axis=axis)
        )
    return jnp.concatenate(columns, axis=1 - axis)


def field_columns(field):
    padded = field.reshape(FRAMES, WIDTH + 2, HEIGHT, 3 * CHAN)
    return jnp.concatenate(
        [padded[:, c : c + WIDTH].reshape(CELLS, 3 * CHAN) for c in range(3)], axis=1
    )


def forward_section(s, w, taps, slope, last):
    field = taps[s].reshape(FRAMES * (WIDTH + 2) * HEIGHT, 3 * CHAN)
    lhs = field_columns(field)
    late = dot(lhs, tap_block(w, s, (1, 2), lambda b, c: (b, c), 0))
    early = dot(lhs[: 2 * PLANE], tap_block(w, s, (0,), lambda b, c: (b, c), 0))
    total = late[:, CHAN:] + jnp.concatenate(
        [
            jnp.zeros((PLANE, CHAN), F32),
            late[:PLANE, :CHAN],
            late[PLANE : 3 * PLANE, :CHAN] + early,
        ],
        axis=0,
    )
    pre = total * SCALE
    sigma = jax.nn.sigmoid(pre)
    slope[s] = sigma * (1.0 + pre * (1.0 - sigma))

    @pl.when(s < last)
    def _():
        def store(b, moved):
            taps[s + 1, :, 1 : 1 + WIDTH, :, b * CHAN : (b + 1) * CHAN] = moved

        store_shifted(store, pre * sigma)


def shifted_delta(s, upstream, slope, back):
    delta = upstream[...] * slope[s]

    def store(b, moved):
        back[:, 1 : 1 + WIDTH, :, b * CHAN : (b + 1) * CHAN] = moved

    store_shifted(store, delta)


def weight_grad(s, taps, back, put, done):
    field = taps[s, :, 1 : 1 + WIDTH, :, CHAN : 2 * CHAN].reshape(CELLS, CHAN)
    turned = field.astype(F32).T.astype(BF16)
    for a in range(3):
        frames = 2 + a
        lhs = turned[:, : frames * PLANE]
        rhs = jnp.concatenate(
            [
                back[2 - a : 2 - a + frames, 2 - c : 2 - c + WIDTH].reshape(
                    frames * PLANE, 3 * CHAN
                )
                for c in range(3)
            ],
            axis=1,
        )
        out = dot(lhs, rhs) * GRAD_SCALE
        for c in range(3):
            for b in range(3):
                first = (c * 3 + 2 - b) * CHAN
                put((a * 3 + b) * 3 + c, out[:, first : first + CHAN])
        if a > 0:
            done(a - 1)


def input_grad(s, w, back, upstream):
    field = back[...].reshape(FRAMES * (WIDTH + 2) * HEIGHT, 3 * CHAN)
    lhs = field_columns(field)
    flip = lambda b, c: (2 - b, 2 - c)
    late = dot_turned(lhs, tap_block(w, s, (1, 2), flip, 1))
    early = dot_turned(lhs[2 * PLANE :], tap_block(w, s, (0,), flip, 1))
    total = late[:, CHAN:] + jnp.concatenate(
        [
            late[PLANE : 2 * PLANE, :CHAN] + early[:PLANE],
            late[2 * PLANE : 3 * PLANE, :CHAN] + early[PLANE:],
            late[3 * PLANE :, :CHAN],
            jnp.zeros((PLANE, CHAN), F32),
        ],
        axis=0,
    )
    upstream[...] = total * SCALE


def crop(clip, offset_y, offset_x, taps):
    row = lax.broadcasted_iota(jnp.int32, (PLANE, clip.shape[-2]), 0)
    col = lax.broadcasted_iota(jnp.int32, (PLANE, clip.shape[-2]), 1)
    clip_w = 16
    want = (row % HEIGHT + offset_y) * clip_w + row // HEIGHT + offset_x
    pick = jnp.where(want == col, 1.0, 0.0).astype(BF16)
    field = jnp.concatenate([dot(pick, clip[t]) for t in range(FRAMES)], axis=0)

    def store(b, moved):
        taps[0, :, 1 : 1 + WIDTH, :, b * CHAN : (b + 1) * CHAN] = moved

    store_shifted(store, field)


def reorder(cotangent, upstream):
    row = lax.broadcasted_iota(jnp.int32, (PLANE, PLANE), 0)
    col = lax.broadcasted_iota(jnp.int32, (PLANE, PLANE), 1)
    pick = jnp.where(row % HEIGHT * WIDTH + row // HEIGHT == col, 1.0, 0.0).astype(BF16)
    for t in range(FRAMES):
        upstream[t * PLANE : (t + 1) * PLANE] = dot(pick, cotangent[t])


def clear_edges(taps, back):
    edge = jnp.zeros((FRAMES, HEIGHT, 3 * CHAN), BF16)

    def wipe(s, _):
        taps[s, :, 0] = edge
        taps[s, :, WIDTH + 1] = edge
        return 0

    lax.fori_loop(0, SECTIONS, wipe, 0)
    back[:, 0] = edge
    back[:, WIDTH + 1] = edge


MESH_ID = pl.DeviceIdType.MESH
HALF = ROWS // 2
PIECE = HALF // 4
SHARD = ROWS // 16


class Place:
    def __init__(self):
        segment = lax.axis_index("segment")
        replica = lax.axis_index("replica")
        self.z, self.hi = segment // 2, segment % 2
        self.lo, self.y, self.core = replica // 8, replica // 2 % 4, replica % 2

    def at(self, dz=0, hi=0, lo=0, dy=0, core=0):
        z = (self.z + dz) % 4
        y = (self.y + dy) % 4
        own = [(self.hi + hi) % 2, (self.lo + lo) % 2, (self.core + core) % 2]
        return (z * 2 + own[0], own[1] * 8 + y * 2 + own[2])

    def partners(self):
        away = [self.at(dz=k) for k in (1, 2, 3)]
        across = [self.at(dz=k, hi=1, lo=1) for k in range(4)]
        return away + across + [self.at(lo=1), self.at(hi=1)] + [self.at(dy=k) for k in (1, 2, 3)] + [self.at(core=1)]


def remote(src, dst, send, receive, device):
    return pltpu.make_async_remote_copy(
        src_ref=src,
        dst_ref=dst,
        send_sem=send,
        recv_sem=receive,
        device_id=device,
        device_id_type=MESH_ID,
    )


DIRECT, PAIR, RING, NEAR = range(4)
MODES = {(1, 0): DIRECT, (3, 0): DIRECT, (2, 0): NEAR, (0, 1): PAIR, (1, 1): RING, (3, 1): RING, (2, 1): RING}
ORDER = ((2, 0), (2, 1), (1, 0), (3, 0), (0, 1), (1, 1), (3, 1))
RELAYS = ((0, 1), (1, 1), (3, 1), (2, 1), (2, 0), (1, 0), (3, 0))


class Gather:
    def __init__(self, here, w, first_send, first_recv, relay_send, relay_recv, core_sem):
        self.here, self.w = here, w
        self.first_send, self.first_recv = first_send, first_recv
        self.relay_send, self.relay_recv = relay_send, relay_recv
        self.core_sem = core_sem
        self.own = here.z * 2 + here.hi

    def rows(self, s, core, start, count):
        first = core * HALF + start * PIECE
        return self.w.at[s, pl.ds(pl.multiple_of(first, PIECE), count * PIECE)]

    def mine(self, s, start, count):
        return self.rows(s, self.here.core, start, count)

    def first_parts(self, s, mode, lo):
        if mode == DIRECT:
            return [self.mine(s, 0, 4)]
        if mode == PAIR:
            return [self.mine(s, 2 * lo, 2)]
        if mode == RING:
            return [self.mine(s, self.here.y, 1)]
        return [self.mine(s, self.here.y, 1), self.mine(s, (self.here.y + 2) % 4, 1)]

    def firsts(self, dz, dh):
        lo = (self.here.lo + dh) % 2
        slot = 2 * ORDER.index((dz, dh))
        for n, part in enumerate(self.first_parts(self.own, MODES[dz, dh], lo)):
            yield remote(
                part,
                part,
                self.first_send.at[slot + n],
                self.first_recv.at[self.own, n],
                self.here.at(dz=dz, hi=dh, lo=dh),
            )

    def start(self):
        for z in range(4):

            @pl.when(self.here.z == z)
            def _():
                for target, dh in ((0, 1), (2, 1), (1, 1), (3, 1), (0, 0), (2, 0), (1, 0), (3, 0)):
                    dz = (target - z) % 4
                    if (dz, dh) != (0, 0):
                        for copy in self.firsts(dz, dh):
                            copy.start()

    def by_mode(self, s, act):
        dz = (self.here.z + 4 - s // 2) % 4
        dh = (self.here.hi + s) % 2
        for mode in range(4):
            hits = [key for key, value in MODES.items() if value == mode]
            if hits:
                cond = (dz == hits[0][0]) & (dh == hits[0][1])
                for key in hits[1:]:
                    cond = cond | ((dz == key[0]) & (dh == key[1]))

                @pl.when(cond)
                def _():
                    act(mode)

    def wait(self, part, receive):
        remote(part, part, self.first_send.at[0], receive, self.here.at()).wait_recv()

    def relays(self, s, mode):
        here = self.here
        if mode == PAIR:
            hops = [(here.at(lo=1), self.mine(s, 2 * here.lo, 2), self.mine(s, 2 - 2 * here.lo, 2))]
        elif mode == DIRECT:
            hops = []
        else:
            hops = [
                (here.at(dy=k), self.mine(s, here.y, 1), self.mine(s, (here.y + 4 - k) % 4, 1))
                for k in ((1, 3, 2) if mode == RING else (1, 3))
            ]
        for n, (device, part, back) in enumerate(hops):
            yield (
                remote(part, part, self.relay_send.at[s, n], self.relay_recv.at[s, n], device),
                back,
                self.relay_recv.at[s, n],
            )

    def relay(self, s, mode):
        if mode != DIRECT:
            self.wait(self.first_parts(s, mode, self.here.lo)[0], self.first_recv.at[s, 0])
        for copy, _, _ in self.relays(s, mode):
            copy.start()

    def core_copy(self, s):
        part = self.mine(s, 0, 4)
        return remote(
            part, part, self.core_sem.at[0, s], self.core_sem.at[1, s], self.here.at(core=1)
        )

    def swap(self, s):
        def act(mode):
            for n, part in enumerate(self.first_parts(s, mode, self.here.lo)):
                if n > 0 or mode == DIRECT:
                    self.wait(part, self.first_recv.at[s, n])
            for _, part, receive in self.relays(s, mode):
                self.wait(part, receive)

        self.by_mode(s, act)
        self.core_copy(s).start()

    def arrive(self, s):
        self.wait(self.rows(s, 1 - self.here.core, 0, 4), self.core_sem.at[1, s])

    def finish(self):
        for dz, dh in ORDER:
            for copy in self.firsts(dz, dh):
                copy.wait_send()

        def each(s, _):
            @pl.when(s != self.own)
            def _():
                def act(mode):
                    for copy, _, _ in self.relays(s, mode):
                        copy.wait_send()

                self.by_mode(s, act)
                self.core_copy(s).wait_send()

            return 0

        lax.fori_loop(0, SECTIONS, each, 0)


class Exchange:
    def __init__(self, here, total, give, taken, summed, ring, kept, crossed, sems):
        self.here = here
        self.total, self.give, self.taken, self.summed = total, give, taken, summed
        self.ring, self.kept, self.crossed = ring, kept, crossed
        self.core_sem, self.ring_send, self.ring_recv, self.cross_send, self.cross_recv = sems

    def shard(self, i, j, core):
        start = pl.multiple_of((2 * j + core) * SHARD, 8)
        return self.total[i, pl.ds(start, SHARD)]

    def core_copy(self, i, lo):
        return remote(
            self.give.at[i, lo],
            self.taken.at[i, lo],
            self.core_sem.at[0, i, lo],
            self.core_sem.at[1, i, lo],
            self.here.at(core=1),
        )

    def to_core(self, i, lo):
        for y in range(4):
            self.give[i, lo, y] = self.shard(i, lo * 4 + y, 1 - self.here.core).astype(BF16)
        self.core_copy(i, lo).start()

    def ring_copy(self, i, lo, k):
        return remote(
            self.summed.at[i, lo, (self.here.y + k) % 4],
            self.ring.at[i, lo, k - 1],
            self.ring_send.at[i, lo, k - 1],
            self.ring_recv.at[i, lo, k - 1],
            self.here.at(dy=k),
        )

    def to_ring(self, i, lo):
        self.core_copy(i, lo).wait_recv()
        for y in range(4):
            both = self.shard(i, lo * 4 + y, self.here.core) + self.taken[i, lo, y].astype(F32)
            self.summed[i, lo, y] = both.astype(BF16)
        for k in (2, 1, 3):
            self.ring_copy(i, lo, k).start()

    def cross_copy(self, i, slot):
        hi, lo = ((0, 1), (1, 0), (1, 1))[slot]
        return remote(
            self.kept.at[i, (self.here.lo + lo) % 2],
            self.crossed.at[slot],
            self.cross_send.at[slot],
            self.cross_recv.at[slot],
            self.here.at(hi=hi, lo=lo),
        )

    def to_cross(self, i, lo):
        here = self.here
        for k in (1, 3, 2):
            self.ring_copy(i, lo, k).wait_recv()
        value = self.summed[i, lo, here.y].astype(F32)
        for k in range(3):
            value = value + self.ring[i, lo, k].astype(F32)
        self.kept[i, lo] = value.astype(BF16)

        @pl.when((here.hi == i) & (here.lo != lo))
        def _():
            self.cross_copy(i, 0).start()

        @pl.when((here.hi != i) & (here.lo == lo))
        def _():
            self.cross_copy(i, 1).start()

        @pl.when((here.hi != i) & (here.lo != lo))
        def _():
            self.cross_copy(i, 2).start()

    def across(self):
        for i in (1, 0):
            for lo in range(2):
                self.to_cross(i, lo)

    def finish(self, grads):
        for slot in range(3):
            self.cross_copy(0, slot).wait_recv()
        value = self.kept[self.here.hi, self.here.lo].astype(F32)
        for slot in range(3):
            value = value + self.crossed[slot].astype(F32)
        grads[...] = value
        for i in range(2):
            for lo in range(2):
                self.core_copy(i, lo).wait_send()
                for k in (1, 2, 3):
                    self.ring_copy(i, lo, k).wait_send()
        for slot in range(3):
            self.cross_copy(0, slot).wait_send()


def moments(moment, second, stale):
    first = beta_one * moment + (1.0 - beta_one) * stale
    square = beta_two * second + (1.0 - beta_two) * stale * stale
    return first, square


class Renewal:
    def __init__(self, here, fresh, ring_sem, pair_sem, core_sem):
        self.here, self.fresh = here, fresh
        self.ring_sem, self.pair_sem, self.core_sem = ring_sem, pair_sem, core_sem

    def compute(self, rows, moment, second, stale):
        here = self.here
        first, square = moments(moment[...], second[...], stale[...])
        step = learn_rate * first / (jnp.sqrt(square) + adam_eps)
        self.fresh[here.lo, here.y, here.core] = (rows[...].astype(F32) - step).astype(BF16)

    def ring_copy(self, k, back=0):
        part = self.fresh.at[self.here.lo, (self.here.y + back) % 4, self.here.core]
        return remote(
            part, part, self.ring_sem.at[0, k - 1], self.ring_sem.at[1, k - 1], self.here.at(dy=k)
        )

    def pair_copy(self, lo=0):
        part = self.fresh.at[(self.here.lo + lo) % 2, :, self.here.core]
        return remote(part, part, self.pair_sem.at[0], self.pair_sem.at[1], self.here.at(lo=1))

    def core_copy(self, core=0):
        part = self.fresh.at[:, :, (self.here.core + core) % 2]
        return remote(part, part, self.core_sem.at[0], self.core_sem.at[1], self.here.at(core=1))

    def to_ring(self):
        for k in (2, 1, 3):
            self.ring_copy(k).start()

    def to_pair(self):
        for k in (1, 3, 2):
            self.ring_copy(k, 4 - k).wait_recv()
        self.pair_copy().start()

    def to_core(self):
        self.pair_copy(1).wait_recv()
        self.core_copy().start()

    def arrive(self):
        self.core_copy(1).wait_recv()

    def finish(self):
        for k in (1, 2, 3):
            self.ring_copy(k).wait_send()
        self.pair_copy().wait_send()
        self.core_copy().wait_send()


def window_kernel(
    offsets,
    clips,
    weights,
    shards16,
    moment,
    second,
    stale,
    cotangent,
    grads,
    new_weights,
    w,
    taps,
    back,
    slope,
    upstream,
    rows,
    clip,
    given,
    old,
    fresh,
    total,
    give,
    taken,
    summed,
    ring,
    kept,
    crossed,
    load_sem,
    first_send,
    first_recv,
    relay_send,
    relay_recv,
    core_sem,
    sum_core,
    sum_ring_send,
    sum_ring_recv,
    cross_send,
    cross_recv,
    renew_ring,
    renew_pair,
    renew_core,
):
    here = Place()
    gather = Gather(here, w, first_send, first_recv, relay_send, relay_recv, core_sem)
    exchange = Exchange(
        here,
        total,
        give,
        taken,
        summed,
        ring,
        kept,
        crossed,
        (sum_core, sum_ring_send, sum_ring_recv, cross_send, cross_recv),
    )
    renewal = Renewal(here, fresh, renew_ring, renew_pair, renew_core)
    load = pltpu.make_async_copy(weights, w.at[gather.own], load_sem.at[0])
    load.start()
    loads = [
        pltpu.make_async_copy(source, place, load_sem.at[n + 1])
        for n, (source, place) in enumerate(
            (
                (clips.at[here.hi], clip),
                (cotangent.at[here.hi], given),
                (shards16.at[here.lo * 8 + here.y * 2 + here.core], rows),
                (moment, old.at[0]),
                (second, old.at[1]),
                (stale, old.at[2]),
            )
        )
    ]
    barrier = pltpu.get_barrier_semaphore()
    partners = here.partners()
    for partner in partners:
        pl.semaphore_signal(barrier, inc=1, device_id=partner, device_id_type=MESH_ID)
    for other in loads:
        other.start()
    load.wait()
    pl.semaphore_wait(barrier, len(partners))
    gather.start()

    clear_edges(taps, back)
    for other in loads:
        other.wait()
    crop(clip, offsets[here.hi, 0], offsets[here.hi, 1], taps)
    reorder(given, upstream)
    renewal.compute(rows, old.at[0], old.at[1], old.at[2])

    for dz, dh in RELAYS:
        gather.relay((here.z + 4 - dz) % 4 * 2 + (here.hi + dh) % 2, MODES[dz, dh])
    renewal.to_ring()

    def forward(tick, _):
        @pl.when((tick < SECTIONS) & (tick != gather.own))
        def _():
            gather.swap(tick)

        s = tick - 1

        @pl.when(s >= 0)
        def _():
            @pl.when(s != gather.own)
            def _():
                gather.arrive(s)

            forward_section(s, w, taps, slope, SECTIONS - 1)

        return 0

    lax.fori_loop(0, SECTIONS + 1, forward, 0)
    renewal.to_pair()
    last = 2 * here.z

    def backward(i, _):
        s = SECTIONS - 1 - i
        shifted_delta(s, upstream, slope, back)

        @pl.when(s == last)
        def _():
            exchange.to_ring(1, 0)
            exchange.to_ring(1, 1)

        @pl.when(s < last + 2)
        def _():
            def put(tap, block):
                total[s % 2, tap * CHAN : (tap + 1) * CHAN] = block

            weight_grad(s, taps, back, put, lambda lo: exchange.to_core(s % 2, lo))

        @pl.when(s > last)
        def _():
            input_grad(s, w, back, upstream)

        return 0

    lax.fori_loop(0, SECTIONS - last, backward, 0)
    exchange.to_ring(0, 0)
    exchange.to_ring(0, 1)
    renewal.to_core()
    exchange.across()
    renewal.arrive()
    store = pltpu.make_async_copy(fresh, new_weights, load_sem.at[0])
    store.start()
    exchange.finish(grads)
    renewal.finish()
    gather.finish()
    store.wait()


def window(offsets, clips, weights, moment, second, stale, cotangent):
    vmem = pl.BlockSpec(memory_space=pltpu.VMEM)
    away = pl.BlockSpec(memory_space=pl.ANY)
    dma = pltpu.SemaphoreType.DMA
    shard = jax.ShapeDtypeStruct((SHARD, CHAN), F32)
    return pl.pallas_call(
        window_kernel,
        out_shape=(shard, jax.ShapeDtypeStruct((2, 4, 2, SHARD, CHAN), BF16)),
        in_specs=[pl.BlockSpec(memory_space=pltpu.SMEM)] + [away] * 7,
        out_specs=(vmem, away),
        scratch_shapes=[
            pltpu.VMEM((SECTIONS, ROWS, CHAN), BF16),
            pltpu.VMEM((SECTIONS, FRAMES, WIDTH + 2, HEIGHT, 3 * CHAN), BF16),
            pltpu.VMEM((FRAMES, WIDTH + 2, HEIGHT, 3 * CHAN), BF16),
            pltpu.VMEM((SECTIONS, CELLS, CHAN), F32),
            pltpu.VMEM((CELLS, CHAN), F32),
            pltpu.VMEM((SHARD, CHAN), BF16),
            pltpu.VMEM(clips.shape[1:], BF16),
            pltpu.VMEM(cotangent.shape[1:], BF16),
            pltpu.VMEM((3, SHARD, CHAN), F32),
            pltpu.VMEM((2, 4, 2, SHARD, CHAN), BF16),
            pltpu.VMEM((2, ROWS, CHAN), F32),
            pltpu.VMEM((2, 2, 4, SHARD, CHAN), BF16),
            pltpu.VMEM((2, 2, 4, SHARD, CHAN), BF16),
            pltpu.VMEM((2, 2, 4, SHARD, CHAN), BF16),
            pltpu.VMEM((2, 2, 3, SHARD, CHAN), BF16),
            pltpu.VMEM((2, 2, SHARD, CHAN), BF16),
            pltpu.VMEM((3, SHARD, CHAN), BF16),
            dma((7,)),
            dma((14,)),
            dma((SECTIONS, 2)),
            dma((SECTIONS, 3)),
            dma((SECTIONS, 3)),
            dma((2, SECTIONS)),
            dma((2, 2, 2)),
            dma((2, 2, 3)),
            dma((2, 2, 3)),
            dma((3,)),
            dma((3,)),
            dma((2, 3)),
            dma((2,)),
            dma((2,)),
        ],
        compiler_params=pltpu.CompilerParams(
            vmem_limit_bytes=56 << 20, collective_id=0, has_side_effects=True
        ),
    )(
        offsets,
        clips,
        weights,
        weights.reshape(16, SHARD, CHAN),
        moment,
        second,
        stale,
        cotangent,
    )


def finish_kernel(
    summed, moment, second, stale, gathered, grads, new_moment, new_second, new_weights, *scratch
):
    own, m, v, g, room, load_sem, store_sem = scratch
    places = (room, own, g, m, v)
    loads = [
        pltpu.make_async_copy(source, place, load_sem.at[n])
        for n, (source, place) in enumerate(
            zip((gathered, summed, stale, moment, second), places)
        )
    ]
    stores = [
        pltpu.make_async_copy(place, target, store_sem.at[n])
        for n, (place, target) in enumerate(
            zip((room, own, m, v), (new_weights, grads, new_moment, new_second))
        )
    ]
    for load in loads:
        load.start()
    for n in range(2):
        loads[n].wait()
        stores[n].start()
    for load in loads[2:]:
        load.wait()
    first, square = moments(m[...], v[...], g[...])
    m[...] = first
    v[...] = square
    for store in stores[2:]:
        store.start()
    for store in stores:
        store.wait()


def finish(summed, moment, second, stale, gathered):
    away = pl.BlockSpec(memory_space=pl.ANY)
    shard = jax.ShapeDtypeStruct((SHARD, CHAN), F32)
    return pl.pallas_call(
        finish_kernel,
        out_shape=(shard, shard, shard, jax.ShapeDtypeStruct(gathered.shape, BF16)),
        in_specs=[away] * 5,
        out_specs=(away,) * 4,
        scratch_shapes=[pltpu.VMEM((SHARD, CHAN), F32)] * 4
        + [
            pltpu.VMEM(gathered.shape, BF16),
            pltpu.SemaphoreType.DMA((5,)),
            pltpu.SemaphoreType.DMA((4,)),
        ],
        compiler_params=pltpu.CompilerParams(vmem_limit_bytes=56 << 20),
    )(summed, moment, second, stale, gathered)


def shards(clips, offsets, weights, moment, second, stale_grads, cotangent):
    micro = clips.shape[0]
    summed, fresh = window(
        offsets,
        clips.reshape(micro, FRAMES, -1, CHAN),
        weights[0],
        moment[0],
        second[0],
        stale_grads[0],
        cotangent.reshape(micro, FRAMES, PLANE, CHAN),
    )
    grads, first_new, second_new, fresh = finish(
        summed, moment[0], second[0], stale_grads[0], fresh
    )
    return (grads[None], first_new[None], second_new[None], fresh.reshape(1, ROWS, CHAN))


def solution(mesh):
    placed = (
        P("replica", None, None, None, None),
        P("replica", None),
        P("segment", None, None),
        P("segment", "replica", None),
        P("segment", "replica", None),
        P("segment", "replica", None),
        P("replica", None, None, None, None),
    )
    return jax.shard_map(
        shards,
        mesh=mesh,
        in_specs=placed,
        out_specs=(
            P("segment", "replica", None),
            P("segment", "replica", None),
            P("segment", "replica", None),
            P("segment", None, None),
        ),
        check_vma=False,
    )
```

```python
import math

import jax
import jax.numpy as jnp
from jax import lax
from jax.experimental import pallas as pl
from jax.experimental.pallas import tpu as pltpu
from jax.sharding import PartitionSpec as P

beta_one = 0.9
beta_two = 0.95
learn_rate = 0.05
adam_eps = 1e-08

F32 = jnp.float32
BF16 = jnp.bfloat16
FRAMES, HEIGHT, WIDTH, CHAN = 4, 16, 8, 128
PLANE = HEIGHT * WIDTH
CELLS = FRAMES * PLANE
SECTIONS = 8
TAPS = 27
ROWS = TAPS * CHAN
SCALE = 2.0 / math.sqrt(ROWS)
GRAD_SCALE = SCALE * 4.0 / math.sqrt(32 * CELLS)


def dot(a, b):
    return jnp.dot(a, b, preferred_element_type=F32)


def store_shifted(store, value):
    row = lax.broadcasted_iota(jnp.int32, (CELLS, CHAN), 0) % HEIGHT
    zero = jnp.zeros_like(value)
    for b in range(3):
        if b == 0:
            moved = jnp.where(row == 0, zero, pltpu.roll(value, 1, 0))
        elif b == 1:
            moved = value
        else:
            moved = jnp.where(row == HEIGHT - 1, zero, pltpu.roll(value, CELLS - 1, 0))
        store(b, moved.astype(BF16).reshape(FRAMES, WIDTH, HEIGHT, CHAN))


def tap_rows(w, s, tap):
    return w[s, tap * CHAN : (tap + 1) * CHAN]


def dot_turned(a, b):
    return lax.dot_general(a, b, (((1,), (1,)), ((), ())), preferred_element_type=F32)


def tap_block(w, s, times, turn, axis):
    columns = []
    for a in times:
        taps = [turn(b, c) for c in range(3) for b in range(3)]
        columns.append(
            jnp.concatenate([tap_rows(w, s, (a * 3 + b) * 3 + c) for b, c in taps], axis=axis)
        )
    return jnp.concatenate(columns, axis=1 - axis)


def field_columns(field):
    padded = field.reshape(FRAMES, WIDTH + 2, HEIGHT, 3 * CHAN)
    return jnp.concatenate(
        [padded[:, c : c + WIDTH].reshape(CELLS, 3 * CHAN) for c in range(3)], axis=1
    )


def forward_section(s, w, taps, slope):
    field = taps[s].reshape(FRAMES * (WIDTH + 2) * HEIGHT, 3 * CHAN)
    lhs = field_columns(field)
    late = dot(lhs, tap_block(w, s, (1, 2), lambda b, c: (b, c), 0))
    early = dot(lhs[: 2 * PLANE], tap_block(w, s, (0,), lambda b, c: (b, c), 0))
    total = late[:, CHAN:] + jnp.concatenate(
        [
            jnp.zeros((PLANE, CHAN), F32),
            late[:PLANE, :CHAN],
            late[PLANE : 3 * PLANE, :CHAN] + early,
        ],
        axis=0,
    )
    pre = total * SCALE
    sigma = jax.nn.sigmoid(pre)
    slope[s] = sigma * (1.0 + pre * (1.0 - sigma))

    def store(b, moved):
        taps[s + 1, :, 1 : 1 + WIDTH, :, b * CHAN : (b + 1) * CHAN] = moved

    store_shifted(store, pre * sigma)


def store_delta(s, upstream, slope, back):
    def store(b, moved):
        back[s % 2, :, 1 : 1 + WIDTH, :, b * CHAN : (b + 1) * CHAN] = moved

    store_shifted(store, upstream * slope[s])


def weight_grad(s, taps, back, put, done):
    field = taps[s, :, 1 : 1 + WIDTH, :, CHAN : 2 * CHAN].reshape(CELLS, CHAN)
    turned = field.astype(F32).T.astype(BF16)
    for a in range(3):
        frames = 2 + a
        lhs = turned[:, : frames * PLANE]
        rhs = jnp.concatenate(
            [
                back[s % 2, 2 - a : 2 - a + frames, 2 - c : 2 - c + WIDTH].reshape(
                    frames * PLANE, 3 * CHAN
                )
                for c in range(3)
            ],
            axis=1,
        )
        out = dot(lhs, rhs) * GRAD_SCALE
        for c in range(3):
            for b in range(3):
                first = (c * 3 + 2 - b) * CHAN
                put((a * 3 + b) * 3 + c, out[:, first : first + CHAN])
        if a > 0:
            done(a - 1)


def input_grad(s, w, back, slope):
    field = back[s % 2].reshape(FRAMES * (WIDTH + 2) * HEIGHT, 3 * CHAN)
    lhs = field_columns(field)
    flip = lambda b, c: (2 - b, 2 - c)
    late = dot_turned(lhs, tap_block(w, s, (1, 2), flip, 1))
    early = dot_turned(lhs[2 * PLANE :], tap_block(w, s, (0,), flip, 1))
    total = late[:, CHAN:] + jnp.concatenate(
        [
            late[PLANE : 2 * PLANE, :CHAN] + early[:PLANE],
            late[2 * PLANE : 3 * PLANE, :CHAN] + early[PLANE:],
            late[3 * PLANE :, :CHAN],
            jnp.zeros((PLANE, CHAN), F32),
        ],
        axis=0,
    )
    store_delta(s - 1, total * SCALE, slope, back)


def crop(clip, offset_y, offset_x, taps):
    row = lax.broadcasted_iota(jnp.int32, (PLANE, clip.shape[-2]), 0)
    col = lax.broadcasted_iota(jnp.int32, (PLANE, clip.shape[-2]), 1)
    clip_w = 16
    want = (row % HEIGHT + offset_y) * clip_w + row // HEIGHT + offset_x
    pick = jnp.where(want == col, 1.0, 0.0).astype(BF16)
    field = jnp.concatenate([dot(pick, clip[t]) for t in range(FRAMES)], axis=0)

    def store(b, moved):
        taps[0, :, 1 : 1 + WIDTH, :, b * CHAN : (b + 1) * CHAN] = moved

    store_shifted(store, field)


def reorder(cotangent, upstream):
    row = lax.broadcasted_iota(jnp.int32, (PLANE, PLANE), 0)
    col = lax.broadcasted_iota(jnp.int32, (PLANE, PLANE), 1)
    pick = jnp.where(row % HEIGHT * WIDTH + row // HEIGHT == col, 1.0, 0.0).astype(BF16)
    for t in range(FRAMES):
        upstream[t * PLANE : (t + 1) * PLANE] = dot(pick, cotangent[t])


def clear_edges(taps, back):
    edge = jnp.zeros((FRAMES, HEIGHT, 3 * CHAN), BF16)

    def wipe(s, _):
        taps[s, :, 0] = edge
        taps[s, :, WIDTH + 1] = edge
        return 0

    lax.fori_loop(0, SECTIONS, wipe, 0)
    for n in range(2):
        back[n, :, 0] = edge
        back[n, :, WIDTH + 1] = edge


MESH_ID = pl.DeviceIdType.MESH
HALF = ROWS // 2
PIECE = HALF // 4
SHARD = ROWS // 16


class Place:
    def __init__(self):
        segment = lax.axis_index("segment")
        replica = lax.axis_index("replica")
        self.z, self.hi = segment // 2, segment % 2
        self.lo, self.y, self.core = replica // 8, replica // 2 % 4, replica % 2

    def at(self, dz=0, hi=0, lo=0, dy=0, core=0):
        z = (self.z + dz) % 4
        y = (self.y + dy) % 4
        own = [(self.hi + hi) % 2, (self.lo + lo) % 2, (self.core + core) % 2]
        return (z * 2 + own[0], own[1] * 8 + y * 2 + own[2])

    def partners(self):
        away = [self.at(dz=k) for k in (1, 2, 3)]
        across = [self.at(dz=k, hi=1, lo=1) for k in range(4)]
        return away + across + [self.at(lo=1), self.at(hi=1)] + [self.at(dy=k) for k in (1, 2, 3)] + [self.at(core=1)]


def remote(src, dst, send, receive, device):
    return pltpu.make_async_remote_copy(
        src_ref=src,
        dst_ref=dst,
        send_sem=send,
        recv_sem=receive,
        device_id=device,
        device_id_type=MESH_ID,
    )


DIRECT, PAIR, RING, NEAR = range(4)
MODES = {(1, 0): DIRECT, (3, 0): DIRECT, (2, 0): NEAR, (0, 1): DIRECT, (1, 1): RING, (3, 1): RING, (2, 1): RING}
ORDER = ((2, 0), (2, 1), (1, 0), (3, 0), (0, 1), (1, 1), (3, 1))
RELAYS = ((1, 1), (3, 1), (2, 1), (2, 0))
SENDS = (((1, 1), (2, 1), (3, 1), (2, 0), (0, 1), (1, 0), (3, 0)), ((3, 1), (1, 1), (2, 1), (2, 0), (3, 0), (0, 1), (1, 0)), ((2, 1), (3, 1), (1, 1), (2, 0), (3, 0), (0, 1), (1, 0)), ((1, 1), (2, 1), (3, 1), (2, 0), (1, 0), (3, 0), (0, 1)))


class Gather:
    def __init__(self, here, w, first_send, first_recv, relay_send, relay_recv, core_sem):
        self.here, self.w = here, w
        self.first_send, self.first_recv = first_send, first_recv
        self.relay_send, self.relay_recv = relay_send, relay_recv
        self.core_sem = core_sem
        self.own = here.z * 2 + here.hi

    def rows(self, s, core, start, count):
        first = core * HALF + start * PIECE
        return self.w.at[s, pl.ds(pl.multiple_of(first, PIECE), count * PIECE)]

    def mine(self, s, start, count):
        return self.rows(s, self.here.core, start, count)

    def first_parts(self, s, mode, lo):
        if mode == DIRECT:
            return [self.mine(s, 0, 4)]
        if mode == PAIR:
            return [self.mine(s, 2 * lo, 2)]
        if mode == RING:
            return [self.mine(s, self.here.y, 1)]
        return [self.mine(s, self.here.y, 1), self.mine(s, (self.here.y + 2) % 4, 1)]

    def firsts(self, dz, dh):
        lo = (self.here.lo + dh) % 2
        slot = 2 * ORDER.index((dz, dh))
        for n, part in enumerate(self.first_parts(self.own, MODES[dz, dh], lo)):
            yield remote(
                part,
                part,
                self.first_send.at[slot + n],
                self.first_recv.at[self.own, n],
                self.here.at(dz=dz, hi=dh, lo=dh),
            )

    def start(self):
        for z in range(4):

            @pl.when(self.here.z == z)
            def _():
                for dz, dh in SENDS[z]:
                    for copy in self.firsts(dz, dh):
                        copy.start()

    def by_mode(self, s, act):
        dz = (self.here.z + 4 - s // 2) % 4
        dh = (self.here.hi + s) % 2
        for mode in range(4):
            hits = [key for key, value in MODES.items() if value == mode]
            if hits:
                cond = (dz == hits[0][0]) & (dh == hits[0][1])
                for key in hits[1:]:
                    cond = cond | ((dz == key[0]) & (dh == key[1]))

                @pl.when(cond)
                def _():
                    act(mode)

    def wait(self, part, receive):
        remote(part, part, self.first_send.at[0], receive, self.here.at()).wait_recv()

    def relays(self, s, mode):
        here = self.here
        if mode == PAIR:
            hops = [(here.at(lo=1), self.mine(s, 2 * here.lo, 2), self.mine(s, 2 - 2 * here.lo, 2))]
        elif mode == DIRECT:
            hops = []
        else:
            hops = [
                (here.at(dy=k), self.mine(s, here.y, 1), self.mine(s, (here.y + 4 - k) % 4, 1))
                for k in ((1, 3, 2) if mode == RING else (1, 3))
            ]
        for n, (device, part, back) in enumerate(hops):
            yield (
                remote(part, part, self.relay_send.at[s, n], self.relay_recv.at[s, n], device),
                back,
                self.relay_recv.at[s, n],
            )

    def relay(self, s, mode):
        if mode != DIRECT:
            self.wait(self.first_parts(s, mode, self.here.lo)[0], self.first_recv.at[s, 0])
        for copy, _, _ in self.relays(s, mode):
            copy.start()

    def core_copy(self, s):
        part = self.mine(s, 0, 4)
        return remote(
            part, part, self.core_sem.at[0, s], self.core_sem.at[1, s], self.here.at(core=1)
        )

    def swap(self, s):
        def act(mode):
            for n, part in enumerate(self.first_parts(s, mode, self.here.lo)):
                if n > 0 or mode == DIRECT:
                    self.wait(part, self.first_recv.at[s, n])
            for _, part, receive in self.relays(s, mode):
                self.wait(part, receive)

        self.by_mode(s, act)
        self.core_copy(s).start()

    def arrive(self, s):
        self.wait(self.rows(s, 1 - self.here.core, 0, 4), self.core_sem.at[1, s])

    def finish(self):
        for dz, dh in ORDER:
            for copy in self.firsts(dz, dh):
                copy.wait_send()

        def each(s, _):
            @pl.when(s != self.own)
            def _():
                def act(mode):
                    for copy, _, _ in self.relays(s, mode):
                        copy.wait_send()

                self.by_mode(s, act)
                self.core_copy(s).wait_send()

            return 0

        lax.fori_loop(0, SECTIONS, each, 0)


class Exchange:
    def __init__(self, here, total, give, taken, summed, ring, kept, crossed, sems):
        self.here = here
        self.total, self.give, self.taken, self.summed = total, give, taken, summed
        self.ring, self.kept, self.crossed = ring, kept, crossed
        self.core_sem, self.ring_send, self.ring_recv, self.cross_send, self.cross_recv = sems

    def shard(self, i, j, core):
        start = pl.multiple_of((2 * j + core) * SHARD, 8)
        return self.total[i, pl.ds(start, SHARD)]

    def core_copy(self, i, lo):
        return remote(
            self.give.at[i, lo],
            self.taken.at[i, lo],
            self.core_sem.at[0, i, lo],
            self.core_sem.at[1, i, lo],
            self.here.at(core=1),
        )

    def to_core(self, i, lo):
        for y in range(4):
            self.give[i, lo, y] = self.shard(i, lo * 4 + y, 1 - self.here.core).astype(BF16)
        self.core_copy(i, lo).start()

    def ring_copy(self, i, lo, k):
        return remote(
            self.summed.at[i, lo, (self.here.y + k) % 4],
            self.ring.at[i, lo, k - 1],
            self.ring_send.at[i, lo, k - 1],
            self.ring_recv.at[i, lo, k - 1],
            self.here.at(dy=k),
        )

    def to_ring(self, i, lo):
        self.core_copy(i, lo).wait_recv()
        for y in range(4):
            both = self.shard(i, lo * 4 + y, self.here.core) + self.taken[i, lo, y].astype(F32)
            self.summed[i, lo, y] = both.astype(BF16)
        for k in (2, 1, 3):
            self.ring_copy(i, lo, k).start()

    def cross_copy(self, i, slot):
        hi, lo = ((0, 1), (1, 0), (1, 1))[slot]
        return remote(
            self.kept.at[i, (self.here.lo + lo) % 2],
            self.crossed.at[slot],
            self.cross_send.at[slot],
            self.cross_recv.at[slot],
            self.here.at(hi=hi, lo=lo),
        )

    def to_cross(self, i, lo):
        here = self.here
        for k in (1, 3, 2):
            self.ring_copy(i, lo, k).wait_recv()
        value = self.summed[i, lo, here.y].astype(F32)
        for k in range(3):
            value = value + self.ring[i, lo, k].astype(F32)
        self.kept[i, lo] = value.astype(BF16)

        @pl.when((here.hi == i) & (here.lo != lo))
        def _():
            self.cross_copy(i, 0).start()

        @pl.when((here.hi != i) & (here.lo == lo))
        def _():
            self.cross_copy(i, 1).start()

        @pl.when((here.hi != i) & (here.lo != lo))
        def _():
            self.cross_copy(i, 2).start()

    def across(self):
        for i in (1, 0):
            for lo in range(2):
                self.to_cross(i, lo)

    def finish(self, grads):
        for slot in range(3):
            self.cross_copy(0, slot).wait_recv()
        value = self.kept[self.here.hi, self.here.lo].astype(F32)
        for slot in range(3):
            value = value + self.crossed[slot].astype(F32)
        grads[...] = value
        for i in range(2):
            for lo in range(2):
                self.core_copy(i, lo).wait_send()
                for k in (1, 2, 3):
                    self.ring_copy(i, lo, k).wait_send()
        for slot in range(3):
            self.cross_copy(0, slot).wait_send()


def moments(moment, second, stale):
    first = beta_one * moment + (1.0 - beta_one) * stale
    square = beta_two * second + (1.0 - beta_two) * stale * stale
    return first, square


class Renewal:
    def __init__(self, here, fresh, ring_sem, pair_sem, core_sem):
        self.here, self.fresh = here, fresh
        self.ring_sem, self.pair_sem, self.core_sem = ring_sem, pair_sem, core_sem

    def compute(self, rows, moment, second, stale):
        here = self.here
        first, square = moments(moment[...], second[...], stale[...])
        step = learn_rate * first / (jnp.sqrt(square) + adam_eps)
        self.fresh[here.lo, here.y, here.core] = (rows[...].astype(F32) - step).astype(BF16)

    def ring_copy(self, k, back=0):
        part = self.fresh.at[self.here.lo, (self.here.y + back) % 4, self.here.core]
        return remote(
            part, part, self.ring_sem.at[0, k - 1], self.ring_sem.at[1, k - 1], self.here.at(dy=k)
        )

    def pair_copy(self, lo=0):
        part = self.fresh.at[(self.here.lo + lo) % 2, :, self.here.core]
        return remote(part, part, self.pair_sem.at[0], self.pair_sem.at[1], self.here.at(lo=1))

    def core_copy(self, core=0):
        part = self.fresh.at[:, :, (self.here.core + core) % 2]
        return remote(part, part, self.core_sem.at[0], self.core_sem.at[1], self.here.at(core=1))

    def to_ring(self):
        for k in (2, 1, 3):
            self.ring_copy(k).start()

    def to_pair(self):
        for k in (1, 3, 2):
            self.ring_copy(k, 4 - k).wait_recv()
        self.pair_copy().start()

    def to_core(self):
        self.pair_copy(1).wait_recv()
        self.core_copy().start()

    def arrive(self):
        self.core_copy(1).wait_recv()

    def finish(self):
        for k in (1, 2, 3):
            self.ring_copy(k).wait_send()
        self.pair_copy().wait_send()
        self.core_copy().wait_send()


def window_kernel(
    offsets,
    clips,
    weights,
    shards16,
    moment,
    second,
    stale,
    cotangent,
    grads,
    new_weights,
    w,
    taps,
    back,
    slope,
    upstream,
    rows,
    clip,
    given,
    old,
    fresh,
    total,
    give,
    taken,
    summed,
    ring,
    kept,
    crossed,
    load_sem,
    first_send,
    first_recv,
    relay_send,
    relay_recv,
    core_sem,
    sum_core,
    sum_ring_send,
    sum_ring_recv,
    cross_send,
    cross_recv,
    renew_ring,
    renew_pair,
    renew_core,
):
    here = Place()
    gather = Gather(here, w, first_send, first_recv, relay_send, relay_recv, core_sem)
    exchange = Exchange(
        here,
        total,
        give,
        taken,
        summed,
        ring,
        kept,
        crossed,
        (sum_core, sum_ring_send, sum_ring_recv, cross_send, cross_recv),
    )
    renewal = Renewal(here, fresh, renew_ring, renew_pair, renew_core)
    load = pltpu.make_async_copy(weights, w.at[gather.own], load_sem.at[0])
    load.start()
    loads = [
        pltpu.make_async_copy(source, place, load_sem.at[n + 1])
        for n, (source, place) in enumerate(
            (
                (clips.at[here.hi], clip),
                (cotangent.at[here.hi], given),
                (shards16.at[here.lo * 8 + here.y * 2 + here.core], rows),
                (moment, old.at[0]),
                (second, old.at[1]),
                (stale, old.at[2]),
            )
        )
    ]
    barrier = pltpu.get_barrier_semaphore()
    partners = here.partners()
    for partner in partners:
        pl.semaphore_signal(barrier, inc=1, device_id=partner, device_id_type=MESH_ID)
    for other in loads:
        other.start()
    load.wait()
    pl.semaphore_wait(barrier, len(partners))
    gather.start()

    clear_edges(taps, back)
    for other in loads:
        other.wait()
    crop(clip, offsets[here.hi, 0], offsets[here.hi, 1], taps)
    reorder(given, upstream)
    renewal.compute(rows, old.at[0], old.at[1], old.at[2])

    for dz, dh in RELAYS:
        gather.relay((here.z + 4 - dz) % 4 * 2 + (here.hi + dh) % 2, MODES[dz, dh])
    renewal.to_ring()

    def forward(tick, _):
        @pl.when((tick < SECTIONS) & (tick != gather.own))
        def _():
            gather.swap(tick)

        s = tick - 1

        @pl.when(s >= 0)
        def _():
            @pl.when(s != gather.own)
            def _():
                gather.arrive(s)

            forward_section(s, w, taps, slope)

        return 0

    lax.fori_loop(0, SECTIONS + 1, forward, 0)
    renewal.to_pair()
    last = 2 * here.z

    def backward(i, _):
        s = SECTIONS - 1 - i

        @pl.when(s == last)
        def _():
            exchange.to_ring(1, 0)
            exchange.to_ring(1, 1)

        @pl.when(s < last + 2)
        def _():
            def put(tap, block):
                total[s % 2, tap * CHAN : (tap + 1) * CHAN] = block

            weight_grad(s, taps, back, put, lambda lo: exchange.to_core(s % 2, lo))

        @pl.when(s > last)
        def _():
            input_grad(s, w, back, slope)

        return 0

    store_delta(SECTIONS - 1, upstream[...], slope, back)
    lax.fori_loop(0, SECTIONS - last, backward, 0)
    exchange.to_ring(0, 0)
    exchange.to_ring(0, 1)
    renewal.to_core()
    gather.finish()
    exchange.across()
    renewal.arrive()
    store = pltpu.make_async_copy(fresh, new_weights, load_sem.at[0])
    store.start()
    exchange.finish(grads)
    renewal.finish()
    store.wait()


def window(offsets, clips, weights, moment, second, stale, cotangent):
    vmem = pl.BlockSpec(memory_space=pltpu.VMEM)
    away = pl.BlockSpec(memory_space=pl.ANY)
    dma = pltpu.SemaphoreType.DMA
    shard = jax.ShapeDtypeStruct((SHARD, CHAN), F32)
    return pl.pallas_call(
        window_kernel,
        out_shape=(shard, jax.ShapeDtypeStruct((2, 4, 2, SHARD, CHAN), BF16)),
        in_specs=[pl.BlockSpec(memory_space=pltpu.SMEM)] + [away] * 7,
        out_specs=(vmem, away),
        scratch_shapes=[
            pltpu.VMEM((SECTIONS, ROWS, CHAN), BF16),
            pltpu.VMEM((SECTIONS + 1, FRAMES, WIDTH + 2, HEIGHT, 3 * CHAN), BF16),
            pltpu.VMEM((2, FRAMES, WIDTH + 2, HEIGHT, 3 * CHAN), BF16),
            pltpu.VMEM((SECTIONS, CELLS, CHAN), F32),
            pltpu.VMEM((CELLS, CHAN), F32),
            pltpu.VMEM((SHARD, CHAN), BF16),
            pltpu.VMEM(clips.shape[1:], BF16),
            pltpu.VMEM(cotangent.shape[1:], BF16),
            pltpu.VMEM((3, SHARD, CHAN), F32),
            pltpu.VMEM((2, 4, 2, SHARD, CHAN), BF16),
            pltpu.VMEM((2, ROWS, CHAN), F32),
            pltpu.VMEM((2, 2, 4, SHARD, CHAN), BF16),
            pltpu.VMEM((2, 2, 4, SHARD, CHAN), BF16),
            pltpu.VMEM((2, 2, 4, SHARD, CHAN), BF16),
            pltpu.VMEM((2, 2, 3, SHARD, CHAN), BF16),
            pltpu.VMEM((2, 2, SHARD, CHAN), BF16),
            pltpu.VMEM((3, SHARD, CHAN), BF16),
            dma((7,)),
            dma((14,)),
            dma((SECTIONS, 2)),
            dma((SECTIONS, 3)),
            dma((SECTIONS, 3)),
            dma((2, SECTIONS)),
            dma((2, 2, 2)),
            dma((2, 2, 3)),
            dma((2, 2, 3)),
            dma((3,)),
            dma((3,)),
            dma((2, 3)),
            dma((2,)),
            dma((2,)),
        ],
        compiler_params=pltpu.CompilerParams(
            vmem_limit_bytes=56 << 20, collective_id=0, has_side_effects=True
        ),
    )(
        offsets,
        clips,
        weights,
        weights.reshape(16, SHARD, CHAN),
        moment,
        second,
        stale,
        cotangent,
    )


def finish_kernel(
    summed, moment, second, stale, gathered, grads, new_moment, new_second, new_weights, *scratch
):
    own, m, v, g, room, load_sem, store_sem = scratch
    places = (room, own, g, m, v)
    loads = [
        pltpu.make_async_copy(source, place, load_sem.at[n])
        for n, (source, place) in enumerate(
            zip((gathered, summed, stale, moment, second), places)
        )
    ]
    stores = [
        pltpu.make_async_copy(place, target, store_sem.at[n])
        for n, (place, target) in enumerate(
            zip((room, own, m, v), (new_weights, grads, new_moment, new_second))
        )
    ]
    for load in loads:
        load.start()
    for n in range(2):
        loads[n].wait()
        stores[n].start()
    for load in loads[2:]:
        load.wait()
    first, square = moments(m[...], v[...], g[...])
    m[...] = first
    v[...] = square
    for store in stores[2:]:
        store.start()
    for store in stores:
        store.wait()


def finish(summed, moment, second, stale, gathered):
    away = pl.BlockSpec(memory_space=pl.ANY)
    shard = jax.ShapeDtypeStruct((SHARD, CHAN), F32)
    return pl.pallas_call(
        finish_kernel,
        out_shape=(shard, shard, shard, jax.ShapeDtypeStruct(gathered.shape, BF16)),
        in_specs=[away] * 5,
        out_specs=(away,) * 4,
        scratch_shapes=[pltpu.VMEM((SHARD, CHAN), F32)] * 4
        + [
            pltpu.VMEM(gathered.shape, BF16),
            pltpu.SemaphoreType.DMA((5,)),
            pltpu.SemaphoreType.DMA((4,)),
        ],
        compiler_params=pltpu.CompilerParams(vmem_limit_bytes=56 << 20),
    )(summed, moment, second, stale, gathered)


def shards(clips, offsets, weights, moment, second, stale_grads, cotangent):
    micro = clips.shape[0]
    summed, fresh = window(
        offsets,
        clips.reshape(micro, FRAMES, -1, CHAN),
        weights[0],
        moment[0],
        second[0],
        stale_grads[0],
        cotangent.reshape(micro, FRAMES, PLANE, CHAN),
    )
    grads, first_new, second_new, fresh = finish(
        summed, moment[0], second[0], stale_grads[0], fresh
    )
    return (grads[None], first_new[None], second_new[None], fresh.reshape(1, ROWS, CHAN))


def solution(mesh):
    placed = (
        P("replica", None, None, None, None),
        P("replica", None),
        P("segment", None, None),
        P("segment", "replica", None),
        P("segment", "replica", None),
        P("segment", "replica", None),
        P("replica", None, None, None, None),
    )
    return jax.shard_map(
        shards,
        mesh=mesh,
        in_specs=placed,
        out_specs=(
            P("segment", "replica", None),
            P("segment", "replica", None),
            P("segment", "replica", None),
            P("segment", None, None),
        ),
        check_vma=False,
    )
```

```python
import math

import jax
import jax.numpy as jnp
from jax import lax
from jax.experimental import pallas as pl
from jax.experimental.pallas import tpu as pltpu
from jax.sharding import PartitionSpec as P

beta_one = 0.9
beta_two = 0.95
learn_rate = 0.05
adam_eps = 1e-08

F32 = jnp.float32
BF16 = jnp.bfloat16
FRAMES, HEIGHT, WIDTH, CHAN = 4, 16, 8, 128
PLANE = HEIGHT * WIDTH
CELLS = FRAMES * PLANE
SECTIONS = 8
TAPS = 27
ROWS = TAPS * CHAN
SCALE = 2.0 / math.sqrt(ROWS)
GRAD_SCALE = SCALE * 4.0 / math.sqrt(32 * CELLS)


def dot(a, b):
    return jnp.dot(a, b, preferred_element_type=F32)


def store_shifted(store, value):
    row = lax.broadcasted_iota(jnp.int32, (CELLS, CHAN), 0) % HEIGHT
    zero = jnp.zeros_like(value)
    for b in range(3):
        if b == 0:
            moved = jnp.where(row == 0, zero, pltpu.roll(value, 1, 0))
        elif b == 1:
            moved = value
        else:
            moved = jnp.where(row == HEIGHT - 1, zero, pltpu.roll(value, CELLS - 1, 0))
        store(b, moved.astype(BF16).reshape(FRAMES, WIDTH, HEIGHT, CHAN))


def tap_rows(w, s, tap):
    return w[s, tap * CHAN : (tap + 1) * CHAN]


def dot_turned(a, b):
    return lax.dot_general(a, b, (((1,), (1,)), ((), ())), preferred_element_type=F32)


def tap_block(w, s, times, turn, axis):
    columns = []
    for a in times:
        taps = [turn(b, c) for c in range(3) for b in range(3)]
        columns.append(
            jnp.concatenate([tap_rows(w, s, (a * 3 + b) * 3 + c) for b, c in taps], axis=axis)
        )
    return jnp.concatenate(columns, axis=1 - axis)


def field_columns(field):
    padded = field.reshape(FRAMES, WIDTH + 2, HEIGHT, 3 * CHAN)
    return jnp.concatenate(
        [padded[:, c : c + WIDTH].reshape(CELLS, 3 * CHAN) for c in range(3)], axis=1
    )


def forward_section(s, w, taps, slope):
    field = taps[s].reshape(FRAMES * (WIDTH + 2) * HEIGHT, 3 * CHAN)
    lhs = field_columns(field)
    late = dot(lhs, tap_block(w, s, (1, 2), lambda b, c: (b, c), 0))
    early = dot(lhs[: 2 * PLANE], tap_block(w, s, (0,), lambda b, c: (b, c), 0))
    total = late[:, CHAN:] + jnp.concatenate(
        [
            jnp.zeros((PLANE, CHAN), F32),
            late[:PLANE, :CHAN],
            late[PLANE : 3 * PLANE, :CHAN] + early,
        ],
        axis=0,
    )
    pre = total * SCALE
    sigma = jax.nn.sigmoid(pre)
    slope[s] = sigma * (1.0 + pre * (1.0 - sigma))

    def store(b, moved):
        taps[s + 1, :, 1 : 1 + WIDTH, :, b * CHAN : (b + 1) * CHAN] = moved

    store_shifted(store, pre * sigma)


def store_delta(s, upstream, slope, back):
    def store(b, moved):
        back[s % 2, :, 1 : 1 + WIDTH, :, b * CHAN : (b + 1) * CHAN] = moved

    store_shifted(store, upstream * slope[s])


def weight_grad(s, taps, back, put, done):
    field = taps[s, :, 1 : 1 + WIDTH, :, CHAN : 2 * CHAN].reshape(CELLS, CHAN)
    turned = field.astype(F32).T.astype(BF16)
    for a in range(3):
        frames = 2 + a
        lhs = turned[:, : frames * PLANE]
        rhs = jnp.concatenate(
            [
                back[s % 2, 2 - a : 2 - a + frames, 2 - c : 2 - c + WIDTH].reshape(
                    frames * PLANE, 3 * CHAN
                )
                for c in range(3)
            ],
            axis=1,
        )
        out = dot(lhs, rhs) * GRAD_SCALE
        for c in range(3):
            for b in range(3):
                first = (c * 3 + 2 - b) * CHAN
                put((a * 3 + b) * 3 + c, out[:, first : first + CHAN])
        if a > 0:
            done(a - 1)


def input_grad(s, w, back, slope):
    field = back[s % 2].reshape(FRAMES * (WIDTH + 2) * HEIGHT, 3 * CHAN)
    lhs = field_columns(field)
    flip = lambda b, c: (2 - b, 2 - c)
    late = dot_turned(lhs, tap_block(w, s, (1, 2), flip, 1))
    early = dot_turned(lhs[2 * PLANE :], tap_block(w, s, (0,), flip, 1))
    total = late[:, CHAN:] + jnp.concatenate(
        [
            late[PLANE : 2 * PLANE, :CHAN] + early[:PLANE],
            late[2 * PLANE : 3 * PLANE, :CHAN] + early[PLANE:],
            late[3 * PLANE :, :CHAN],
            jnp.zeros((PLANE, CHAN), F32),
        ],
        axis=0,
    )
    store_delta(s - 1, total * SCALE, slope, back)


def crop(clip, offset_y, offset_x, taps):
    row = lax.broadcasted_iota(jnp.int32, (PLANE, clip.shape[-2]), 0)
    col = lax.broadcasted_iota(jnp.int32, (PLANE, clip.shape[-2]), 1)
    clip_w = 16
    want = (row % HEIGHT + offset_y) * clip_w + row // HEIGHT + offset_x
    pick = jnp.where(want == col, 1.0, 0.0).astype(BF16)
    field = jnp.concatenate([dot(pick, clip[t]) for t in range(FRAMES)], axis=0)

    def store(b, moved):
        taps[0, :, 1 : 1 + WIDTH, :, b * CHAN : (b + 1) * CHAN] = moved

    store_shifted(store, field)


def reorder(cotangent, upstream):
    row = lax.broadcasted_iota(jnp.int32, (PLANE, PLANE), 0)
    col = lax.broadcasted_iota(jnp.int32, (PLANE, PLANE), 1)
    pick = jnp.where(row % HEIGHT * WIDTH + row // HEIGHT == col, 1.0, 0.0).astype(BF16)
    for t in range(FRAMES):
        upstream[t * PLANE : (t + 1) * PLANE] = dot(pick, cotangent[t])


def clear_edges(taps, back):
    edge = jnp.zeros((FRAMES, HEIGHT, 3 * CHAN), BF16)

    def wipe(s, _):
        taps[s, :, 0] = edge
        taps[s, :, WIDTH + 1] = edge
        return 0

    lax.fori_loop(0, SECTIONS, wipe, 0)
    for n in range(2):
        back[n, :, 0] = edge
        back[n, :, WIDTH + 1] = edge


MESH_ID = pl.DeviceIdType.MESH
HALF = ROWS // 2
PIECE = HALF // 4
SHARD = ROWS // 16


class Place:
    def __init__(self):
        segment = lax.axis_index("segment")
        replica = lax.axis_index("replica")
        self.z, self.hi = segment // 2, segment % 2
        self.lo, self.y, self.core = replica // 8, replica // 2 % 4, replica % 2

    def at(self, dz=0, hi=0, lo=0, dy=0, core=0):
        z = (self.z + dz) % 4
        y = (self.y + dy) % 4
        own = [(self.hi + hi) % 2, (self.lo + lo) % 2, (self.core + core) % 2]
        return (z * 2 + own[0], own[1] * 8 + y * 2 + own[2])

    def partners(self):
        away = [self.at(dz=k) for k in (1, 2, 3)]
        across = [self.at(dz=k, hi=1, lo=1) for k in range(4)]
        return away + across + [self.at(lo=1), self.at(hi=1)] + [self.at(dy=k) for k in (1, 2, 3)] + [self.at(core=1)]


def remote(src, dst, send, receive, device):
    return pltpu.make_async_remote_copy(
        src_ref=src,
        dst_ref=dst,
        send_sem=send,
        recv_sem=receive,
        device_id=device,
        device_id_type=MESH_ID,
    )


DIRECT, PAIR, RING, NEAR = range(4)
MODES = {(1, 0): DIRECT, (3, 0): DIRECT, (2, 0): NEAR, (0, 1): DIRECT, (1, 1): RING, (3, 1): RING, (2, 1): RING}
ORDER = ((2, 0), (2, 1), (1, 0), (3, 0), (0, 1), (1, 1), (3, 1))
RELAYS = ((1, 1), (3, 1), (2, 1), (2, 0))
SENDS = (((1, 1), (2, 1), (3, 1), (2, 0), (0, 1), (1, 0), (3, 0)), ((3, 1), (1, 1), (2, 1), (2, 0), (3, 0), (0, 1), (1, 0)), ((2, 1), (3, 1), (1, 1), (2, 0), (3, 0), (0, 1), (1, 0)), ((1, 1), (2, 1), (3, 1), (2, 0), (1, 0), (3, 0), (0, 1)))


class Gather:
    def __init__(self, here, w, first_send, first_recv, relay_send, relay_recv, core_sem):
        self.here, self.w = here, w
        self.first_send, self.first_recv = first_send, first_recv
        self.relay_send, self.relay_recv = relay_send, relay_recv
        self.core_sem = core_sem
        self.own = here.z * 2 + here.hi

    def rows(self, s, core, start, count):
        first = core * HALF + start * PIECE
        return self.w.at[s, pl.ds(pl.multiple_of(first, PIECE), count * PIECE)]

    def mine(self, s, start, count):
        return self.rows(s, self.here.core, start, count)

    def first_parts(self, s, mode, lo):
        if mode == DIRECT:
            return [self.mine(s, 0, 4)]
        if mode == PAIR:
            return [self.mine(s, 2 * lo, 2)]
        if mode == RING:
            return [self.mine(s, self.here.y, 1)]
        return [self.mine(s, self.here.y, 1), self.mine(s, (self.here.y + 2) % 4, 1)]

    def firsts(self, dz, dh):
        lo = (self.here.lo + dh) % 2
        slot = 2 * ORDER.index((dz, dh))
        for n, part in enumerate(self.first_parts(self.own, MODES[dz, dh], lo)):
            yield remote(
                part,
                part,
                self.first_send.at[slot + n],
                self.first_recv.at[self.own, n],
                self.here.at(dz=dz, hi=dh, lo=dh),
            )

    def start(self):
        for z in range(4):

            @pl.when(self.here.z == z)
            def _():
                for dz, dh in SENDS[z]:
                    for copy in self.firsts(dz, dh):
                        copy.start()

    def by_mode(self, s, act):
        dz = (self.here.z + 4 - s // 2) % 4
        dh = (self.here.hi + s) % 2
        for mode in range(4):
            hits = [key for key, value in MODES.items() if value == mode]
            if hits:
                cond = (dz == hits[0][0]) & (dh == hits[0][1])
                for key in hits[1:]:
                    cond = cond | ((dz == key[0]) & (dh == key[1]))

                @pl.when(cond)
                def _():
                    act(mode)

    def wait(self, part, receive):
        remote(part, part, self.first_send.at[0], receive, self.here.at()).wait_recv()

    def relays(self, s, mode):
        here = self.here
        if mode == PAIR:
            hops = [(here.at(lo=1), self.mine(s, 2 * here.lo, 2), self.mine(s, 2 - 2 * here.lo, 2))]
        elif mode == DIRECT:
            hops = []
        else:
            hops = [
                (here.at(dy=k), self.mine(s, here.y, 1), self.mine(s, (here.y + 4 - k) % 4, 1))
                for k in ((2, 1, 3) if mode == RING else (1, 3))
            ]
        for n, (device, part, back) in enumerate(hops):
            yield (
                remote(part, part, self.relay_send.at[s, n], self.relay_recv.at[s, n], device),
                back,
                self.relay_recv.at[s, n],
            )

    def relay(self, s, mode):
        if mode != DIRECT:
            self.wait(self.first_parts(s, mode, self.here.lo)[0], self.first_recv.at[s, 0])
        for copy, _, _ in self.relays(s, mode):
            copy.start()

    def core_copy(self, s):
        part = self.mine(s, 0, 4)
        return remote(
            part, part, self.core_sem.at[0, s], self.core_sem.at[1, s], self.here.at(core=1)
        )

    def swap(self, s):
        def act(mode):
            for n, part in enumerate(self.first_parts(s, mode, self.here.lo)):
                if n > 0 or mode == DIRECT:
                    self.wait(part, self.first_recv.at[s, n])
            for _, part, receive in self.relays(s, mode):
                self.wait(part, receive)

        self.by_mode(s, act)
        self.core_copy(s).start()

    def arrive(self, s):
        self.wait(self.rows(s, 1 - self.here.core, 0, 4), self.core_sem.at[1, s])

    def finish(self):
        for dz, dh in ORDER:
            for copy in self.firsts(dz, dh):
                copy.wait_send()

        def each(s, _):
            @pl.when(s != self.own)
            def _():
                def act(mode):
                    for copy, _, _ in self.relays(s, mode):
                        copy.wait_send()

                self.by_mode(s, act)
                self.core_copy(s).wait_send()

            return 0

        lax.fori_loop(0, SECTIONS, each, 0)


class Exchange:
    def __init__(self, here, total, give, taken, summed, ring, kept, crossed, sems):
        self.here = here
        self.total, self.give, self.taken, self.summed = total, give, taken, summed
        self.ring, self.kept, self.crossed = ring, kept, crossed
        self.core_sem, self.ring_send, self.ring_recv, self.cross_send, self.cross_recv = sems

    def shard(self, i, j, core):
        start = pl.multiple_of((2 * j + core) * SHARD, 8)
        return self.total[i, pl.ds(start, SHARD)]

    def core_copy(self, i, lo):
        return remote(
            self.give.at[i, lo],
            self.taken.at[i, lo],
            self.core_sem.at[0, i, lo],
            self.core_sem.at[1, i, lo],
            self.here.at(core=1),
        )

    def to_core(self, i, lo):
        for y in range(4):
            self.give[i, lo, y] = self.shard(i, lo * 4 + y, 1 - self.here.core).astype(BF16)
        self.core_copy(i, lo).start()

    def ring_copy(self, i, lo, k):
        return remote(
            self.summed.at[i, lo, (self.here.y + k) % 4],
            self.ring.at[i, lo, k - 1],
            self.ring_send.at[i, lo, k - 1],
            self.ring_recv.at[i, lo, k - 1],
            self.here.at(dy=k),
        )

    def to_ring(self, i, lo):
        self.core_copy(i, lo).wait_recv()
        for y in range(4):
            both = self.shard(i, lo * 4 + y, self.here.core) + self.taken[i, lo, y].astype(F32)
            self.summed[i, lo, y] = both.astype(BF16)
        for k in (2, 1, 3):
            self.ring_copy(i, lo, k).start()

    def cross_copy(self, i, slot):
        hi, lo = ((0, 1), (1, 0), (1, 1))[slot]
        return remote(
            self.kept.at[i, (self.here.lo + lo) % 2],
            self.crossed.at[slot],
            self.cross_send.at[slot],
            self.cross_recv.at[slot],
            self.here.at(hi=hi, lo=lo),
        )

    def to_cross(self, i, lo):
        here = self.here
        for k in (1, 3, 2):
            self.ring_copy(i, lo, k).wait_recv()
        value = self.summed[i, lo, here.y].astype(F32)
        for k in range(3):
            value = value + self.ring[i, lo, k].astype(F32)
        self.kept[i, lo] = value.astype(BF16)

        @pl.when((here.hi == i) & (here.lo != lo))
        def _():
            self.cross_copy(i, 0).start()

        @pl.when((here.hi != i) & (here.lo == lo))
        def _():
            self.cross_copy(i, 1).start()

        @pl.when((here.hi != i) & (here.lo != lo))
        def _():
            self.cross_copy(i, 2).start()

    def across(self):
        for i in (1, 0):
            for lo in range(2):
                self.to_cross(i, lo)

    def finish(self, grads):
        for slot in range(3):
            self.cross_copy(0, slot).wait_recv()
        value = self.kept[self.here.hi, self.here.lo].astype(F32)
        for slot in range(3):
            value = value + self.crossed[slot].astype(F32)
        grads[...] = value
        for i in range(2):
            for lo in range(2):
                self.core_copy(i, lo).wait_send()
                for k in (1, 2, 3):
                    self.ring_copy(i, lo, k).wait_send()
        for slot in range(3):
            self.cross_copy(0, slot).wait_send()


def moments(moment, second, stale):
    first = beta_one * moment + (1.0 - beta_one) * stale
    square = beta_two * second + (1.0 - beta_two) * stale * stale
    return first, square


class Renewal:
    def __init__(self, here, fresh, ring_sem, pair_sem, core_sem):
        self.here, self.fresh = here, fresh
        self.ring_sem, self.pair_sem, self.core_sem = ring_sem, pair_sem, core_sem

    def compute(self, rows, moment, second, stale):
        here = self.here
        first, square = moments(moment[...], second[...], stale[...])
        step = learn_rate * first / (jnp.sqrt(square) + adam_eps)
        self.fresh[here.lo, here.y, here.core] = (rows[...].astype(F32) - step).astype(BF16)

    def ring_copy(self, k, back=0):
        part = self.fresh.at[self.here.lo, (self.here.y + back) % 4, self.here.core]
        return remote(
            part, part, self.ring_sem.at[0, k - 1], self.ring_sem.at[1, k - 1], self.here.at(dy=k)
        )

    def pair_copy(self, lo=0):
        part = self.fresh.at[(self.here.lo + lo) % 2, :, self.here.core]
        return remote(part, part, self.pair_sem.at[0], self.pair_sem.at[1], self.here.at(lo=1))

    def core_copy(self, core=0):
        part = self.fresh.at[:, :, (self.here.core + core) % 2]
        return remote(part, part, self.core_sem.at[0], self.core_sem.at[1], self.here.at(core=1))

    def to_ring(self):
        for k in (2, 1, 3):
            self.ring_copy(k).start()

    def to_pair(self):
        for k in (1, 3, 2):
            self.ring_copy(k, 4 - k).wait_recv()
        self.pair_copy().start()

    def to_core(self):
        self.pair_copy(1).wait_recv()
        self.core_copy().start()

    def arrive(self):
        self.core_copy(1).wait_recv()

    def finish(self):
        for k in (1, 2, 3):
            self.ring_copy(k).wait_send()
        self.pair_copy().wait_send()
        self.core_copy().wait_send()


def window_kernel(
    offsets,
    clips,
    weights,
    shards16,
    moment,
    second,
    stale,
    cotangent,
    grads,
    new_weights,
    w,
    taps,
    back,
    slope,
    upstream,
    rows,
    clip,
    given,
    old,
    fresh,
    total,
    give,
    taken,
    summed,
    ring,
    kept,
    crossed,
    load_sem,
    first_send,
    first_recv,
    relay_send,
    relay_recv,
    core_sem,
    sum_core,
    sum_ring_send,
    sum_ring_recv,
    cross_send,
    cross_recv,
    renew_ring,
    renew_pair,
    renew_core,
):
    here = Place()
    gather = Gather(here, w, first_send, first_recv, relay_send, relay_recv, core_sem)
    exchange = Exchange(
        here,
        total,
        give,
        taken,
        summed,
        ring,
        kept,
        crossed,
        (sum_core, sum_ring_send, sum_ring_recv, cross_send, cross_recv),
    )
    renewal = Renewal(here, fresh, renew_ring, renew_pair, renew_core)
    load = pltpu.make_async_copy(weights, w.at[gather.own], load_sem.at[0])
    load.start()
    loads = [
        pltpu.make_async_copy(source, place, load_sem.at[n + 1])
        for n, (source, place) in enumerate(
            (
                (clips.at[here.hi], clip),
                (cotangent.at[here.hi], given),
                (shards16.at[here.lo * 8 + here.y * 2 + here.core], rows),
                (moment, old.at[0]),
                (second, old.at[1]),
                (stale, old.at[2]),
            )
        )
    ]
    barrier = pltpu.get_barrier_semaphore()
    partners = here.partners()
    for partner in partners:
        pl.semaphore_signal(barrier, inc=1, device_id=partner, device_id_type=MESH_ID)
    for other in loads:
        other.start()
    load.wait()
    pl.semaphore_wait(barrier, len(partners))
    gather.start()

    clear_edges(taps, back)
    for other in loads:
        other.wait()
    crop(clip, offsets[here.hi, 0], offsets[here.hi, 1], taps)
    reorder(given, upstream)
    renewal.compute(rows, old.at[0], old.at[1], old.at[2])

    for dz, dh in RELAYS:
        gather.relay((here.z + 4 - dz) % 4 * 2 + (here.hi + dh) % 2, MODES[dz, dh])
    renewal.to_ring()

    def forward(tick, _):
        @pl.when((tick < SECTIONS) & (tick != gather.own))
        def _():
            gather.swap(tick)

        s = tick - 2

        @pl.when(s >= 0)
        def _():
            @pl.when(s != gather.own)
            def _():
                gather.arrive(s)

            forward_section(s, w, taps, slope)

        return 0

    lax.fori_loop(0, SECTIONS + 2, forward, 0)
    renewal.to_pair()
    last = 2 * here.z

    def backward(i, _):
        s = SECTIONS - 1 - i

        @pl.when(s == last)
        def _():
            exchange.to_ring(1, 0)
            exchange.to_ring(1, 1)

        @pl.when(s < last + 2)
        def _():
            def put(tap, block):
                total[s % 2, tap * CHAN : (tap + 1) * CHAN] = block

            weight_grad(s, taps, back, put, lambda lo: exchange.to_core(s % 2, lo))

        @pl.when(s > last)
        def _():
            input_grad(s, w, back, slope)

        return 0

    store_delta(SECTIONS - 1, upstream[...], slope, back)
    lax.fori_loop(0, SECTIONS - last, backward, 0)
    exchange.to_ring(0, 0)
    exchange.to_ring(0, 1)
    renewal.to_core()
    gather.finish()
    exchange.across()
    renewal.arrive()
    store = pltpu.make_async_copy(fresh, new_weights, load_sem.at[0])
    store.start()
    exchange.finish(grads)
    renewal.finish()
    store.wait()


def window(offsets, clips, weights, moment, second, stale, cotangent):
    vmem = pl.BlockSpec(memory_space=pltpu.VMEM)
    away = pl.BlockSpec(memory_space=pl.ANY)
    dma = pltpu.SemaphoreType.DMA
    shard = jax.ShapeDtypeStruct((SHARD, CHAN), F32)
    return pl.pallas_call(
        window_kernel,
        out_shape=(shard, jax.ShapeDtypeStruct((2, 4, 2, SHARD, CHAN), BF16)),
        in_specs=[pl.BlockSpec(memory_space=pltpu.SMEM)] + [away] * 7,
        out_specs=(vmem, away),
        scratch_shapes=[
            pltpu.VMEM((SECTIONS, ROWS, CHAN), BF16),
            pltpu.VMEM((SECTIONS + 1, FRAMES, WIDTH + 2, HEIGHT, 3 * CHAN), BF16),
            pltpu.VMEM((2, FRAMES, WIDTH + 2, HEIGHT, 3 * CHAN), BF16),
            pltpu.VMEM((SECTIONS, CELLS, CHAN), F32),
            pltpu.VMEM((CELLS, CHAN), F32),
            pltpu.VMEM((SHARD, CHAN), BF16),
            pltpu.VMEM(clips.shape[1:], BF16),
            pltpu.VMEM(cotangent.shape[1:], BF16),
            pltpu.VMEM((3, SHARD, CHAN), F32),
            pltpu.VMEM((2, 4, 2, SHARD, CHAN), BF16),
            pltpu.VMEM((2, ROWS, CHAN), F32),
            pltpu.VMEM((2, 2, 4, SHARD, CHAN), BF16),
            pltpu.VMEM((2, 2, 4, SHARD, CHAN), BF16),
            pltpu.VMEM((2, 2, 4, SHARD, CHAN), BF16),
            pltpu.VMEM((2, 2, 3, SHARD, CHAN), BF16),
            pltpu.VMEM((2, 2, SHARD, CHAN), BF16),
            pltpu.VMEM((3, SHARD, CHAN), BF16),
            dma((7,)),
            dma((14,)),
            dma((SECTIONS, 2)),
            dma((SECTIONS, 3)),
            dma((SECTIONS, 3)),
            dma((2, SECTIONS)),
            dma((2, 2, 2)),
            dma((2, 2, 3)),
            dma((2, 2, 3)),
            dma((3,)),
            dma((3,)),
            dma((2, 3)),
            dma((2,)),
            dma((2,)),
        ],
        compiler_params=pltpu.CompilerParams(
            vmem_limit_bytes=56 << 20, collective_id=0, has_side_effects=True
        ),
    )(
        offsets,
        clips,
        weights,
        weights.reshape(16, SHARD, CHAN),
        moment,
        second,
        stale,
        cotangent,
    )


def finish_kernel(
    summed, moment, second, stale, gathered, grads, new_moment, new_second, new_weights, *scratch
):
    own, m, v, g, room, load_sem, store_sem = scratch
    places = (room, own, g, m, v)
    loads = [
        pltpu.make_async_copy(source, place, load_sem.at[n])
        for n, (source, place) in enumerate(
            zip((gathered, summed, stale, moment, second), places)
        )
    ]
    stores = [
        pltpu.make_async_copy(place, target, store_sem.at[n])
        for n, (place, target) in enumerate(
            zip((room, own, m, v), (new_weights, grads, new_moment, new_second))
        )
    ]
    for load in loads:
        load.start()
    for n in range(2):
        loads[n].wait()
        stores[n].start()
    for load in loads[2:]:
        load.wait()
    first, square = moments(m[...], v[...], g[...])
    m[...] = first
    v[...] = square
    for store in stores[2:]:
        store.start()
    for store in stores:
        store.wait()


def finish(summed, moment, second, stale, gathered):
    away = pl.BlockSpec(memory_space=pl.ANY)
    shard = jax.ShapeDtypeStruct((SHARD, CHAN), F32)
    return pl.pallas_call(
        finish_kernel,
        out_shape=(shard, shard, shard, jax.ShapeDtypeStruct(gathered.shape, BF16)),
        in_specs=[away] * 5,
        out_specs=(away,) * 4,
        scratch_shapes=[pltpu.VMEM((SHARD, CHAN), F32)] * 4
        + [
            pltpu.VMEM(gathered.shape, BF16),
            pltpu.SemaphoreType.DMA((5,)),
            pltpu.SemaphoreType.DMA((4,)),
        ],
        compiler_params=pltpu.CompilerParams(vmem_limit_bytes=56 << 20),
    )(summed, moment, second, stale, gathered)


def shards(clips, offsets, weights, moment, second, stale_grads, cotangent):
    micro = clips.shape[0]
    summed, fresh = window(
        offsets,
        clips.reshape(micro, FRAMES, -1, CHAN),
        weights[0],
        moment[0],
        second[0],
        stale_grads[0],
        cotangent.reshape(micro, FRAMES, PLANE, CHAN),
    )
    grads, first_new, second_new, fresh = finish(
        summed, moment[0], second[0], stale_grads[0], fresh
    )
    return (grads[None], first_new[None], second_new[None], fresh.reshape(1, ROWS, CHAN))


def solution(mesh):
    placed = (
        P("replica", None, None, None, None),
        P("replica", None),
        P("segment", None, None),
        P("segment", "replica", None),
        P("segment", "replica", None),
        P("segment", "replica", None),
        P("replica", None, None, None, None),
    )
    return jax.shard_map(
        shards,
        mesh=mesh,
        in_specs=placed,
        out_specs=(
            P("segment", "replica", None),
            P("segment", "replica", None),
            P("segment", "replica", None),
            P("segment", None, None),
        ),
        check_vma=False,
    )
```

```python
import math

import jax
import jax.numpy as jnp
from jax import lax
from jax.experimental import pallas as pl
from jax.experimental.pallas import tpu as pltpu
from jax.sharding import PartitionSpec as P

beta_one = 0.9
beta_two = 0.95
learn_rate = 0.05
adam_eps = 1e-08

F32 = jnp.float32
BF16 = jnp.bfloat16
FRAMES, HEIGHT, WIDTH, CHAN = 4, 16, 8, 128
PLANE = HEIGHT * WIDTH
CELLS = FRAMES * PLANE
SECTIONS = 8
TAPS = 27
ROWS = TAPS * CHAN
SCALE = 2.0 / math.sqrt(ROWS)
GRAD_SCALE = SCALE * 4.0 / math.sqrt(32 * CELLS)


def dot(a, b):
    return jnp.dot(a, b, preferred_element_type=F32)


def store_shifted(store, value):
    row = lax.broadcasted_iota(jnp.int32, (CELLS, CHAN), 0) % HEIGHT
    zero = jnp.zeros_like(value)
    for b in range(3):
        if b == 0:
            moved = jnp.where(row == 0, zero, pltpu.roll(value, 1, 0))
        elif b == 1:
            moved = value
        else:
            moved = jnp.where(row == HEIGHT - 1, zero, pltpu.roll(value, CELLS - 1, 0))
        store(b, moved.astype(BF16).reshape(FRAMES, WIDTH, HEIGHT, CHAN))


def tap_rows(w, s, tap):
    return w[s, tap * CHAN : (tap + 1) * CHAN]


def dot_turned(a, b):
    return lax.dot_general(a, b, (((1,), (1,)), ((), ())), preferred_element_type=F32)


def tap_block(w, s, times, turn, axis):
    columns = []
    for a in times:
        taps = [turn(b, c) for c in range(3) for b in range(3)]
        columns.append(
            jnp.concatenate([tap_rows(w, s, (a * 3 + b) * 3 + c) for b, c in taps], axis=axis)
        )
    return jnp.concatenate(columns, axis=1 - axis)


def field_columns(field):
    padded = field.reshape(FRAMES, WIDTH + 2, HEIGHT, 3 * CHAN)
    return jnp.concatenate(
        [padded[:, c : c + WIDTH].reshape(CELLS, 3 * CHAN) for c in range(3)], axis=1
    )


def forward_section(s, w, taps, slope):
    field = taps[s].reshape(FRAMES * (WIDTH + 2) * HEIGHT, 3 * CHAN)
    lhs = field_columns(field)
    late = dot(lhs, tap_block(w, s, (1, 2), lambda b, c: (b, c), 0))
    early = dot(lhs[: 2 * PLANE], tap_block(w, s, (0,), lambda b, c: (b, c), 0))
    total = late[:, CHAN:] + jnp.concatenate(
        [
            jnp.zeros((PLANE, CHAN), F32),
            late[:PLANE, :CHAN],
            late[PLANE : 3 * PLANE, :CHAN] + early,
        ],
        axis=0,
    )
    pre = total * SCALE
    sigma = jax.nn.sigmoid(pre)
    slope[s] = sigma * (1.0 + pre * (1.0 - sigma))

    def store(b, moved):
        taps[s + 1, :, 1 : 1 + WIDTH, :, b * CHAN : (b + 1) * CHAN] = moved

    store_shifted(store, pre * sigma)


def store_delta(s, upstream, slope, back):
    def store(b, moved):
        back[s % 2, :, 1 : 1 + WIDTH, :, b * CHAN : (b + 1) * CHAN] = moved

    store_shifted(store, upstream * slope[s])


def weight_grad(s, taps, back, put, done):
    field = taps[s, :, 1 : 1 + WIDTH, :, CHAN : 2 * CHAN].reshape(CELLS, CHAN)
    turned = field.astype(F32).T.astype(BF16)
    for a in range(3):
        frames = 2 + a
        lhs = turned[:, : frames * PLANE]
        rhs = jnp.concatenate(
            [
                back[s % 2, 2 - a : 2 - a + frames, 2 - c : 2 - c + WIDTH].reshape(
                    frames * PLANE, 3 * CHAN
                )
                for c in range(3)
            ],
            axis=1,
        )
        out = dot(lhs, rhs) * GRAD_SCALE
        for c in range(3):
            for b in range(3):
                first = (c * 3 + 2 - b) * CHAN
                put((a * 3 + b) * 3 + c, out[:, first : first + CHAN])
        if a > 0:
            done(a - 1)


def input_grad(s, w, back, slope):
    field = back[s % 2].reshape(FRAMES * (WIDTH + 2) * HEIGHT, 3 * CHAN)
    lhs = field_columns(field)
    flip = lambda b, c: (2 - b, 2 - c)
    late = dot_turned(lhs, tap_block(w, s, (1, 2), flip, 1))
    early = dot_turned(lhs[2 * PLANE :], tap_block(w, s, (0,), flip, 1))
    total = late[:, CHAN:] + jnp.concatenate(
        [
            late[PLANE : 2 * PLANE, :CHAN] + early[:PLANE],
            late[2 * PLANE : 3 * PLANE, :CHAN] + early[PLANE:],
            late[3 * PLANE :, :CHAN],
            jnp.zeros((PLANE, CHAN), F32),
        ],
        axis=0,
    )
    store_delta(s - 1, total * SCALE, slope, back)


def crop(clip, offset_y, offset_x, taps):
    row = lax.broadcasted_iota(jnp.int32, (PLANE, clip.shape[-2]), 0)
    col = lax.broadcasted_iota(jnp.int32, (PLANE, clip.shape[-2]), 1)
    clip_w = 16
    want = (row % HEIGHT + offset_y) * clip_w + row // HEIGHT + offset_x
    pick = jnp.where(want == col, 1.0, 0.0).astype(BF16)
    field = jnp.concatenate([dot(pick, clip[t]) for t in range(FRAMES)], axis=0)

    def store(b, moved):
        taps[0, :, 1 : 1 + WIDTH, :, b * CHAN : (b + 1) * CHAN] = moved

    store_shifted(store, field)


def reorder(cotangent, upstream):
    row = lax.broadcasted_iota(jnp.int32, (PLANE, PLANE), 0)
    col = lax.broadcasted_iota(jnp.int32, (PLANE, PLANE), 1)
    pick = jnp.where(row % HEIGHT * WIDTH + row // HEIGHT == col, 1.0, 0.0).astype(BF16)
    for t in range(FRAMES):
        upstream[t * PLANE : (t + 1) * PLANE] = dot(pick, cotangent[t])


def clear_edges(taps, back):
    edge = jnp.zeros((FRAMES, HEIGHT, 3 * CHAN), BF16)

    def wipe(s, _):
        taps[s, :, 0] = edge
        taps[s, :, WIDTH + 1] = edge
        return 0

    lax.fori_loop(0, SECTIONS, wipe, 0)
    for n in range(2):
        back[n, :, 0] = edge
        back[n, :, WIDTH + 1] = edge


MESH_ID = pl.DeviceIdType.MESH
HALF = ROWS // 2
PIECE = HALF // 4
SHARD = ROWS // 16


class Place:
    def __init__(self):
        segment = lax.axis_index("segment")
        replica = lax.axis_index("replica")
        self.z, self.hi = segment // 2, segment % 2
        self.lo, self.y, self.core = replica // 8, replica // 2 % 4, replica % 2

    def at(self, dz=0, hi=0, lo=0, dy=0, core=0):
        z = (self.z + dz) % 4
        y = (self.y + dy) % 4
        own = [(self.hi + hi) % 2, (self.lo + lo) % 2, (self.core + core) % 2]
        return (z * 2 + own[0], own[1] * 8 + y * 2 + own[2])

    def partners(self):
        away = [self.at(dz=k) for k in (1, 2, 3)]
        across = [self.at(dz=k, hi=1, lo=1) for k in range(4)]
        return away + across + [self.at(lo=1), self.at(hi=1)] + [self.at(dy=k) for k in (1, 2, 3)] + [self.at(core=1)]


def remote(src, dst, send, receive, device):
    return pltpu.make_async_remote_copy(
        src_ref=src,
        dst_ref=dst,
        send_sem=send,
        recv_sem=receive,
        device_id=device,
        device_id_type=MESH_ID,
    )


DIRECT, PAIR, RING, NEAR = range(4)
MODES = {(1, 0): DIRECT, (3, 0): DIRECT, (2, 0): NEAR, (0, 1): DIRECT, (1, 1): RING, (3, 1): RING, (2, 1): RING}
ORDER = ((2, 0), (2, 1), (1, 0), (3, 0), (0, 1), (1, 1), (3, 1))
RELAYS = ((1, 1), (3, 1), (2, 1), (2, 0))
SENDS = (((2, 1), (3, 1), (1, 1), (2, 0), (0, 1), (3, 0), (1, 0)), ((3, 1), (1, 1), (2, 1), (2, 0), (3, 0), (1, 0), (0, 1)), ((2, 1), (1, 1), (3, 1), (2, 0), (0, 1), (1, 0), (3, 0)), ((1, 1), (3, 1), (2, 1), (2, 0), (1, 0), (3, 0), (0, 1)))


class Gather:
    def __init__(self, here, w, first_send, first_recv, relay_send, relay_recv, core_sem):
        self.here, self.w = here, w
        self.first_send, self.first_recv = first_send, first_recv
        self.relay_send, self.relay_recv = relay_send, relay_recv
        self.core_sem = core_sem
        self.own = here.z * 2 + here.hi

    def rows(self, s, core, start, count):
        first = core * HALF + start * PIECE
        return self.w.at[s, pl.ds(pl.multiple_of(first, PIECE), count * PIECE)]

    def mine(self, s, start, count):
        return self.rows(s, self.here.core, start, count)

    def first_parts(self, s, mode, lo):
        if mode == DIRECT:
            return [self.mine(s, 0, 4)]
        if mode == PAIR:
            return [self.mine(s, 2 * lo, 2)]
        if mode == RING:
            return [self.mine(s, self.here.y, 1)]
        return [self.mine(s, self.here.y, 1), self.mine(s, (self.here.y + 2) % 4, 1)]

    def firsts(self, dz, dh):
        lo = (self.here.lo + dh) % 2
        slot = 2 * ORDER.index((dz, dh))
        for n, part in enumerate(self.first_parts(self.own, MODES[dz, dh], lo)):
            yield remote(
                part,
                part,
                self.first_send.at[slot + n],
                self.first_recv.at[self.own, n],
                self.here.at(dz=dz, hi=dh, lo=dh),
            )

    def start(self):
        for z in range(4):

            @pl.when(self.here.z == z)
            def _():
                for dz, dh in SENDS[z]:
                    for copy in self.firsts(dz, dh):
                        copy.start()

    def by_mode(self, s, act):
        dz = (self.here.z + 4 - s // 2) % 4
        dh = (self.here.hi + s) % 2
        for mode in range(4):
            hits = [key for key, value in MODES.items() if value == mode]
            if hits:
                cond = (dz == hits[0][0]) & (dh == hits[0][1])
                for key in hits[1:]:
                    cond = cond | ((dz == key[0]) & (dh == key[1]))

                @pl.when(cond)
                def _():
                    act(mode)

    def wait(self, part, receive):
        remote(part, part, self.first_send.at[0], receive, self.here.at()).wait_recv()

    def relays(self, s, mode):
        here = self.here
        if mode == PAIR:
            hops = [(here.at(lo=1), self.mine(s, 2 * here.lo, 2), self.mine(s, 2 - 2 * here.lo, 2))]
        elif mode == DIRECT:
            hops = []
        else:
            hops = [
                (here.at(dy=k), self.mine(s, here.y, 1), self.mine(s, (here.y + 4 - k) % 4, 1))
                for k in ((2, 1, 3) if mode == RING else (1, 3))
            ]
        for n, (device, part, back) in enumerate(hops):
            yield (
                remote(part, part, self.relay_send.at[s, n], self.relay_recv.at[s, n], device),
                back,
                self.relay_recv.at[s, n],
            )

    def relay(self, s, mode):
        if mode != DIRECT:
            self.wait(self.first_parts(s, mode, self.here.lo)[0], self.first_recv.at[s, 0])
        for copy, _, _ in self.relays(s, mode):
            copy.start()

    def core_copy(self, s):
        part = self.mine(s, 0, 4)
        return remote(
            part, part, self.core_sem.at[0, s], self.core_sem.at[1, s], self.here.at(core=1)
        )

    def swap(self, s):
        def act(mode):
            for n, part in enumerate(self.first_parts(s, mode, self.here.lo)):
                if n > 0 or mode == DIRECT:
                    self.wait(part, self.first_recv.at[s, n])
            for _, part, receive in self.relays(s, mode):
                self.wait(part, receive)

        self.by_mode(s, act)
        self.core_copy(s).start()

    def arrive(self, s):
        self.wait(self.rows(s, 1 - self.here.core, 0, 4), self.core_sem.at[1, s])

    def finish(self):
        for dz, dh in ORDER:
            for copy in self.firsts(dz, dh):
                copy.wait_send()

        def each(s, _):
            @pl.when(s != self.own)
            def _():
                def act(mode):
                    for copy, _, _ in self.relays(s, mode):
                        copy.wait_send()

                self.by_mode(s, act)
                self.core_copy(s).wait_send()

            return 0

        lax.fori_loop(0, SECTIONS, each, 0)


class Exchange:
    def __init__(self, here, total, give, taken, summed, ring, kept, crossed, sems):
        self.here = here
        self.total, self.give, self.taken, self.summed = total, give, taken, summed
        self.ring, self.kept, self.crossed = ring, kept, crossed
        self.core_sem, self.ring_send, self.ring_recv, self.cross_send, self.cross_recv = sems

    def shard(self, i, j, core):
        start = pl.multiple_of((2 * j + core) * SHARD, 8)
        return self.total[i, pl.ds(start, SHARD)]

    def core_copy(self, i, lo):
        return remote(
            self.give.at[i, lo],
            self.taken.at[i, lo],
            self.core_sem.at[0, i, lo],
            self.core_sem.at[1, i, lo],
            self.here.at(core=1),
        )

    def to_core(self, i, lo):
        for y in range(4):
            self.give[i, lo, y] = self.shard(i, lo * 4 + y, 1 - self.here.core).astype(BF16)
        self.core_copy(i, lo).start()

    def ring_copy(self, i, lo, k):
        return remote(
            self.summed.at[i, lo, (self.here.y + k) % 4],
            self.ring.at[i, lo, k - 1],
            self.ring_send.at[i, lo, k - 1],
            self.ring_recv.at[i, lo, k - 1],
            self.here.at(dy=k),
        )

    def to_ring(self, i, lo):
        self.core_copy(i, lo).wait_recv()
        for y in range(4):
            both = self.shard(i, lo * 4 + y, self.here.core) + self.taken[i, lo, y].astype(F32)
            self.summed[i, lo, y] = both.astype(BF16)
        for k in (2, 1, 3):
            self.ring_copy(i, lo, k).start()

    def cross_copy(self, i, slot):
        hi, lo = ((0, 1), (1, 0), (1, 1))[slot]
        return remote(
            self.kept.at[i, (self.here.lo + lo) % 2],
            self.crossed.at[slot],
            self.cross_send.at[slot],
            self.cross_recv.at[slot],
            self.here.at(hi=hi, lo=lo),
        )

    def to_cross(self, i, lo):
        here = self.here
        for k in (1, 3, 2):
            self.ring_copy(i, lo, k).wait_recv()
        value = self.summed[i, lo, here.y].astype(F32)
        for k in range(3):
            value = value + self.ring[i, lo, k].astype(F32)
        self.kept[i, lo] = value.astype(BF16)

        @pl.when((here.hi == i) & (here.lo != lo))
        def _():
            self.cross_copy(i, 0).start()

        @pl.when((here.hi != i) & (here.lo == lo))
        def _():
            self.cross_copy(i, 1).start()

        @pl.when((here.hi != i) & (here.lo != lo))
        def _():
            self.cross_copy(i, 2).start()

    def across(self):
        for lo in range(2):
            for i in (1, 0):
                self.to_cross(i, lo)

    def finish(self, grads):
        for slot in range(3):
            self.cross_copy(0, slot).wait_recv()
        value = self.kept[self.here.hi, self.here.lo].astype(F32)
        for slot in range(3):
            value = value + self.crossed[slot].astype(F32)
        grads[...] = value
        for i in range(2):
            for lo in range(2):
                self.core_copy(i, lo).wait_send()
                for k in (1, 2, 3):
                    self.ring_copy(i, lo, k).wait_send()
        for slot in range(3):
            self.cross_copy(0, slot).wait_send()


def moments(moment, second, stale):
    first = beta_one * moment + (1.0 - beta_one) * stale
    square = beta_two * second + (1.0 - beta_two) * stale * stale
    return first, square


class Renewal:
    def __init__(self, here, fresh, ring_sem, pair_sem, core_sem):
        self.here, self.fresh = here, fresh
        self.ring_sem, self.pair_sem, self.core_sem = ring_sem, pair_sem, core_sem

    def compute(self, rows, moment, second, stale):
        here = self.here
        first, square = moments(moment[...], second[...], stale[...])
        step = learn_rate * first / (jnp.sqrt(square) + adam_eps)
        self.fresh[here.lo, here.y, here.core] = (rows[...].astype(F32) - step).astype(BF16)

    def ring_copy(self, k, back=0):
        part = self.fresh.at[self.here.lo, (self.here.y + back) % 4, self.here.core]
        return remote(
            part, part, self.ring_sem.at[0, k - 1], self.ring_sem.at[1, k - 1], self.here.at(dy=k)
        )

    def pair_copy(self, lo=0):
        part = self.fresh.at[(self.here.lo + lo) % 2, :, self.here.core]
        return remote(part, part, self.pair_sem.at[0], self.pair_sem.at[1], self.here.at(lo=1))

    def core_copy(self, core=0):
        part = self.fresh.at[:, :, (self.here.core + core) % 2]
        return remote(part, part, self.core_sem.at[0], self.core_sem.at[1], self.here.at(core=1))

    def to_ring(self):
        for k in (2, 1, 3):
            self.ring_copy(k).start()

    def to_pair(self):
        for k in (1, 3, 2):
            self.ring_copy(k, 4 - k).wait_recv()
        self.pair_copy().start()

    def to_core(self):
        self.pair_copy(1).wait_recv()
        self.core_copy().start()

    def arrive(self):
        self.core_copy(1).wait_recv()

    def finish(self):
        for k in (1, 2, 3):
            self.ring_copy(k).wait_send()
        self.pair_copy().wait_send()
        self.core_copy().wait_send()


def window_kernel(
    offsets,
    clips,
    weights,
    shards16,
    moment,
    second,
    stale,
    cotangent,
    grads,
    new_weights,
    w,
    taps,
    back,
    slope,
    upstream,
    rows,
    clip,
    given,
    old,
    fresh,
    total,
    give,
    taken,
    summed,
    ring,
    kept,
    crossed,
    load_sem,
    first_send,
    first_recv,
    relay_send,
    relay_recv,
    core_sem,
    sum_core,
    sum_ring_send,
    sum_ring_recv,
    cross_send,
    cross_recv,
    renew_ring,
    renew_pair,
    renew_core,
):
    here = Place()
    gather = Gather(here, w, first_send, first_recv, relay_send, relay_recv, core_sem)
    exchange = Exchange(
        here,
        total,
        give,
        taken,
        summed,
        ring,
        kept,
        crossed,
        (sum_core, sum_ring_send, sum_ring_recv, cross_send, cross_recv),
    )
    renewal = Renewal(here, fresh, renew_ring, renew_pair, renew_core)
    load = pltpu.make_async_copy(weights, w.at[gather.own], load_sem.at[0])
    load.start()
    loads = [
        pltpu.make_async_copy(source, place, load_sem.at[n + 1])
        for n, (source, place) in enumerate(
            (
                (clips.at[here.hi], clip),
                (cotangent.at[here.hi], given),
                (shards16.at[here.lo * 8 + here.y * 2 + here.core], rows),
                (moment, old.at[0]),
                (second, old.at[1]),
                (stale, old.at[2]),
            )
        )
    ]
    barrier = pltpu.get_barrier_semaphore()
    partners = here.partners()
    for partner in partners:
        pl.semaphore_signal(barrier, inc=1, device_id=partner, device_id_type=MESH_ID)
    for other in loads:
        other.start()
    load.wait()
    pl.semaphore_wait(barrier, len(partners))
    gather.start()

    clear_edges(taps, back)
    for other in loads:
        other.wait()
    crop(clip, offsets[here.hi, 0], offsets[here.hi, 1], taps)
    reorder(given, upstream)
    renewal.compute(rows, old.at[0], old.at[1], old.at[2])

    for dz, dh in RELAYS:
        gather.relay((here.z + 4 - dz) % 4 * 2 + (here.hi + dh) % 2, MODES[dz, dh])
    renewal.to_ring()

    def forward(tick, _):
        @pl.when((tick < SECTIONS) & (tick != gather.own))
        def _():
            gather.swap(tick)

        s = tick - 2

        @pl.when(s >= 0)
        def _():
            @pl.when(s != gather.own)
            def _():
                gather.arrive(s)

            forward_section(s, w, taps, slope)

        return 0

    lax.fori_loop(0, SECTIONS + 2, forward, 0)
    renewal.to_pair()
    last = 2 * here.z

    def backward(i, _):
        s = SECTIONS - 1 - i

        @pl.when(s == last)
        def _():
            exchange.to_ring(1, 0)

        @pl.when(s < last + 2)
        def _():
            def put(tap, block):
                total[s % 2, tap * CHAN : (tap + 1) * CHAN] = block

            weight_grad(s, taps, back, put, lambda lo: exchange.to_core(s % 2, lo))

        @pl.when(s > last)
        def _():
            input_grad(s, w, back, slope)

        return 0

    store_delta(SECTIONS - 1, upstream[...], slope, back)
    lax.fori_loop(0, SECTIONS - last, backward, 0)
    exchange.to_ring(1, 1)
    exchange.to_ring(0, 0)
    exchange.to_ring(0, 1)
    renewal.to_core()
    gather.finish()
    exchange.across()
    renewal.arrive()
    store = pltpu.make_async_copy(fresh, new_weights, load_sem.at[0])
    store.start()
    exchange.finish(grads)
    renewal.finish()
    store.wait()


def window(offsets, clips, weights, moment, second, stale, cotangent):
    vmem = pl.BlockSpec(memory_space=pltpu.VMEM)
    away = pl.BlockSpec(memory_space=pl.ANY)
    dma = pltpu.SemaphoreType.DMA
    shard = jax.ShapeDtypeStruct((SHARD, CHAN), F32)
    return pl.pallas_call(
        window_kernel,
        out_shape=(shard, jax.ShapeDtypeStruct((2, 4, 2, SHARD, CHAN), BF16)),
        in_specs=[pl.BlockSpec(memory_space=pltpu.SMEM)] + [away] * 7,
        out_specs=(vmem, away),
        scratch_shapes=[
            pltpu.VMEM((SECTIONS, ROWS, CHAN), BF16),
            pltpu.VMEM((SECTIONS + 1, FRAMES, WIDTH + 2, HEIGHT, 3 * CHAN), BF16),
            pltpu.VMEM((2, FRAMES, WIDTH + 2, HEIGHT, 3 * CHAN), BF16),
            pltpu.VMEM((SECTIONS, CELLS, CHAN), F32),
            pltpu.VMEM((CELLS, CHAN), F32),
            pltpu.VMEM((SHARD, CHAN), BF16),
            pltpu.VMEM(clips.shape[1:], BF16),
            pltpu.VMEM(cotangent.shape[1:], BF16),
            pltpu.VMEM((3, SHARD, CHAN), F32),
            pltpu.VMEM((2, 4, 2, SHARD, CHAN), BF16),
            pltpu.VMEM((2, ROWS, CHAN), F32),
            pltpu.VMEM((2, 2, 4, SHARD, CHAN), BF16),
            pltpu.VMEM((2, 2, 4, SHARD, CHAN), BF16),
            pltpu.VMEM((2, 2, 4, SHARD, CHAN), BF16),
            pltpu.VMEM((2, 2, 3, SHARD, CHAN), BF16),
            pltpu.VMEM((2, 2, SHARD, CHAN), BF16),
            pltpu.VMEM((3, SHARD, CHAN), BF16),
            dma((7,)),
            dma((14,)),
            dma((SECTIONS, 2)),
            dma((SECTIONS, 3)),
            dma((SECTIONS, 3)),
            dma((2, SECTIONS)),
            dma((2, 2, 2)),
            dma((2, 2, 3)),
            dma((2, 2, 3)),
            dma((3,)),
            dma((3,)),
            dma((2, 3)),
            dma((2,)),
            dma((2,)),
        ],
        compiler_params=pltpu.CompilerParams(
            vmem_limit_bytes=56 << 20, collective_id=0, has_side_effects=True
        ),
    )(
        offsets,
        clips,
        weights,
        weights.reshape(16, SHARD, CHAN),
        moment,
        second,
        stale,
        cotangent,
    )


def finish_kernel(
    summed, moment, second, stale, gathered, grads, new_moment, new_second, new_weights, *scratch
):
    own, m, v, g, room, load_sem, store_sem = scratch
    places = (room, own, g, m, v)
    loads = [
        pltpu.make_async_copy(source, place, load_sem.at[n])
        for n, (source, place) in enumerate(
            zip((gathered, summed, stale, moment, second), places)
        )
    ]
    stores = [
        pltpu.make_async_copy(place, target, store_sem.at[n])
        for n, (place, target) in enumerate(
            zip((room, own, m, v), (new_weights, grads, new_moment, new_second))
        )
    ]
    for load in loads:
        load.start()
    for n in range(2):
        loads[n].wait()
        stores[n].start()
    for load in loads[2:]:
        load.wait()
    first, square = moments(m[...], v[...], g[...])
    m[...] = first
    v[...] = square
    for store in stores[2:]:
        store.start()
    for store in stores:
        store.wait()


def finish(summed, moment, second, stale, gathered):
    away = pl.BlockSpec(memory_space=pl.ANY)
    shard = jax.ShapeDtypeStruct((SHARD, CHAN), F32)
    return pl.pallas_call(
        finish_kernel,
        out_shape=(shard, shard, shard, jax.ShapeDtypeStruct(gathered.shape, BF16)),
        in_specs=[away] * 5,
        out_specs=(away,) * 4,
        scratch_shapes=[pltpu.VMEM((SHARD, CHAN), F32)] * 4
        + [
            pltpu.VMEM(gathered.shape, BF16),
            pltpu.SemaphoreType.DMA((5,)),
            pltpu.SemaphoreType.DMA((4,)),
        ],
        compiler_params=pltpu.CompilerParams(vmem_limit_bytes=56 << 20),
    )(summed, moment, second, stale, gathered)


def shards(clips, offsets, weights, moment, second, stale_grads, cotangent):
    micro = clips.shape[0]
    summed, fresh = window(
        offsets,
        clips.reshape(micro, FRAMES, -1, CHAN),
        weights[0],
        moment[0],
        second[0],
        stale_grads[0],
        cotangent.reshape(micro, FRAMES, PLANE, CHAN),
    )
    grads, first_new, second_new, fresh = finish(
        summed, moment[0], second[0], stale_grads[0], fresh
    )
    return (grads[None], first_new[None], second_new[None], fresh.reshape(1, ROWS, CHAN))


def solution(mesh):
    placed = (
        P("replica", None, None, None, None),
        P("replica", None),
        P("segment", None, None),
        P("segment", "replica", None),
        P("segment", "replica", None),
        P("segment", "replica", None),
        P("replica", None, None, None, None),
    )
    return jax.shard_map(
        shards,
        mesh=mesh,
        in_specs=placed,
        out_specs=(
            P("segment", "replica", None),
            P("segment", "replica", None),
            P("segment", "replica", None),
            P("segment", None, None),
        ),
        check_vma=False,
    )
```

```python
import math

import jax
import jax.numpy as jnp
from jax import lax
from jax.experimental import pallas as pl
from jax.experimental.pallas import tpu as pltpu
from jax.sharding import PartitionSpec as P

beta_one = 0.9
beta_two = 0.95
learn_rate = 0.05
adam_eps = 1e-08

F32 = jnp.float32
BF16 = jnp.bfloat16
FRAMES, HEIGHT, WIDTH, CHAN = 4, 16, 8, 128
PLANE = HEIGHT * WIDTH
CELLS = FRAMES * PLANE
SECTIONS = 8
TAPS = 27
ROWS = TAPS * CHAN
SCALE = 2.0 / math.sqrt(ROWS)
GRAD_SCALE = SCALE * 4.0 / math.sqrt(32 * CELLS)


def dot(a, b):
    return jnp.dot(a, b, preferred_element_type=F32)


def store_shifted(store, value):
    row = lax.broadcasted_iota(jnp.int32, (CELLS, CHAN), 0) % HEIGHT
    zero = jnp.zeros_like(value)
    for b in range(3):
        if b == 0:
            moved = jnp.where(row == 0, zero, pltpu.roll(value, 1, 0))
        elif b == 1:
            moved = value
        else:
            moved = jnp.where(row == HEIGHT - 1, zero, pltpu.roll(value, CELLS - 1, 0))
        store(b, moved.astype(BF16).reshape(FRAMES, WIDTH, HEIGHT, CHAN))


def tap_rows(w, s, tap):
    return w[s, tap * CHAN : (tap + 1) * CHAN]


def dot_turned(a, b):
    return lax.dot_general(a, b, (((1,), (1,)), ((), ())), preferred_element_type=F32)


def tap_block(w, s, times, turn, axis):
    columns = []
    for a in times:
        taps = [turn(b, c) for c in range(3) for b in range(3)]
        columns.append(
            jnp.concatenate([tap_rows(w, s, (a * 3 + b) * 3 + c) for b, c in taps], axis=axis)
        )
    return jnp.concatenate(columns, axis=1 - axis)


def field_columns(field):
    padded = field.reshape(FRAMES, WIDTH + 2, HEIGHT, 3 * CHAN)
    return jnp.concatenate(
        [padded[:, c : c + WIDTH].reshape(CELLS, 3 * CHAN) for c in range(3)], axis=1
    )


def forward_section(s, w, taps, slope):
    field = taps[s].reshape(FRAMES * (WIDTH + 2) * HEIGHT, 3 * CHAN)
    lhs = field_columns(field)
    late = dot(lhs, tap_block(w, s, (1, 2), lambda b, c: (b, c), 0))
    early = dot(lhs[: 2 * PLANE], tap_block(w, s, (0,), lambda b, c: (b, c), 0))
    total = late[:, CHAN:] + jnp.concatenate(
        [
            jnp.zeros((PLANE, CHAN), F32),
            late[:PLANE, :CHAN],
            late[PLANE : 3 * PLANE, :CHAN] + early,
        ],
        axis=0,
    )
    pre = total * SCALE
    sigma = jax.nn.sigmoid(pre)
    slope[s] = sigma * (1.0 + pre * (1.0 - sigma))

    def store(b, moved):
        taps[s + 1, :, 1 : 1 + WIDTH, :, b * CHAN : (b + 1) * CHAN] = moved

    store_shifted(store, pre * sigma)


def store_delta(s, upstream, slope, back):
    def store(b, moved):
        back[s % 2, :, 1 : 1 + WIDTH, :, b * CHAN : (b + 1) * CHAN] = moved

    store_shifted(store, upstream * slope[s])


def weight_grad(s, taps, back, put, done):
    field = taps[s, :, 1 : 1 + WIDTH, :, CHAN : 2 * CHAN].reshape(CELLS, CHAN)
    turned = field.astype(F32).T.astype(BF16)
    for a in range(3):
        frames = 2 + a
        lhs = turned[:, : frames * PLANE]
        rhs = jnp.concatenate(
            [
                back[s % 2, 2 - a : 2 - a + frames, 2 - c : 2 - c + WIDTH].reshape(
                    frames * PLANE, 3 * CHAN
                )
                for c in range(3)
            ],
            axis=1,
        )
        out = dot(lhs, rhs) * GRAD_SCALE
        for c in range(3):
            for b in range(3):
                first = (c * 3 + 2 - b) * CHAN
                put((a * 3 + b) * 3 + c, out[:, first : first + CHAN])
        if a > 0:
            done(a - 1)


def input_grad(s, w, back, slope):
    field = back[s % 2].reshape(FRAMES * (WIDTH + 2) * HEIGHT, 3 * CHAN)
    lhs = field_columns(field)
    flip = lambda b, c: (2 - b, 2 - c)
    late = dot_turned(lhs, tap_block(w, s, (1, 2), flip, 1))
    early = dot_turned(lhs[2 * PLANE :], tap_block(w, s, (0,), flip, 1))
    total = late[:, CHAN:] + jnp.concatenate(
        [
            late[PLANE : 2 * PLANE, :CHAN] + early[:PLANE],
            late[2 * PLANE : 3 * PLANE, :CHAN] + early[PLANE:],
            late[3 * PLANE :, :CHAN],
            jnp.zeros((PLANE, CHAN), F32),
        ],
        axis=0,
    )
    store_delta(s - 1, total * SCALE, slope, back)


def crop(clip, offset_y, offset_x, taps):
    row = lax.broadcasted_iota(jnp.int32, (PLANE, clip.shape[-2]), 0)
    col = lax.broadcasted_iota(jnp.int32, (PLANE, clip.shape[-2]), 1)
    clip_w = 16
    want = (row % HEIGHT + offset_y) * clip_w + row // HEIGHT + offset_x
    pick = jnp.where(want == col, 1.0, 0.0).astype(BF16)
    field = jnp.concatenate([dot(pick, clip[t]) for t in range(FRAMES)], axis=0)

    def store(b, moved):
        taps[0, :, 1 : 1 + WIDTH, :, b * CHAN : (b + 1) * CHAN] = moved

    store_shifted(store, field)


def reorder(cotangent, upstream):
    row = lax.broadcasted_iota(jnp.int32, (PLANE, PLANE), 0)
    col = lax.broadcasted_iota(jnp.int32, (PLANE, PLANE), 1)
    pick = jnp.where(row % HEIGHT * WIDTH + row // HEIGHT == col, 1.0, 0.0).astype(BF16)
    for t in range(FRAMES):
        upstream[t * PLANE : (t + 1) * PLANE] = dot(pick, cotangent[t])


def clear_edges(taps, back):
    edge = jnp.zeros((FRAMES, HEIGHT, 3 * CHAN), BF16)

    def wipe(s, _):
        taps[s, :, 0] = edge
        taps[s, :, WIDTH + 1] = edge
        return 0

    lax.fori_loop(0, SECTIONS, wipe, 0)
    for n in range(2):
        back[n, :, 0] = edge
        back[n, :, WIDTH + 1] = edge


MESH_ID = pl.DeviceIdType.MESH
HALF = ROWS // 2
PIECE = HALF // 4
SHARD = ROWS // 16


class Place:
    def __init__(self):
        segment = lax.axis_index("segment")
        replica = lax.axis_index("replica")
        self.z, self.hi = segment // 2, segment % 2
        self.lo, self.y, self.core = replica // 8, replica // 2 % 4, replica % 2

    def at(self, dz=0, hi=0, lo=0, dy=0, core=0):
        z = (self.z + dz) % 4
        y = (self.y + dy) % 4
        own = [(self.hi + hi) % 2, (self.lo + lo) % 2, (self.core + core) % 2]
        return (z * 2 + own[0], own[1] * 8 + y * 2 + own[2])

    def partners(self):
        away = [self.at(dz=k) for k in (1, 2, 3)]
        across = [self.at(dz=k, hi=1, lo=1) for k in range(4)]
        return away + across + [self.at(lo=1), self.at(hi=1)] + [self.at(dy=k) for k in (1, 2, 3)] + [self.at(core=1)]


def remote(src, dst, send, receive, device):
    return pltpu.make_async_remote_copy(
        src_ref=src,
        dst_ref=dst,
        send_sem=send,
        recv_sem=receive,
        device_id=device,
        device_id_type=MESH_ID,
    )


DIRECT, PAIR, RING, NEAR = range(4)
MODES = {(1, 0): PAIR, (3, 0): DIRECT, (2, 0): NEAR, (0, 1): DIRECT, (1, 1): RING, (3, 1): RING, (2, 1): RING}
ORDER = ((2, 0), (2, 1), (1, 0), (3, 0), (0, 1), (1, 1), (3, 1))
RELAYS = ((1, 1), (3, 1), (2, 1), (2, 0), (1, 0))
SENDS = (((1, 1), (2, 1), (3, 1), (2, 0), (1, 0), (0, 1), (3, 0)), ((3, 1), (1, 1), (2, 1), (2, 0), (1, 0), (3, 0), (0, 1)), ((2, 1), (3, 1), (1, 1), (2, 0), (1, 0), (3, 0), (0, 1)), ((1, 1), (2, 1), (3, 1), (2, 0), (1, 0), (3, 0), (0, 1)))


class Gather:
    def __init__(self, here, w, first_send, first_recv, relay_send, relay_recv, core_sem):
        self.here, self.w = here, w
        self.first_send, self.first_recv = first_send, first_recv
        self.relay_send, self.relay_recv = relay_send, relay_recv
        self.core_sem = core_sem
        self.own = here.z * 2 + here.hi

    def rows(self, s, core, start, count):
        first = core * HALF + start * PIECE
        return self.w.at[s, pl.ds(pl.multiple_of(first, PIECE), count * PIECE)]

    def mine(self, s, start, count):
        return self.rows(s, self.here.core, start, count)

    def first_parts(self, s, mode, lo):
        if mode == DIRECT:
            return [self.mine(s, 0, 4)]
        if mode == PAIR:
            return [self.mine(s, 2 * lo, 2)]
        if mode == RING:
            return [self.mine(s, self.here.y, 1)]
        return [self.mine(s, self.here.y, 1), self.mine(s, (self.here.y + 2) % 4, 1)]

    def firsts(self, dz, dh):
        lo = (self.here.lo + dh) % 2
        slot = 2 * ORDER.index((dz, dh))
        for n, part in enumerate(self.first_parts(self.own, MODES[dz, dh], lo)):
            yield remote(
                part,
                part,
                self.first_send.at[slot + n],
                self.first_recv.at[self.own, n],
                self.here.at(dz=dz, hi=dh, lo=dh),
            )

    def start(self):
        for z in range(4):

            @pl.when(self.here.z == z)
            def _():
                for dz, dh in SENDS[z]:
                    for copy in self.firsts(dz, dh):
                        copy.start()

    def by_mode(self, s, act):
        dz = (self.here.z + 4 - s // 2) % 4
        dh = (self.here.hi + s) % 2
        for mode in range(4):
            hits = [key for key, value in MODES.items() if value == mode]
            if hits:
                cond = (dz == hits[0][0]) & (dh == hits[0][1])
                for key in hits[1:]:
                    cond = cond | ((dz == key[0]) & (dh == key[1]))

                @pl.when(cond)
                def _():
                    act(mode)

    def wait(self, part, receive):
        remote(part, part, self.first_send.at[0], receive, self.here.at()).wait_recv()

    def relays(self, s, mode):
        here = self.here
        if mode == PAIR:
            hops = [(here.at(lo=1), self.mine(s, 2 * here.lo, 2), self.mine(s, 2 - 2 * here.lo, 2))]
        elif mode == DIRECT:
            hops = []
        else:
            hops = [
                (here.at(dy=k), self.mine(s, here.y, 1), self.mine(s, (here.y + 4 - k) % 4, 1))
                for k in ((2, 1, 3) if mode == RING else (1, 3))
            ]
        for n, (device, part, back) in enumerate(hops):
            yield (
                remote(part, part, self.relay_send.at[s, n], self.relay_recv.at[s, n], device),
                back,
                self.relay_recv.at[s, n],
            )

    def relay(self, s, mode):
        if mode != DIRECT:
            self.wait(self.first_parts(s, mode, self.here.lo)[0], self.first_recv.at[s, 0])
        for copy, _, _ in self.relays(s, mode):
            copy.start()

    def core_copy(self, s):
        part = self.mine(s, 0, 4)
        return remote(
            part, part, self.core_sem.at[0, s], self.core_sem.at[1, s], self.here.at(core=1)
        )

    def swap(self, s):
        def act(mode):
            for n, part in enumerate(self.first_parts(s, mode, self.here.lo)):
                if n > 0 or mode == DIRECT:
                    self.wait(part, self.first_recv.at[s, n])
            for _, part, receive in self.relays(s, mode):
                self.wait(part, receive)

        self.by_mode(s, act)
        self.core_copy(s).start()

    def arrive(self, s):
        self.wait(self.rows(s, 1 - self.here.core, 0, 4), self.core_sem.at[1, s])

    def finish(self):
        for dz, dh in ORDER:
            for copy in self.firsts(dz, dh):
                copy.wait_send()

        def each(s, _):
            @pl.when(s != self.own)
            def _():
                def act(mode):
                    for copy, _, _ in self.relays(s, mode):
                        copy.wait_send()

                self.by_mode(s, act)
                self.core_copy(s).wait_send()

            return 0

        lax.fori_loop(0, SECTIONS, each, 0)


class Exchange:
    def __init__(self, here, total, give, taken, summed, ring, kept, crossed, sems):
        self.here = here
        self.total, self.give, self.taken, self.summed = total, give, taken, summed
        self.ring, self.kept, self.crossed = ring, kept, crossed
        self.core_sem, self.ring_send, self.ring_recv, self.cross_send, self.cross_recv = sems

    def shard(self, i, j, core):
        start = pl.multiple_of((2 * j + core) * SHARD, 8)
        return self.total[i, pl.ds(start, SHARD)]

    def core_copy(self, i, lo):
        return remote(
            self.give.at[i, lo],
            self.taken.at[i, lo],
            self.core_sem.at[0, i, lo],
            self.core_sem.at[1, i, lo],
            self.here.at(core=1),
        )

    def to_core(self, i, lo):
        for y in range(4):
            self.give[i, lo, y] = self.shard(i, lo * 4 + y, 1 - self.here.core).astype(BF16)
        self.core_copy(i, lo).start()

    def ring_copy(self, i, lo, k):
        return remote(
            self.summed.at[i, lo, (self.here.y + k) % 4],
            self.ring.at[i, lo, k - 1],
            self.ring_send.at[i, lo, k - 1],
            self.ring_recv.at[i, lo, k - 1],
            self.here.at(dy=k),
        )

    def to_ring(self, i, lo):
        self.core_copy(i, lo).wait_recv()
        for y in range(4):
            both = self.shard(i, lo * 4 + y, self.here.core) + self.taken[i, lo, y].astype(F32)
            self.summed[i, lo, y] = both.astype(BF16)
        for k in (2, 1, 3):
            self.ring_copy(i, lo, k).start()

    def cross_copy(self, i, slot):
        hi, lo = ((0, 1), (1, 0), (1, 1))[slot]
        return remote(
            self.kept.at[i, (self.here.lo + lo) % 2],
            self.crossed.at[slot],
            self.cross_send.at[slot],
            self.cross_recv.at[slot],
            self.here.at(hi=hi, lo=lo),
        )

    def to_cross(self, i, lo):
        here = self.here
        for k in (1, 3, 2):
            self.ring_copy(i, lo, k).wait_recv()
        value = self.summed[i, lo, here.y].astype(F32)
        for k in range(3):
            value = value + self.ring[i, lo, k].astype(F32)
        self.kept[i, lo] = value.astype(BF16)

        @pl.when((here.hi == i) & (here.lo != lo))
        def _():
            self.cross_copy(i, 0).start()

        @pl.when((here.hi != i) & (here.lo == lo))
        def _():
            self.cross_copy(i, 1).start()

        @pl.when((here.hi != i) & (here.lo != lo))
        def _():
            self.cross_copy(i, 2).start()

    def across(self):
        for i in (1, 0):
            for lo in range(2):
                self.to_cross(i, lo)

    def finish(self, grads):
        for slot in range(3):
            self.cross_copy(0, slot).wait_recv()
        value = self.kept[self.here.hi, self.here.lo].astype(F32)
        for slot in range(3):
            value = value + self.crossed[slot].astype(F32)
        grads[...] = value
        for i in range(2):
            for lo in range(2):
                self.core_copy(i, lo).wait_send()
                for k in (1, 2, 3):
                    self.ring_copy(i, lo, k).wait_send()
        for slot in range(3):
            self.cross_copy(0, slot).wait_send()


def moments(moment, second, stale):
    first = beta_one * moment + (1.0 - beta_one) * stale
    square = beta_two * second + (1.0 - beta_two) * stale * stale
    return first, square


class Renewal:
    def __init__(self, here, fresh, ring_sem, pair_sem, core_sem):
        self.here, self.fresh = here, fresh
        self.ring_sem, self.pair_sem, self.core_sem = ring_sem, pair_sem, core_sem

    def compute(self, rows, moment, second, stale):
        here = self.here
        first, square = moments(moment[...], second[...], stale[...])
        step = learn_rate * first / (jnp.sqrt(square) + adam_eps)
        self.fresh[here.lo, here.y, here.core] = (rows[...].astype(F32) - step).astype(BF16)

    def ring_copy(self, k, back=0):
        part = self.fresh.at[self.here.lo, (self.here.y + back) % 4, self.here.core]
        return remote(
            part, part, self.ring_sem.at[0, k - 1], self.ring_sem.at[1, k - 1], self.here.at(dy=k)
        )

    def pair_copy(self, lo=0):
        part = self.fresh.at[(self.here.lo + lo) % 2, :, self.here.core]
        return remote(part, part, self.pair_sem.at[0], self.pair_sem.at[1], self.here.at(lo=1))

    def core_copy(self, core=0):
        part = self.fresh.at[:, :, (self.here.core + core) % 2]
        return remote(part, part, self.core_sem.at[0], self.core_sem.at[1], self.here.at(core=1))

    def to_ring(self):
        for k in (2, 1, 3):
            self.ring_copy(k).start()

    def to_pair(self):
        for k in (1, 3, 2):
            self.ring_copy(k, 4 - k).wait_recv()
        self.pair_copy().start()

    def to_core(self):
        self.pair_copy(1).wait_recv()
        self.core_copy().start()

    def arrive(self):
        self.core_copy(1).wait_recv()

    def finish(self):
        for k in (1, 2, 3):
            self.ring_copy(k).wait_send()
        self.pair_copy().wait_send()
        self.core_copy().wait_send()


def window_kernel(
    offsets,
    clips,
    weights,
    shards16,
    moment,
    second,
    stale,
    cotangent,
    grads,
    new_weights,
    w,
    taps,
    back,
    slope,
    upstream,
    rows,
    clip,
    given,
    old,
    fresh,
    total,
    give,
    taken,
    summed,
    ring,
    kept,
    crossed,
    load_sem,
    first_send,
    first_recv,
    relay_send,
    relay_recv,
    core_sem,
    sum_core,
    sum_ring_send,
    sum_ring_recv,
    cross_send,
    cross_recv,
    renew_ring,
    renew_pair,
    renew_core,
):
    here = Place()
    gather = Gather(here, w, first_send, first_recv, relay_send, relay_recv, core_sem)
    exchange = Exchange(
        here,
        total,
        give,
        taken,
        summed,
        ring,
        kept,
        crossed,
        (sum_core, sum_ring_send, sum_ring_recv, cross_send, cross_recv),
    )
    renewal = Renewal(here, fresh, renew_ring, renew_pair, renew_core)
    load = pltpu.make_async_copy(weights, w.at[gather.own], load_sem.at[0])
    load.start()
    loads = [
        pltpu.make_async_copy(source, place, load_sem.at[n + 1])
        for n, (source, place) in enumerate(
            (
                (clips.at[here.hi], clip),
                (cotangent.at[here.hi], given),
                (shards16.at[here.lo * 8 + here.y * 2 + here.core], rows),
                (moment, old.at[0]),
                (second, old.at[1]),
                (stale, old.at[2]),
            )
        )
    ]
    barrier = pltpu.get_barrier_semaphore()
    partners = here.partners()
    for partner in partners:
        pl.semaphore_signal(barrier, inc=1, device_id=partner, device_id_type=MESH_ID)
    for other in loads:
        other.start()
    load.wait()
    pl.semaphore_wait(barrier, len(partners))
    gather.start()

    clear_edges(taps, back)
    for other in loads:
        other.wait()
    crop(clip, offsets[here.hi, 0], offsets[here.hi, 1], taps)
    reorder(given, upstream)
    renewal.compute(rows, old.at[0], old.at[1], old.at[2])

    for dz, dh in RELAYS:
        gather.relay((here.z + 4 - dz) % 4 * 2 + (here.hi + dh) % 2, MODES[dz, dh])
    renewal.to_ring()

    def forward(tick, _):
        @pl.when((tick < SECTIONS) & (tick != gather.own))
        def _():
            gather.swap(tick)

        s = tick - 2

        @pl.when(s >= 0)
        def _():
            @pl.when(s != gather.own)
            def _():
                gather.arrive(s)

            forward_section(s, w, taps, slope)

        return 0

    lax.fori_loop(0, SECTIONS + 2, forward, 0)
    renewal.to_pair()
    last = 2 * here.z

    def backward(i, _):
        s = SECTIONS - 1 - i

        @pl.when(s == last)
        def _():
            exchange.to_ring(1, 0)
            exchange.to_ring(1, 1)

        @pl.when(s < last + 2)
        def _():
            def put(tap, block):
                total[s % 2, tap * CHAN : (tap + 1) * CHAN] = block

            weight_grad(s, taps, back, put, lambda lo: exchange.to_core(s % 2, lo))

        @pl.when(s > last)
        def _():
            input_grad(s, w, back, slope)

        return 0

    store_delta(SECTIONS - 1, upstream[...], slope, back)
    lax.fori_loop(0, SECTIONS - last, backward, 0)
    exchange.to_ring(0, 0)
    exchange.to_ring(0, 1)
    renewal.to_core()
    gather.finish()
    exchange.across()
    renewal.arrive()
    store = pltpu.make_async_copy(fresh, new_weights, load_sem.at[0])
    store.start()
    exchange.finish(grads)
    renewal.finish()
    store.wait()


def window(offsets, clips, weights, moment, second, stale, cotangent):
    vmem = pl.BlockSpec(memory_space=pltpu.VMEM)
    away = pl.BlockSpec(memory_space=pl.ANY)
    dma = pltpu.SemaphoreType.DMA
    shard = jax.ShapeDtypeStruct((SHARD, CHAN), F32)
    return pl.pallas_call(
        window_kernel,
        out_shape=(shard, jax.ShapeDtypeStruct((2, 4, 2, SHARD, CHAN), BF16)),
        in_specs=[pl.BlockSpec(memory_space=pltpu.SMEM)] + [away] * 7,
        out_specs=(vmem, away),
        scratch_shapes=[
            pltpu.VMEM((SECTIONS, ROWS, CHAN), BF16),
            pltpu.VMEM((SECTIONS + 1, FRAMES, WIDTH + 2, HEIGHT, 3 * CHAN), BF16),
            pltpu.VMEM((2, FRAMES, WIDTH + 2, HEIGHT, 3 * CHAN), BF16),
            pltpu.VMEM((SECTIONS, CELLS, CHAN), F32),
            pltpu.VMEM((CELLS, CHAN), F32),
            pltpu.VMEM((SHARD, CHAN), BF16),
            pltpu.VMEM(clips.shape[1:], BF16),
            pltpu.VMEM(cotangent.shape[1:], BF16),
            pltpu.VMEM((3, SHARD, CHAN), F32),
            pltpu.VMEM((2, 4, 2, SHARD, CHAN), BF16),
            pltpu.VMEM((2, ROWS, CHAN), F32),
            pltpu.VMEM((2, 2, 4, SHARD, CHAN), BF16),
            pltpu.VMEM((2, 2, 4, SHARD, CHAN), BF16),
            pltpu.VMEM((2, 2, 4, SHARD, CHAN), BF16),
            pltpu.VMEM((2, 2, 3, SHARD, CHAN), BF16),
            pltpu.VMEM((2, 2, SHARD, CHAN), BF16),
            pltpu.VMEM((3, SHARD, CHAN), BF16),
            dma((7,)),
            dma((14,)),
            dma((SECTIONS, 2)),
            dma((SECTIONS, 3)),
            dma((SECTIONS, 3)),
            dma((2, SECTIONS)),
            dma((2, 2, 2)),
            dma((2, 2, 3)),
            dma((2, 2, 3)),
            dma((3,)),
            dma((3,)),
            dma((2, 3)),
            dma((2,)),
            dma((2,)),
        ],
        compiler_params=pltpu.CompilerParams(
            vmem_limit_bytes=56 << 20, collective_id=0, has_side_effects=True
        ),
    )(
        offsets,
        clips,
        weights,
        weights.reshape(16, SHARD, CHAN),
        moment,
        second,
        stale,
        cotangent,
    )


def finish_kernel(
    summed, moment, second, stale, gathered, grads, new_moment, new_second, new_weights, *scratch
):
    own, m, v, g, room, load_sem, store_sem = scratch
    places = (room, own, g, m, v)
    loads = [
        pltpu.make_async_copy(source, place, load_sem.at[n])
        for n, (source, place) in enumerate(
            zip((gathered, summed, stale, moment, second), places)
        )
    ]
    stores = [
        pltpu.make_async_copy(place, target, store_sem.at[n])
        for n, (place, target) in enumerate(
            zip((room, own, m, v), (new_weights, grads, new_moment, new_second))
        )
    ]
    for load in loads:
        load.start()
    for n in range(2):
        loads[n].wait()
        stores[n].start()
    for load in loads[2:]:
        load.wait()
    first, square = moments(m[...], v[...], g[...])
    m[...] = first
    v[...] = square
    for store in stores[2:]:
        store.start()
    for store in stores:
        store.wait()


def finish(summed, moment, second, stale, gathered):
    away = pl.BlockSpec(memory_space=pl.ANY)
    shard = jax.ShapeDtypeStruct((SHARD, CHAN), F32)
    return pl.pallas_call(
        finish_kernel,
        out_shape=(shard, shard, shard, jax.ShapeDtypeStruct(gathered.shape, BF16)),
        in_specs=[away] * 5,
        out_specs=(away,) * 4,
        scratch_shapes=[pltpu.VMEM((SHARD, CHAN), F32)] * 4
        + [
            pltpu.VMEM(gathered.shape, BF16),
            pltpu.SemaphoreType.DMA((5,)),
            pltpu.SemaphoreType.DMA((4,)),
        ],
        compiler_params=pltpu.CompilerParams(vmem_limit_bytes=56 << 20),
    )(summed, moment, second, stale, gathered)


def shards(clips, offsets, weights, moment, second, stale_grads, cotangent):
    micro = clips.shape[0]
    summed, fresh = window(
        offsets,
        clips.reshape(micro, FRAMES, -1, CHAN),
        weights[0],
        moment[0],
        second[0],
        stale_grads[0],
        cotangent.reshape(micro, FRAMES, PLANE, CHAN),
    )
    grads, first_new, second_new, fresh = finish(
        summed, moment[0], second[0], stale_grads[0], fresh
    )
    return (grads[None], first_new[None], second_new[None], fresh.reshape(1, ROWS, CHAN))


def solution(mesh):
    placed = (
        P("replica", None, None, None, None),
        P("replica", None),
        P("segment", None, None),
        P("segment", "replica", None),
        P("segment", "replica", None),
        P("segment", "replica", None),
        P("replica", None, None, None, None),
    )
    return jax.shard_map(
        shards,
        mesh=mesh,
        in_specs=placed,
        out_specs=(
            P("segment", "replica", None),
            P("segment", "replica", None),
            P("segment", "replica", None),
            P("segment", None, None),
        ),
        check_vma=False,
    )
```
